32 devices in a mesh: tile: 8 (over z, x), hid: 4 (over y, core).
Axes of the slice: x: 2, y: 2, z: 4, core: 2. Of those that a mesh axis runs over, the one named last changes fastest.
Arguments:
- item_lengths: int32 [2], replicated, may hold values from 1 to 1280, 2048 in all
- refresh_slots: int32 [16], P('tile'), may hold values from -1 to 1, as said below
- layer_input: bfloat16 [2048, 3072], P('tile', 'hid'), may hold values from -6 to 6
- key_weight: bfloat16 [3072, 3072], P(None, 'hid'), may hold values from -0.109375 to 0.109375
- value_weight: bfloat16 [3072, 3072], P(None, 'hid'), may hold values from -0.109375 to 0.109375
- queries: bfloat16 [2048, 3072], P('tile', 'hid'), may hold values from -28 to 28
- key_cache: bfloat16 [2048, 3072], P('tile', 'hid'), may hold values from -4 to 4
- value_cache: bfloat16 [2048, 3072], P('tile', 'hid'), may hold values from -6 to 6
- out_weight: bfloat16 [3072, 3072], P('hid'), may hold values from -0.109375 to 0.109375
Outputs:
- attention_out: bfloat16 [2048, 3072], P('tile', 'hid')
The draws below stay inside these ranges and needn't reach their ends.
Inputs may be any that keep to these rules, and one draw needn't show every extreme that they name: `refresh_slots`: each device's 2 entries name distinct local blocks first, then -1; in every draw some device recomputes all 2 of its blocks, which one varies.
All inputs are finite; a program needn't handle non-finite values.
Results may differ from the reference program's by a relative error of at most 0.0086.
Values may be sent and summed in bfloat16 or wider, within the bound.
No kernel may reach another device: no remote copies, remote signals or barrier semaphores. Data moves between devices by JAX's collectives and lax.ppermute only.
A program may use at most 128 MiB of HBM per device.

```python
import math
import jax
import jax.numpy as jnp
import numpy as np
from jax import lax

D = 3072
HEADS = 48
HD = 64
BLOCK = 128
TOKENS = 2048
BLK_DEV = 2
BLOCKS = 16
N_TILE = 8


def drawn_pair(key):
    query_seed = jax.random.fold_in(key, 11)
    keys_seed = jax.random.fold_in(key, 12)
    width = HEADS * HD
    query_part = 3.0 * jnp.clip(jax.random.normal(query_seed, (TOKENS, width), jnp.float32), -6.0, 6.0)
    key_part = jnp.clip(jax.random.normal(keys_seed, (TOKENS, width), jnp.float32), -4.0, 4.0)
    return (query_part, key_part)


def draw_queries(key, part):
    return drawn_pair(key)[0].astype(jnp.bfloat16)


def draw_key_cache(key, part):
    return drawn_pair(key)[1].astype(jnp.bfloat16)


def draw_refresh_slots(key, part):
    flag_seed = jax.random.fold_in(key, 21)
    busy_seed = jax.random.fold_in(key, 22)
    devices_count = BLOCKS // BLK_DEV
    flags = jax.random.randint(flag_seed, (BLOCKS,), 0, 10) == 0
    busiest = jax.random.randint(busy_seed, (), 0, devices_count)
    owner = jnp.arange(BLOCKS, dtype=jnp.int32) // BLK_DEV
    flags = jnp.logical_or(flags, owner == busiest)
    table = flags.reshape(devices_count, BLK_DEV).astype(jnp.int32)
    order = jnp.argsort(1 - table, axis=1, stable=True).astype(jnp.int32)
    sorted_flags = jnp.take_along_axis(table, order, axis=1)
    slots = jnp.where(sorted_flags == 1, order, -1)
    return slots.reshape(BLOCKS).astype(jnp.int32)


def levels(rng, shape, split, least, high):
    def one(dim, blocks):
        draws = jax.random.uniform(jax.random.fold_in(jax.random.fold_in(rng, 6), dim), (blocks,), jnp.float32, least / len(split), high / len(split))
        return jnp.repeat(jnp.exp(draws), shape[dim] // blocks).reshape((-1,) + (1,) * (len(shape) - dim - 1))

    factor_of = one(*split[0])
    for cut in split[1:]:
        factor_of = factor_of * one(*cut)
    return factor_of


def length_profile(count, total, limit, slope):
    weights = [(1 << 20) // math.isqrt(grade ** slope) + 1 for grade in range(2, count + 1)]
    rest, given = total - limit - (count - 1), [1] * (count - 1)
    while rest > 0:
        candidates = [i for i in range(count - 1) if given[i] < limit]
        mass, left = sum([weights[i] for i in candidates]), rest
        for i in candidates:
            addition = min(limit - given[i], max(1, left * weights[i] // mass), rest)
            given[i] = given[i] + addition
            rest = rest - addition
    return np.array([limit] + given)


def uneven(stream_key, number_of, total, bound, slope):
    if number_of == 2:
        one = jax.random.randint(stream_key, (), max(1, total - bound), min(bound, total - 1) + 1)
        return jnp.stack([one, total - one])
    sizes = jnp.asarray(length_profile(number_of, total, bound, slope), jnp.int32)
    pairs = (number_of - 1) // 2
    donor, receiver = sizes[1:1 + 2 * pairs:2], sizes[2:2 + 2 * pairs:2]
    margin = jnp.minimum(donor - 1, bound - receiver)
    moved = jax.random.randint(jax.random.fold_in(stream_key, 1), (pairs,), 0, 1 << 20) % (margin + 1)
    sizes = sizes.at[1:1 + 2 * pairs:2].set(donor - moved).at[2:2 + 2 * pairs:2].set(receiver + moved)
    return sizes[jax.random.permutation(jax.random.fold_in(stream_key, 2), number_of)]


def bell_draw(own_key, dims, deviation, most, shards=(), kind=jnp.bfloat16):
    drawn = jax.random.normal(own_key, dims, jnp.float32) * deviation
    if len(shards) > 0:
        drawn = levels(own_key, dims, shards, -0.22, 0.18) * drawn
    return jnp.clip(drawn, min=-most, max=most).astype(kind)


def setup_inputs(seed: int = 0) -> dict:
    key_list = jax.random.split(jax.random.key(seed), 10)
    return {
        "item_lengths": uneven(key_list[0], 2, TOKENS, TOKENS * 5 // 8, 0).astype(jnp.int32),
        "refresh_slots": draw_refresh_slots(jax.random.fold_in(key_list[9], 71), 0),
        "layer_input": bell_draw(key_list[2], (TOKENS, D), 1.0, 6.0, ((0, 8), (1, 4))),
        "key_weight": bell_draw(key_list[3], (D, HEADS * HD), D ** -0.5, 0.109375, ((1, 4),)),
        "value_weight": bell_draw(key_list[4], (D, HEADS * HD), D ** -0.5, 0.109375, ((1, 4),)),
        "queries": draw_queries(jax.random.fold_in(key_list[9], 71), 0),
        "key_cache": draw_key_cache(jax.random.fold_in(key_list[9], 71), 0),
        "value_cache": bell_draw(key_list[7], (TOKENS, HEADS * HD), 1.0, 6.0, ((0, 8), (1, 4))),
        "out_weight": bell_draw(key_list[8], (HEADS * HD, D), (HEADS * HD) ** -0.5, 0.109375, ((0, 4),)),
    }


def reference(item_lengths, refresh_slots, layer_input, key_weight, value_weight, queries, key_cache, value_cache, out_weight):
    local_ids = jnp.arange(BLK_DEV, dtype=jnp.int32)
    slot_table = refresh_slots.reshape(N_TILE, BLK_DEV)
    refreshed = jnp.any(slot_table[:, :, None] == local_ids[None, None, :], axis=1).reshape(BLOCKS)
    width = HEADS * HD
    input_blocks = layer_input.reshape(BLOCKS, BLOCK, D)
    key_blocks = key_cache.reshape(BLOCKS, BLOCK, width)
    value_blocks = value_cache.reshape(BLOCKS, BLOCK, width)

    def refresh(operands):
        flag, rows_in, old_keys, old_values = operands

        def recompute(unused):
            new_keys = jnp.dot(rows_in, key_weight, preferred_element_type=jnp.float32).astype(jnp.bfloat16)
            new_values = jnp.dot(rows_in, value_weight, preferred_element_type=jnp.float32).astype(jnp.bfloat16)
            return new_keys, new_values

        def keep_old(unused):
            return old_keys, old_values

        return lax.cond(flag, recompute, keep_old, 0)

    fresh_keys, fresh_values = lax.map(refresh, (refreshed, input_blocks, key_blocks, value_blocks))
    fresh_keys = fresh_keys.reshape(TOKENS, width)
    fresh_values = fresh_values.reshape(TOKENS, width)
    item = (jnp.arange(TOKENS, dtype=jnp.int32) >= item_lengths[0]).astype(jnp.int32)
    same_item = item[:, None] == item[None, :]

    def one_head(head_index):
        column = head_index * HD
        query_head = lax.dynamic_slice_in_dim(queries, column, HD, 1)
        key_head = lax.dynamic_slice_in_dim(fresh_keys, column, HD, 1)
        value_head = lax.dynamic_slice_in_dim(fresh_values, column, HD, 1)
        scores = jnp.dot(query_head, key_head.T, preferred_element_type=jnp.float32) * 0.125
        scores = jnp.where(same_item, scores, -jnp.inf)
        top = jnp.max(scores, axis=1, keepdims=True)
        weights = jnp.exp(scores - top)
        totals = jnp.sum(weights, axis=1, keepdims=True)
        summed = jnp.dot(weights.astype(jnp.bfloat16), value_head, preferred_element_type=jnp.float32)
        return (summed / totals).astype(jnp.bfloat16)

    per_head = lax.map(one_head, jnp.arange(HEADS, dtype=jnp.int32))
    attention = jnp.transpose(per_head, (1, 0, 2)).reshape(TOKENS, width)
    return jnp.dot(attention, out_weight, preferred_element_type=jnp.float32).astype(jnp.bfloat16)
```

```python
import functools

import jax
import jax.numpy as jnp
from jax import lax
from jax.experimental import pallas as pl
from jax.experimental.pallas import tpu as pltpu
from jax.sharding import PartitionSpec as P

HD = 64
BLOCK = 128
RUN = 4
NEG = -1e30
SCALE = 0.125 * 1.4426950408889634
AXES = ("tile", "hid")
BF = jnp.bfloat16
F32 = jnp.float32


def move(value, tile_mask, hid_mask):
    tiles, hids = lax.axis_size("tile"), lax.axis_size("hid")
    pairs = [
        (t * hids + h, (t ^ tile_mask) * hids + (h ^ hid_mask))
        for t in range(tiles)
        for h in range(hids)
    ]
    return lax.ppermute(value, AXES, pairs)


def params(**kw):
    return pltpu.CompilerParams(vmem_limit_bytes=48 * 2**20, **kw)


def pack_queries_kernel(sc, q_ref, *outs):
    half = q_ref.shape[0] // 2
    width = q_ref.shape[1] // RUN
    for low in range(RUN):

        @pl.when(sc[0] == low)
        def _(low=low):
            for i in range(RUN):
                cols = slice(width * (low ^ i), width * (low ^ i) + width)
                outs[i][:, :width] = q_ref[:half, cols]
                outs[i][:, width:] = q_ref[half:, cols]


def pack_queries(low, queries):
    rows, width = queries.shape
    vmem = pl.BlockSpec(memory_space=pltpu.VMEM)
    out = jax.ShapeDtypeStruct((rows // 2, 2 * width // RUN), BF)
    return pl.pallas_call(
        pack_queries_kernel,
        in_specs=[pl.BlockSpec(memory_space=pltpu.SMEM), vmem],
        out_specs=[vmem] * RUN,
        out_shape=[out] * RUN,
        name="pack_queries",
        compiler_params=params(),
    )(low.reshape(1), queries)


def refresh_kernel(sc, x_own, x_y, x_c, wk, wv, kc, vc, *rest):
    outs, (acck, accv) = rest[:RUN], rest[RUN:]
    step = pl.program_id(0)
    width = kc.shape[1] // RUN
    busy = sc[2] + sc[3] > 0

    @pl.when(busy)
    def _():
        for k in range(4):

            @pl.when(step == k)
            def _(k=k):
                x = (x_own, x_y, x_c.at[0], x_c.at[1])[k][...]
                dk = jnp.dot(x, wk[...], preferred_element_type=F32)
                dv = jnp.dot(x, wv[...], preferred_element_type=F32)
                if k == 0:
                    acck[...] = dk
                    accv[...] = dv
                else:
                    acck[...] += dk
                    accv[...] += dv

    @pl.when(step == 3)
    def _():
        for low in range(RUN):

            @pl.when(sc[1] == low)
            def _(low=low):
                for b in range(kc.shape[0] // BLOCK):
                    rows = slice(b * BLOCK, (b + 1) * BLOCK)

                    def emit(src_k, src_v):
                        for i in range(RUN):
                            cols = slice(width * (low ^ i), width * (low ^ i) + width)
                            outs[i][rows, :width] = src_k[rows, cols].astype(BF)
                            outs[i][rows, width:] = src_v[rows, cols].astype(BF)

                    @pl.when(sc[2 + b] > 0)
                    def _():
                        emit(acck, accv)

                    @pl.when(sc[2 + b] == 0)
                    def _():
                        emit(kc, vc)


def refresh(low, hid, slots, x_own, x_y, x_c, wk, wv, kc, vc):
    rows, width = kc.shape
    flags = [jnp.any(slots == b).astype(jnp.int32) for b in range(rows // BLOCK)]
    scalars = jnp.stack([hid, low] + flags).astype(jnp.int32)

    def full(*shape):
        return pl.BlockSpec(shape, lambda k, sc: (0,) * len(shape))

    def weight_map(k, sc):
        part = (k % 2) * 2 + k // 2
        return (jnp.where(sc[2] + sc[3] > 0, sc[0] ^ part, sc[0]), 0)

    weight = pl.BlockSpec((width, width), weight_map)
    chunk = (rows, 2 * width // RUN)
    return pl.pallas_call(
        refresh_kernel,
        grid_spec=pltpu.PrefetchScalarGridSpec(
            num_scalar_prefetch=1,
            grid=(4,),
            in_specs=[
                full(rows, width),
                full(rows, width),
                full(2, rows, width),
                weight,
                weight,
                full(rows, width),
                full(rows, width),
            ],
            out_specs=[full(*chunk)] * RUN,
            scratch_shapes=[pltpu.VMEM((rows, width), F32)] * 2,
        ),
        out_shape=[jax.ShapeDtypeStruct(chunk, BF)] * RUN,
        name="refresh",
        compiler_params=params(dimension_semantics=("arbitrary",)),
    )(scalars, x_own, x_y, x_c, wk, wv, kc, vc)


def attend_kernel(sc, *refs, n_q, n_kv, slot):
    q_refs, kv_refs = refs[:n_q], refs[n_q : n_q + n_kv]
    out_refs = refs[n_q + n_kv : 2 * n_q + n_kv]
    kext, vext = refs[2 * n_q + n_kv :]
    heads = kext.shape[0]
    half = slot // 2
    width = heads * HD
    split = sc[0]

    def flags(start, rows, first, second):
        item0 = start + lax.broadcasted_iota(jnp.int32, (rows, HD), 0) < split
        lane = lax.broadcasted_iota(jnp.int32, (rows, HD), 1)
        one = jnp.where(item0, first, second)
        two = jnp.where(item0, second, first)
        return jnp.where(lane == 0, one, jnp.where(lane == 1, two, 0.0)).astype(BF)

    row = 0
    for kv in kv_refs:
        for part in range(kv.shape[0] // slot):
            rows = pl.ds(row, slot)
            src = slice(part * slot, (part + 1) * slot)
            aux = flags(sc[1 + n_q + row // slot], slot, 0.0, NEG)
            ones = jnp.ones((slot, HD), BF)
            for h in range(heads):
                kext[h, rows, :] = jnp.concatenate([kv[src, h * HD : (h + 1) * HD], aux], 1)
                cols = slice(width + h * HD, width + (h + 1) * HD)
                vext[h, rows, :] = jnp.concatenate([kv[src, cols], ones], 1)
            row += slot
    for i in range(n_q):
        for r in range(2):
            aux = flags(sc[1 + i] + r * half, half, 1.0, 0.0)
            for h in range(heads):
                cols = slice(r * width + h * HD, r * width + (h + 1) * HD)
                q = jnp.concatenate([q_refs[i][:, cols], aux], 1)
                s = lax.dot_general(
                    q, kext[h], (((1,), (1,)), ((), ())), preferred_element_type=F32
                )
                top = jnp.max(s, axis=1, keepdims=True)
                p = jnp.exp2((s - top) * SCALE).astype(BF)
                o = jnp.dot(p, vext[h], preferred_element_type=F32)
                out_refs[i][:, cols] = (o[:, :HD] / o[:, HD:]).astype(BF)


def attend(scalars, q_parts, kv_parts, slot):
    keys = sum(kv.shape[0] for kv in kv_parts)
    heads = kv_parts[0].shape[1] // (2 * HD)
    vmem = pl.BlockSpec(memory_space=pltpu.VMEM)
    return pl.pallas_call(
        functools.partial(attend_kernel, n_q=len(q_parts), n_kv=len(kv_parts), slot=slot),
        in_specs=[pl.BlockSpec(memory_space=pltpu.SMEM)]
        + [vmem] * (len(q_parts) + len(kv_parts)),
        out_specs=[vmem] * len(q_parts),
        out_shape=[jax.ShapeDtypeStruct(q.shape, BF) for q in q_parts],
        scratch_shapes=[pltpu.VMEM((heads, keys, 2 * HD), BF)] * 2,
        name="attend",
        compiler_params=params(),
    )(scalars, *q_parts, *kv_parts)


def project_kernel(sc, a0, a1, a2, a3, w, keep, send, lhs):
    step = pl.program_id(0)
    half = a0.shape[0]
    width = a0.shape[1] // 2

    @pl.when(step == 0)
    def _():
        for low in range(RUN):

            @pl.when(sc[1] == low)
            def _(low=low):
                for i, a in enumerate((a0, a1, a2, a3)):
                    cols = slice(width * (low ^ i), width * (low ^ i) + width)
                    lhs[:half, cols] = a[:, :width]
                    lhs[half:, cols] = a[:, width:]

    sums = jnp.dot(lhs[...], w[...], preferred_element_type=F32)

    @pl.when(step == 0)
    def _():
        send[...] = sums.astype(BF)

    @pl.when(step == 1)
    def _():
        keep[...] = sums


def project(low, hid, mask, parts, w):
    rows = 2 * parts[0].shape[0]
    width = w.shape[0]
    scalars = jnp.stack([hid, low]).astype(jnp.int32)

    def full(*shape):
        return pl.BlockSpec(shape, lambda k, sc: (0,) * len(shape))

    return pl.pallas_call(
        project_kernel,
        grid_spec=pltpu.PrefetchScalarGridSpec(
            num_scalar_prefetch=1,
            grid=(2,),
            in_specs=[full(*parts[0].shape)] * RUN
            + [pl.BlockSpec((width, width), lambda k, sc: (0, sc[0] ^ mask ^ (1 - k)))],
            out_specs=[full(rows, width), full(rows, width)],
            scratch_shapes=[pltpu.VMEM((rows, width), BF)],
        ),
        out_shape=[
            jax.ShapeDtypeStruct((rows, width), F32),
            jax.ShapeDtypeStruct((rows, width), BF),
        ],
        name="project",
        compiler_params=params(dimension_semantics=("arbitrary",)),
    )(scalars, *parts, w)


def body(
    item_lengths,
    refresh_slots,
    layer_input,
    key_weight,
    value_weight,
    queries,
    key_cache,
    value_cache,
    out_weight,
):
    rows = queries.shape[0]
    tile = lax.axis_index("tile")
    hid = lax.axis_index("hid")
    tiles = lax.axis_size("tile")
    low = tile % RUN
    split = item_lengths[0]

    x_y = move(layer_input, 0, 2)
    x_c = move(jnp.stack([layer_input, x_y]), 0, 1)
    q_parts = pack_queries(low, queries)
    q_parts = [q_parts[0]] + [move(q_parts[i], i, 0) for i in (1, 2, 3)]
    kv = refresh(
        low,
        hid,
        refresh_slots,
        layer_input,
        x_y,
        x_c,
        key_weight,
        value_weight,
        key_cache,
        value_cache,
    )
    kv_parts = [kv[0]] + [move(kv[i], i, 0) for i in (1, 2, 3)]
    masks = list(range(RUN))
    bit = RUN
    while bit < tiles:
        kv_parts = kv_parts + [move(part, bit, 0) for part in kv_parts]
        masks = masks + [m ^ bit for m in masks]
        bit *= 2
    q_start = (tile ^ jnp.arange(RUN, dtype=jnp.int32)) * rows
    k_start = (tile ^ jnp.array(masks, dtype=jnp.int32)) * rows
    scalars = jnp.concatenate([split[None], q_start, k_start]).astype(jnp.int32)
    back = attend(scalars, q_parts, kv_parts, rows)
    parts = [back[0]] + [move(back[i], i, 0) for i in (1, 2, 3)]

    keep_y, send_y = project(low, hid, 2, parts, out_weight)
    via_y = (keep_y + move(send_y, 0, 1).astype(F32)).astype(BF)
    got_y = move(via_y, 0, 2)
    keep, send = project(low, hid, 0, parts, out_weight)
    return (keep + move(send, 0, 1).astype(F32) + got_y.astype(F32)).astype(BF)


def solution(mesh):
    return jax.shard_map(
        body,
        mesh=mesh,
        in_specs=(
            P(),
            P("tile"),
            P("tile", "hid"),
            P(None, "hid"),
            P(None, "hid"),
            P("tile", "hid"),
            P("tile", "hid"),
            P("tile", "hid"),
            P("hid", None),
        ),
        out_specs=P("tile", "hid"),
        check_vma=False,
    )
```

```python
import functools

import jax
import jax.numpy as jnp
from jax import lax
from jax.experimental import pallas as pl
from jax.experimental.pallas import tpu as pltpu
from jax.sharding import PartitionSpec as P

HD = 64
BLOCK = 128
RUN = 4
NEG = -1e30
SCALE = 0.125 * 1.4426950408889634
AXES = ("tile", "hid")
BF = jnp.bfloat16
F32 = jnp.float32


def move(value, tile_mask, hid_mask):
    tiles, hids = lax.axis_size("tile"), lax.axis_size("hid")
    pairs = [
        (t * hids + h, (t ^ tile_mask) * hids + (h ^ hid_mask))
        for t in range(tiles)
        for h in range(hids)
    ]
    return lax.ppermute(value, AXES, pairs)


def params(**kw):
    return pltpu.CompilerParams(vmem_limit_bytes=48 * 2**20, **kw)


def pack_queries_kernel(sc, q_ref, *outs):
    half = q_ref.shape[0] // 2
    width = q_ref.shape[1] // RUN
    for low in range(RUN):

        @pl.when(sc[0] == low)
        def _(low=low):
            for i in range(RUN):
                cols = slice(width * (low ^ i), width * (low ^ i) + width)
                outs[i][:, :width] = q_ref[:half, cols]
                outs[i][:, width:] = q_ref[half:, cols]


def pack_queries(low, queries):
    rows, width = queries.shape
    vmem = pl.BlockSpec(memory_space=pltpu.VMEM)
    out = jax.ShapeDtypeStruct((rows // 2, 2 * width // RUN), BF)
    return pl.pallas_call(
        pack_queries_kernel,
        in_specs=[pl.BlockSpec(memory_space=pltpu.SMEM), vmem],
        out_specs=[vmem] * RUN,
        out_shape=[out] * RUN,
        name="pack_queries",
        compiler_params=params(),
    )(low.reshape(1), queries)


def refresh_kernel(sc, x_own, x_y, x_c, wk, wv, kc, vc, *rest):
    outs, (acck, accv) = rest[:RUN], rest[RUN:]
    step = pl.program_id(0)
    width = kc.shape[1] // RUN
    busy = sc[2] + sc[3] > 0

    @pl.when(busy)
    def _():
        for k in range(4):

            @pl.when(step == k)
            def _(k=k):
                x = (x_own, x_y, x_c.at[0], x_c.at[1])[k][...]
                dk = jnp.dot(x, wk[...], preferred_element_type=F32)
                dv = jnp.dot(x, wv[...], preferred_element_type=F32)
                if k == 0:
                    acck[...] = dk
                    accv[...] = dv
                else:
                    acck[...] += dk
                    accv[...] += dv

    @pl.when(step == 3)
    def _():
        for low in range(RUN):

            @pl.when(sc[1] == low)
            def _(low=low):
                for b in range(kc.shape[0] // BLOCK):
                    rows = slice(b * BLOCK, (b + 1) * BLOCK)

                    def emit(src_k, src_v):
                        for i in range(RUN):
                            cols = slice(width * (low ^ i), width * (low ^ i) + width)
                            outs[i][rows, :width] = src_k[rows, cols].astype(BF)
                            outs[i][rows, width:] = src_v[rows, cols].astype(BF)

                    @pl.when(sc[2 + b] > 0)
                    def _():
                        emit(acck, accv)

                    @pl.when(sc[2 + b] == 0)
                    def _():
                        emit(kc, vc)


def refresh(low, hid, slots, x_own, x_y, x_c, wk, wv, kc, vc):
    rows, width = kc.shape
    flags = [jnp.any(slots == b).astype(jnp.int32) for b in range(rows // BLOCK)]
    scalars = jnp.stack([hid, low] + flags).astype(jnp.int32)

    def full(*shape):
        return pl.BlockSpec(shape, lambda k, sc: (0,) * len(shape))

    def weight_map(k, sc):
        part = (k % 2) * 2 + k // 2
        return (jnp.where(sc[2] + sc[3] > 0, sc[0] ^ part, sc[0]), 0)

    weight = pl.BlockSpec((width, width), weight_map)
    chunk = (rows, 2 * width // RUN)
    return pl.pallas_call(
        refresh_kernel,
        grid_spec=pltpu.PrefetchScalarGridSpec(
            num_scalar_prefetch=1,
            grid=(4,),
            in_specs=[
                full(rows, width),
                full(rows, width),
                full(2, rows, width),
                weight,
                weight,
                full(rows, width),
                full(rows, width),
            ],
            out_specs=[full(*chunk)] * RUN,
            scratch_shapes=[pltpu.VMEM((rows, width), F32)] * 2,
        ),
        out_shape=[jax.ShapeDtypeStruct(chunk, BF)] * RUN,
        name="refresh",
        compiler_params=params(dimension_semantics=("arbitrary",)),
    )(scalars, x_own, x_y, x_c, wk, wv, kc, vc)


def item_flags(start, rows, split, first, second, mask_item=None):
    index = start + lax.broadcasted_iota(jnp.int32, (rows, HD), 0)
    lane = lax.broadcasted_iota(jnp.int32, (rows, HD), 1)
    item = jnp.where(index < split, 0, 1)
    zero, one = item == 0, item == 1
    if mask_item is not None:
        off = item != mask_item
        zero, one = zero | off, one | off
    flag0 = jnp.where(zero, first, second)
    flag1 = jnp.where(one, first, second)
    return jnp.where(lane == 0, flag0, jnp.where(lane == 1, flag1, 0.0)).astype(BF)


def extend_keys(kv_refs, kext, vext, slot, split, start_of):
    heads = kext.shape[0]
    width = heads * HD
    row = 0
    for kv in kv_refs:
        for part in range(kv.shape[0] // slot):
            src = slice(part * slot, (part + 1) * slot)
            aux = item_flags(start_of(row // slot), slot, split, 0.0, NEG)
            ones = jnp.ones((slot, HD), BF)
            for h in range(heads):
                cols = slice(h * HD, (h + 1) * HD)
                kext[h, row : row + slot, :] = jnp.concatenate([kv[src, cols], aux], 1)
                cols = slice(width + h * HD, width + (h + 1) * HD)
                vext[h, row : row + slot, :] = jnp.concatenate([kv[src, cols], ones], 1)
            row += slot


def dot_t(a, b):
    return lax.dot_general(a, b, (((1,), (1,)), ((), ())), preferred_element_type=F32)


def attend_all_kernel(sc, *refs, n_q, n_kv, slot):
    q_refs, kv_refs = refs[:n_q], refs[n_q : n_q + n_kv]
    out_refs = refs[n_q + n_kv : 2 * n_q + n_kv]
    kext, vext = refs[2 * n_q + n_kv :]
    heads, keys = kext.shape[:2]
    half = slot // 2
    width = heads * HD
    split = sc[0]
    chunk = RUN * slot
    extend_keys(kv_refs, kext, vext, slot, split, lambda j: sc[1 + n_q + j])
    for i in range(n_q):
        for r in range(2):
            aux = item_flags(sc[1 + i] + r * half, half, split, 1.0, 0.0)
            for h in range(heads):
                cols = slice(r * width + h * HD, r * width + (h + 1) * HD)
                q = jnp.concatenate([q_refs[i][:, cols], aux], 1)

                def step(j, state, q=q, h=h):
                    top, acc = state
                    rows = pl.ds(pl.multiple_of(j * chunk, chunk), chunk)
                    s = dot_t(q, kext[h, rows, :])
                    new = jnp.maximum(top, jnp.max(s, axis=1, keepdims=True))
                    p = jnp.exp2((s - new) * SCALE).astype(BF)
                    acc = acc * jnp.exp2((top - new) * SCALE)
                    return new, acc + jnp.dot(p, vext[h, rows, :], preferred_element_type=F32)

                start = jnp.full((half, 1), 2 * NEG, F32), jnp.zeros((half, 2 * HD), F32)
                o = lax.fori_loop(0, keys // chunk, step, start)[1]
                out_refs[i][:, cols] = (o[:, :HD] / o[:, HD:]).astype(BF)


VMEM = pl.BlockSpec(memory_space=pltpu.VMEM)
SMEM = pl.BlockSpec(memory_space=pltpu.SMEM)


def attend_all(scalars, q_parts, kv_parts, slot):
    keys = sum(kv.shape[0] for kv in kv_parts)
    heads = kv_parts[0].shape[1] // (2 * HD)
    return pl.pallas_call(
        functools.partial(attend_all_kernel, n_q=len(q_parts), n_kv=len(kv_parts), slot=slot),
        in_specs=[SMEM] + [VMEM] * (len(q_parts) + len(kv_parts)),
        out_specs=[VMEM] * len(q_parts),
        out_shape=[jax.ShapeDtypeStruct(q.shape, BF) for q in q_parts],
        scratch_shapes=[pltpu.VMEM((heads, keys, 2 * HD), BF)] * 2,
        name="attend_all",
        compiler_params=params(),
    )(scalars, *q_parts, *kv_parts)


def softmax_part(q, keys, values):
    s = dot_t(q, keys)
    top = jnp.max(s, axis=1, keepdims=True)
    p = jnp.exp2((s - top) * SCALE).astype(BF)
    return top, jnp.dot(p, values, preferred_element_type=F32)


def attend_guest_kernel(sc, q_ref, k0, k1, k2, k3, out, kext, vext):
    heads = kext.shape[0]
    half = q_ref.shape[0]
    width = heads * HD
    extend_keys((k0, k1, k2, k3), kext, vext, 2 * half, sc[0], lambda j: sc[2 + j])
    lane = lax.broadcasted_iota(jnp.int32, (half, 2 * HD), 1)
    logs = jnp.zeros((half, 2 * HD), F32)
    for r in range(2):
        aux = item_flags(sc[7] + r * half, half, sc[0], 1.0, 0.0, sc[1])
        for h in range(heads):
            cols = slice(r * width + h * HD, r * width + (h + 1) * HD)
            q = jnp.concatenate([q_ref[:, cols], aux], 1)
            top, o = softmax_part(q, kext[h], vext[h])
            out[:, cols] = (o[:, :HD] / o[:, HD:]).astype(BF)
            log = top * SCALE + jnp.log2(o[:, HD : HD + 1])
            high = log.astype(BF).astype(F32)
            mid = (log - high).astype(BF).astype(F32)
            rest = log - high - mid
            at = 3 * (r * heads + h)
            for n, piece in enumerate((high, mid, rest)):
                logs = jnp.where(lane == at + n, piece, logs)
    out[:, 2 * width :] = logs.astype(BF)


def attend_own_kernel(sc, q0, q1, q2, q3, k0, k1, k2, k3, out, kext, vext):
    heads = kext.shape[0]
    half = q0.shape[0]
    width = heads * HD
    extend_keys((k0, k1, k2, k3), kext, vext, 2 * half, sc[0], lambda j: sc[2 + j])
    lane = lax.broadcasted_iota(jnp.int32, (half, 2 * HD), 1)
    for i, q_ref in enumerate((q0, q1, q2, q3)):
        for r in range(2):
            aux = item_flags(sc[2 + i] + r * half, half, sc[0], 1.0, 0.0)
            rows = slice((2 * i + r) * half, (2 * i + r + 1) * half)
            for h in range(heads):
                cols = slice(r * width + h * HD, r * width + (h + 1) * HD)
                q = jnp.concatenate([q_ref[:, cols], aux], 1)
                top, o = softmax_part(q, kext[h], vext[h])
                out[h, rows, :] = jnp.where(lane < HD + HD // 2, o, top)


def attend_merge_kernel(sc, q0, q1, q2, q3, part, kv, guest, o0, o1, o2, o3, kext, vext):
    heads = kext.shape[0]
    half = q0.shape[0]
    width = heads * HD
    outs = (o0, o1, o2, o3)
    extend_keys((kv,), kext, vext, 2 * half, sc[0], lambda j: sc[6])
    logs = guest[:, 2 * width :].astype(F32)
    for i, q_ref in enumerate((q0, q1, q2, q3)):
        for r in range(2):
            aux = item_flags(sc[2 + i] + r * half, half, sc[0], 1.0, 0.0, sc[1])
            rows = slice((2 * i + r) * half, (2 * i + r + 1) * half)
            for h in range(heads):
                cols = slice(r * width + h * HD, r * width + (h + 1) * HD)
                q = jnp.concatenate([q_ref[:, cols], aux], 1)
                own = part[h, rows, :]
                own_log = own[:, 2 * HD - 1 :] * SCALE
                s = dot_t(q, kext[h]) * SCALE
                at = 3 * (r * heads + h)
                log = logs[:, at : at + 1] + logs[:, at + 1 : at + 2] + logs[:, at + 2 : at + 3]
                log = jnp.where(sc[8] == i, log, NEG)
                top = jnp.maximum(own_log, jnp.max(s, axis=1, keepdims=True))
                top = jnp.maximum(top, log)
                p = jnp.exp2(s - top).astype(BF)
                o = jnp.dot(p, vext[h], preferred_element_type=F32)
                o = o + own * jnp.exp2(own_log - top)
                share = jnp.exp2(log - top)
                total = o[:, HD : HD + 1] + share
                far = guest[:, cols].astype(F32) * share
                outs[i][:, cols] = ((o[:, :HD] + far) / total).astype(BF)


def attend_items(tile, low, split, rows, q_parts, kv_parts):
    cube = tile // RUN
    edge_low = jnp.where(cube == 0, RUN - 1, 0)
    edge = low ^ edge_low
    heads = kv_parts[0].shape[1] // (2 * HD)
    own_start = (tile ^ jnp.arange(RUN, dtype=jnp.int32)) * rows
    guest_start = jnp.where(cube == 0, RUN, RUN - 1) * rows
    scalars = jnp.concatenate(
        [jnp.stack([split, cube]), own_start, jnp.stack([guest_start, guest_start, edge])]
    ).astype(jnp.int32)

    def ext(keys):
        return [pltpu.VMEM((heads, keys, 2 * HD), BF)] * 2

    guest_q = move(lax.select_n(edge, *q_parts), RUN, 0)
    guest_kv = move(lax.select_n(edge, *kv_parts), RUN, 0)
    half = rows // 2
    guest = pl.pallas_call(
        attend_guest_kernel,
        in_specs=[SMEM] + [VMEM] * 5,
        out_specs=VMEM,
        out_shape=jax.ShapeDtypeStruct((half, 2 * heads * HD + 2 * HD), BF),
        scratch_shapes=ext(RUN * rows),
        name="attend_guest",
        compiler_params=params(),
    )(scalars, guest_q, *kv_parts)
    guest = move(guest, RUN, 0)
    own = pl.pallas_call(
        attend_own_kernel,
        in_specs=[SMEM] + [VMEM] * 8,
        out_specs=VMEM,
        out_shape=jax.ShapeDtypeStruct((heads, RUN * rows, 2 * HD), F32),
        scratch_shapes=ext(RUN * rows),
        name="attend_own",
        compiler_params=params(),
    )(scalars, *q_parts, *kv_parts)
    return pl.pallas_call(
        attend_merge_kernel,
        in_specs=[SMEM] + [VMEM] * 7,
        out_specs=[VMEM] * RUN,
        out_shape=[jax.ShapeDtypeStruct(q.shape, BF) for q in q_parts],
        scratch_shapes=ext(rows),
        name="attend_merge",
        compiler_params=params(),
    )(scalars, *q_parts, own, guest_kv, guest)


def attend_gathered(tile, split, rows, q_parts, kv_parts):
    masks = list(range(RUN))
    bit = RUN
    while bit < lax.axis_size("tile"):
        kv_parts = kv_parts + [move(jnp.concatenate(kv_parts, 0), bit, 0)]
        masks = masks + [m ^ bit for m in masks]
        bit *= 2
    q_start = (tile ^ jnp.arange(RUN, dtype=jnp.int32)) * rows
    k_start = (tile ^ jnp.array(masks, dtype=jnp.int32)) * rows
    scalars = jnp.concatenate([split[None], q_start, k_start]).astype(jnp.int32)
    return attend_all(scalars, q_parts, kv_parts, rows)


def project_kernel(sc, a0, a1, a2, a3, w, keep, send, lhs):
    step = pl.program_id(0)
    half = a0.shape[0]
    width = a0.shape[1] // 2

    @pl.when(step == 0)
    def _():
        for low in range(RUN):

            @pl.when(sc[1] == low)
            def _(low=low):
                for i, a in enumerate((a0, a1, a2, a3)):
                    cols = slice(width * (low ^ i), width * (low ^ i) + width)
                    lhs[:half, cols] = a[:, :width]
                    lhs[half:, cols] = a[:, width:]

    sums = jnp.dot(lhs[...], w[...], preferred_element_type=F32)

    @pl.when(step == 0)
    def _():
        send[...] = sums.astype(BF)

    @pl.when(step == 1)
    def _():
        keep[...] = sums


def project(low, hid, mask, parts, w):
    rows = 2 * parts[0].shape[0]
    width = w.shape[0]
    scalars = jnp.stack([hid, low]).astype(jnp.int32)

    def full(*shape):
        return pl.BlockSpec(shape, lambda k, sc: (0,) * len(shape))

    return pl.pallas_call(
        project_kernel,
        grid_spec=pltpu.PrefetchScalarGridSpec(
            num_scalar_prefetch=1,
            grid=(2,),
            in_specs=[full(*parts[0].shape)] * RUN
            + [pl.BlockSpec((width, width), lambda k, sc: (0, sc[0] ^ mask ^ (1 - k)))],
            out_specs=[full(rows, width), full(rows, width)],
            scratch_shapes=[pltpu.VMEM((rows, width), BF)],
        ),
        out_shape=[
            jax.ShapeDtypeStruct((rows, width), F32),
            jax.ShapeDtypeStruct((rows, width), BF),
        ],
        name="project",
        compiler_params=params(dimension_semantics=("arbitrary",)),
    )(scalars, *parts, w)


def body(
    item_lengths,
    refresh_slots,
    layer_input,
    key_weight,
    value_weight,
    queries,
    key_cache,
    value_cache,
    out_weight,
):
    rows = queries.shape[0]
    tile = lax.axis_index("tile")
    hid = lax.axis_index("hid")
    tiles = lax.axis_size("tile")
    low = tile % RUN
    split = item_lengths[0]

    x_y = move(layer_input, 0, 2)
    x_c = move(jnp.stack([layer_input, x_y]), 0, 1)
    q_parts = pack_queries(low, queries)
    q_parts = [q_parts[0]] + [move(q_parts[i], i, 0) for i in (1, 2, 3)]
    kv = refresh(
        low,
        hid,
        refresh_slots,
        layer_input,
        x_y,
        x_c,
        key_weight,
        value_weight,
        key_cache,
        value_cache,
    )
    kv_parts = [kv[0]] + [move(kv[i], i, 0) for i in (1, 2, 3)]
    if tiles == 2 * RUN:
        back = attend_items(tile, low, split, rows, q_parts, kv_parts)
    else:
        back = attend_gathered(tile, split, rows, q_parts, kv_parts)
    parts = [back[0]] + [move(back[i], i, 0) for i in (1, 2, 3)]

    keep_y, send_y = project(low, hid, 2, parts, out_weight)
    via_y = (keep_y + move(send_y, 0, 1).astype(F32)).astype(BF)
    got_y = move(via_y, 0, 2)
    keep, send = project(low, hid, 0, parts, out_weight)
    return (keep + move(send, 0, 1).astype(F32) + got_y.astype(F32)).astype(BF)


def solution(mesh):
    return jax.shard_map(
        body,
        mesh=mesh,
        in_specs=(
            P(),
            P("tile"),
            P("tile", "hid"),
            P(None, "hid"),
            P(None, "hid"),
            P("tile", "hid"),
            P("tile", "hid"),
            P("tile", "hid"),
            P("hid", None),
        ),
        out_specs=P("tile", "hid"),
        check_vma=False,
    )
```

```python
import functools

import jax
import jax.numpy as jnp
from jax import lax
from jax.experimental import pallas as pl
from jax.experimental.pallas import tpu as pltpu
from jax.sharding import PartitionSpec as P

HD = 64
BLOCK = 128
RUN = 4
NEG = -1e30
SCALE = 0.125 * 1.4426950408889634
AXES = ("tile", "hid")
BF = jnp.bfloat16
F32 = jnp.float32


def move(value, tile_mask, hid_mask):
    tiles, hids = lax.axis_size("tile"), lax.axis_size("hid")
    pairs = [
        (t * hids + h, (t ^ tile_mask) * hids + (h ^ hid_mask))
        for t in range(tiles)
        for h in range(hids)
    ]
    return lax.ppermute(value, AXES, pairs)


VMEM = pl.BlockSpec(memory_space=pltpu.VMEM)
SMEM = pl.BlockSpec(memory_space=pltpu.SMEM)
ANY = pl.BlockSpec(memory_space=pl.ANY)
TILE, HID, SPLIT, SLOTS = 0, 1, 2, 3
PAD = 16


def call(kernel, name, in_specs, outs, scratch=(), limit=24):
    return pl.pallas_call(
        kernel,
        in_specs=in_specs,
        out_specs=jax.tree.map(lambda _: VMEM, outs),
        out_shape=outs,
        scratch_shapes=list(scratch),
        name=name,
        compiler_params=pltpu.CompilerParams(vmem_limit_bytes=limit * 2**20),
    )


def shape(*dims, dtype=BF):
    return jax.ShapeDtypeStruct(dims, dtype)


def pack_queries_kernel(sc, q_ref, *refs):
    outs, turned = refs[:RUN], refs[RUN]
    low = sc[TILE] % RUN
    width = q_ref.shape[1] // RUN
    turned[...] = q_ref[...].T
    for i in range(RUN):
        rows = pl.ds(pl.multiple_of((low ^ i) * width, width), width)
        outs[i][...] = turned[rows, :]


def prefetch_kernel(sc, x_own, x_c, wk, wv, kc, vc, wo, acc, later, caches, out_w, now, sems):
    hid = sc[HID]
    rows, width = x_own.shape
    busy = sc[SLOTS] >= 0
    for n in range(1, rows // BLOCK):
        busy = busy | (sc[SLOTS + n] >= 0)

    def weights(n):
        w = (wk, wv)[n % 2]
        part = (0, 1, 2, 3)[n // 2]
        start = pl.multiple_of((hid ^ part) * width, width)
        target = now if part < 2 else later
        return pltpu.make_async_copy(w.at[pl.ds(start, width), :], target.at[n % 4], sems.at[n])

    rest = [
        pltpu.make_async_copy(kc, caches.at[0], sems.at[8]),
        pltpu.make_async_copy(vc, caches.at[1], sems.at[9]),
        pltpu.make_async_copy(wo, out_w, sems.at[10]),
    ]

    @pl.when(busy)
    def _():
        for n in range(8):
            weights(n).start()

    for copy in rest:
        copy.start()

    @pl.when(busy)
    def _():
        for part, x in enumerate((x_own, x_c)):
            for n in range(2):
                weights(2 * part + n).wait()
                dots = jnp.dot(x[...], now[2 * part + n], preferred_element_type=F32)
                acc[n] = dots if part == 0 else acc[n] + dots
        for n in range(4, 8):
            weights(n).wait()

    for copy in rest:
        copy.wait()


def refresh_kernel(sc, x_y, x_cy, acc, later, caches, *refs):
    outs, mixed = refs[:RUN], refs[RUN]
    width = x_y.shape[1] // RUN
    blocks = x_y.shape[0] // BLOCK
    low = sc[TILE] % RUN
    fresh = []
    for b in range(blocks):
        hit = sc[SLOTS] == b
        for n in range(1, blocks):
            hit = hit | (sc[SLOTS + n] == b)
        fresh.append(hit)
    busy = fresh[0]
    for hit in fresh[1:]:
        busy = busy | hit

    mixed[...] = caches[...]

    @pl.when(busy)
    def _():
        for n in range(2):
            both = jnp.dot(x_y[...], later[n], preferred_element_type=F32)
            both = both + jnp.dot(x_cy[...], later[2 + n], preferred_element_type=F32)
            total = (acc[n] + both).astype(BF)
            for b in range(blocks):
                rows = slice(b * BLOCK, (b + 1) * BLOCK)
                mixed[n, rows, :] = jnp.where(fresh[b], total[rows, :], caches[n, rows, :])

    for own in range(RUN):

        @pl.when(low == own)
        def _(own=own):
            for i in range(RUN):
                cols = slice(width * (own ^ i), width * (own ^ i) + width)
                outs[i][:, :width] = mixed[0, :, cols]
                outs[i][:, width:] = mixed[1, :, cols]


def item_of(start, dims, axis, split):
    index = start + lax.broadcasted_iota(jnp.int32, dims, axis)
    return jnp.where(index < split, 0, 1)


def query_flags(start, count, split, mask_item=None):
    dims = (HD, count)
    item = item_of(start, dims, 1, split)
    zero, one = item == 0, item == 1
    if mask_item is not None:
        off = item != mask_item
        zero, one = zero | off, one | off
    row = lax.broadcasted_iota(jnp.int32, dims, 0)
    hit = ((row == 0) & zero) | ((row == 1) & one)
    return jnp.where(hit, 1.0, 0.0).astype(BF)


def key_flags(start, count, split):
    dims = (count, HD)
    item = item_of(start, dims, 0, split)
    lane = lax.broadcasted_iota(jnp.int32, dims, 1)
    hit = ((lane == 0) & (item == 1)) | ((lane == 1) & (item == 0))
    return jnp.where(hit, NEG, 0.0).astype(BF)


def extend_keys(kv_refs, starts, split, kext, vext):
    heads = kext.shape[0]
    width = heads * HD
    at = 0
    for kv, start in zip(kv_refs, starts):
        count = kv.shape[0]
        aux = key_flags(start, count, split)
        for h in range(heads):
            cols = slice(h * HD, (h + 1) * HD)
            kext[h, at : at + count, :] = jnp.concatenate([kv[:, cols], aux], 1)
        turned = kv[:, width:].T
        for h in range(heads):
            vext[h, :HD, at : at + count] = turned[h * HD : (h + 1) * HD, :]
            vext[h, HD:, at : at + count] = jnp.ones((PAD, count), BF)
        at += count


def scores_of(kext, h, q_ref, flags):
    q = jnp.concatenate([q_ref[h * HD : (h + 1) * HD, :], flags], 0)
    return jnp.dot(kext[h], q, preferred_element_type=F32)


def softmax_part(s, values):
    top = jnp.max(s, axis=0, keepdims=True)
    p = jnp.exp2((s - top) * SCALE).astype(BF)
    return top, jnp.dot(values, p, preferred_element_type=F32)


def places(sc, rows):
    tile = sc[TILE]
    cube = tile // RUN
    own = [(tile ^ i) * rows for i in range(RUN)]
    far = jnp.where(cube == 0, RUN, RUN - 1) * rows
    edge = (tile % RUN) ^ jnp.where(cube == 0, RUN - 1, 0)
    return cube, own, far, edge


def attend_guest_kernel(sc, q_ref, k0, k1, k2, k3, out, kext, vext):
    heads = kext.shape[0]
    count = q_ref.shape[1]
    cube, own, far, _ = places(sc, count)
    extend_keys((k0, k1, k2, k3), own, sc[SPLIT], kext, vext)
    flags = query_flags(far, count, sc[SPLIT], cube)
    row = lax.broadcasted_iota(jnp.int32, (PAD, count), 0)
    logs = jnp.zeros((PAD, count), F32)
    for h in range(heads):
        top, o = softmax_part(scores_of(kext, h, q_ref, flags), vext[h])
        total = o[HD : HD + 1, :]
        out[h * HD : (h + 1) * HD, :] = (o[:HD, :] / total).astype(BF)
        log = top * SCALE + jnp.log2(total)
        high = log.astype(BF).astype(F32)
        mid = (log - high).astype(BF).astype(F32)
        for n, piece in enumerate((high, mid, log - high - mid)):
            logs = jnp.where(row == 3 * h + n, piece, logs)
    out[heads * HD :, :] = logs.astype(BF)


def attend_own_kernel(sc, q0, q1, q2, q3, k0, k1, k2, k3, out, kext, vext):
    heads = kext.shape[0]
    count = q0.shape[1]
    _, own, _, _ = places(sc, count)
    extend_keys((k0, k1, k2, k3), own, sc[SPLIT], kext, vext)
    for i, q_ref in enumerate((q0, q1, q2, q3)):
        flags = query_flags(own[i], count, sc[SPLIT])
        for h in range(heads):
            top, o = softmax_part(scores_of(kext, h, q_ref, flags), vext[h])
            out[i, h, : HD + 8, :] = o[: HD + 8, :]
            out[i, h, HD + 8 :, :] = jnp.broadcast_to(top, (8, count))


def attend_merge_kernel(sc, q0, q1, q2, q3, part, kv, guest, o0, o1, o2, o3, kext, vext):
    heads = kext.shape[0]
    count = q0.shape[1]
    cube, own, far, edge = places(sc, count)
    extend_keys((kv,), (far,), sc[SPLIT], kext, vext)
    logs = guest[heads * HD :, :].astype(F32)
    for i, (q_ref, out) in enumerate(zip((q0, q1, q2, q3), (o0, o1, o2, o3))):
        flags = query_flags(own[i], count, sc[SPLIT], cube)
        for h in range(heads):
            at = slice(h * HD, (h + 1) * HD)
            s = scores_of(kext, h, q_ref, flags) * SCALE
            log = logs[3 * h : 3 * h + 1, :] + logs[3 * h + 1 : 3 * h + 2, :]
            log = log + logs[3 * h + 2 : 3 * h + 3, :]
            log = jnp.where(edge == i, log, NEG)
            own_log = part[i, h, HD + 8 : HD + 9, :] * SCALE
            top = jnp.maximum(own_log, jnp.max(s, axis=0, keepdims=True))
            top = jnp.maximum(top, log)
            p = jnp.exp2(s - top).astype(BF)
            near = jnp.exp2(own_log - top)
            share = jnp.exp2(log - top)
            o = jnp.dot(vext[h], p, preferred_element_type=F32)
            total = o[HD : HD + 1, :] + part[i, h, HD : HD + 1, :] * near + share
            o = o[:HD, :] + part[i, h, :HD, :] * near + guest[at, :].astype(F32) * share
            out[at, :] = (o / total).astype(BF)


def attend_items(scalars, tile, q_parts, kv_parts):
    rows = kv_parts[0].shape[0]
    heads = q_parts[0].shape[0] // HD
    cube = tile // RUN
    edge = (tile % RUN) ^ jnp.where(cube == 0, RUN - 1, 0)

    def ext(keys):
        return [pltpu.VMEM((heads, keys, 2 * HD), BF), pltpu.VMEM((heads, HD + PAD, keys), BF)]

    guest_q = move(lax.select_n(edge, *q_parts), RUN, 0)
    guest_kv = move(lax.select_n(edge, *kv_parts), RUN, 0)
    guest = call(
        attend_guest_kernel,
        "attend_guest",
        [SMEM] + [VMEM] * 5,
        shape(heads * HD + PAD, rows),
        ext(RUN * rows),
    )(scalars, guest_q, *kv_parts)
    guest = move(guest, RUN, 0)
    own = call(
        attend_own_kernel,
        "attend_own",
        [SMEM] + [VMEM] * 8,
        shape(RUN, heads, HD + PAD, rows, dtype=F32),
        ext(RUN * rows),
    )(scalars, *q_parts, *kv_parts)
    return call(
        attend_merge_kernel,
        "attend_merge",
        [SMEM] + [VMEM] * 7,
        [shape(*q.shape) for q in q_parts],
        ext(rows),
    )(scalars, *q_parts, own, guest_kv, guest)


def attend_all_kernel(sc, starts, q_ref, kv_ref, out, kext, vext, kv_buf, sems, *, slot):
    heads = kext.shape[0]
    keys = kv_ref.shape[0]
    chunk = kv_buf.shape[0]
    flags = query_flags(starts[0], slot, sc[SPLIT])

    def step(j, state):
        rows = pl.ds(pl.multiple_of(j * chunk, chunk), chunk)
        copy = pltpu.make_async_copy(kv_ref.at[rows, :], kv_buf, sems.at[0])
        copy.start()
        copy.wait()
        parts = [kv_buf.at[slice(n * slot, (n + 1) * slot), :] for n in range(chunk // slot)]
        begin = [starts[1 + j * (chunk // slot) + n] for n in range(chunk // slot)]
        extend_keys(parts, begin, sc[SPLIT], kext, vext)
        after = []
        for h in range(heads):
            top, acc = state[h]
            s = scores_of(kext, h, q_ref, flags)
            new = jnp.maximum(top, jnp.max(s, axis=0, keepdims=True))
            p = jnp.exp2((s - new) * SCALE).astype(BF)
            acc = acc * jnp.exp2((top - new) * SCALE)
            after.append((new, acc + jnp.dot(vext[h], p, preferred_element_type=F32)))
        return tuple(after)

    start = jnp.full((1, slot), 2 * NEG, F32), jnp.zeros((HD + PAD, slot), F32)
    state = lax.fori_loop(0, keys // chunk, step, (start,) * heads)
    for h in range(heads):
        o = state[h][1]
        out[h * HD : (h + 1) * HD, :] = (o[:HD, :] / o[HD : HD + 1, :]).astype(BF)


def attend_gathered(scalars, tile, q_parts, kv_parts):
    rows = kv_parts[0].shape[0]
    heads = q_parts[0].shape[0] // HD
    masks = list(range(RUN))
    kv = jnp.concatenate(kv_parts, 0)
    bit = RUN
    while bit < lax.axis_size("tile"):
        kv = jnp.concatenate([kv, move(kv, bit, 0)], 0)
        masks = masks + [m ^ bit for m in masks]
        bit *= 2
    key_starts = (tile ^ jnp.array(masks, dtype=jnp.int32)) * rows
    chunk = RUN * rows
    outs = []
    for i, q in enumerate(q_parts):
        starts = jnp.concatenate([((tile ^ i) * rows)[None], key_starts]).astype(jnp.int32)
        outs.append(
            call(
                functools.partial(attend_all_kernel, slot=rows),
                "attend_all",
                [SMEM, SMEM, VMEM, ANY],
                shape(*q.shape),
                [
                    pltpu.VMEM((heads, chunk, 2 * HD), BF),
                    pltpu.VMEM((heads, HD + PAD, chunk), BF),
                    pltpu.VMEM((chunk, kv.shape[1]), BF),
                    pltpu.SemaphoreType.DMA((1,)),
                ],
            )(scalars, starts, q, kv)
        )
    return outs


def gather_lhs_kernel(sc, a0, a1, a2, a3, w, lhs, out, turned, *, block):
    low = sc[TILE] % RUN
    width = a0.shape[0]
    for i, a in enumerate((a0, a1, a2, a3)):
        rows = pl.ds(pl.multiple_of((low ^ i) * width, width), width)
        turned[rows, :] = a[...]
    lhs[...] = turned[...].T
    out[...] = block_product(sc, lhs, w, block).astype(out.dtype)


def block_product(sc, lhs, w, block):
    width = w.shape[0]
    cols = pl.ds(pl.multiple_of((sc[HID] ^ block) * width, width), width)
    return jnp.dot(lhs[...], w[:, cols], preferred_element_type=F32)


def project_kernel(sc, lhs, w, out, *, block):
    out[...] = block_product(sc, lhs, w, block).astype(out.dtype)


def project(scalars, lhs, w, block, dtype):
    return call(
        functools.partial(project_kernel, block=block),
        "project",
        [SMEM, VMEM, VMEM],
        shape(lhs.shape[0], w.shape[0], dtype=dtype),
    )(scalars, lhs, w)


def body(
    item_lengths,
    refresh_slots,
    layer_input,
    key_weight,
    value_weight,
    queries,
    key_cache,
    value_cache,
    out_weight,
):
    rows, width = queries.shape
    tile = lax.axis_index("tile")
    hid = lax.axis_index("hid")
    scalars = jnp.concatenate([jnp.stack([tile, hid, item_lengths[0]]), refresh_slots])
    scalars = scalars.astype(jnp.int32)

    x_y = move(layer_input, 0, 2)
    x_c = move(layer_input, 0, 1)
    part = width // RUN
    q_parts = call(
        pack_queries_kernel,
        "pack_queries",
        [SMEM, VMEM],
        [shape(part, rows)] * RUN,
        [pltpu.VMEM((width, rows), BF)],
    )(scalars, queries)
    q_parts = [q_parts[0]] + [move(q_parts[i], i, 0) for i in (3, 1, 2)]
    q_parts = [q_parts[0], q_parts[2], q_parts[3], q_parts[1]]
    ready = call(
        prefetch_kernel,
        "prefetch",
        [SMEM, VMEM, VMEM] + [ANY] * 5,
        [
            shape(2, rows, width, dtype=F32),
            shape(4, width, width),
            shape(2, rows, width),
            shape(*out_weight.shape),
        ],
        [pltpu.VMEM((4, width, width), BF), pltpu.SemaphoreType.DMA((11,))],
        28,
    )(scalars, layer_input, x_c, key_weight, value_weight, key_cache, value_cache, out_weight)
    x_y, q_parts, (sums, later, caches, out_w) = lax.optimization_barrier((x_y, q_parts, ready))
    x_cy = move(x_y, 0, 1)
    kv = call(
        refresh_kernel,
        "refresh",
        [SMEM] + [VMEM] * 5,
        [shape(rows, 2 * part)] * RUN,
        [pltpu.VMEM((2, rows, width), BF)],
    )(scalars, x_y, x_cy, sums, later, caches)
    far = move(kv[3], 3, 0)
    kv_parts = [kv[0], move(kv[1], 1, 0), move(kv[2], 2, 0), far]
    if lax.axis_size("tile") == 2 * RUN:
        back = attend_items(scalars, tile, q_parts, kv_parts)
    else:
        back = attend_gathered(scalars, tile, q_parts, kv_parts)
    parts = [back[0]] + [move(back[i], i, 0) for i in (1, 2, 3)]

    lhs, send_y = call(
        functools.partial(gather_lhs_kernel, block=3),
        "project_first",
        [SMEM] + [VMEM] * 5,
        [shape(rows, width), shape(rows, width)],
        [pltpu.VMEM((width, rows), BF)],
    )(scalars, *parts, out_w)
    got = move(send_y, 0, 1)
    keep_y = project(scalars, lhs, out_w, 2, F32)
    via_y = (keep_y + got.astype(F32)).astype(BF)
    via_y, lhs = lax.optimization_barrier((via_y, lhs))
    got_y = move(via_y, 0, 2)
    send = project(scalars, lhs, out_w, 1, BF)
    got = move(send, 0, 1)
    keep = project(scalars, lhs, out_w, 0, F32)
    return (keep + got.astype(F32) + got_y.astype(F32)).astype(BF)


def solution(mesh):
    return jax.shard_map(
        body,
        mesh=mesh,
        in_specs=(
            P(),
            P("tile"),
            P("tile", "hid"),
            P(None, "hid"),
            P(None, "hid"),
            P("tile", "hid"),
            P("tile", "hid"),
            P("tile", "hid"),
            P("hid", None),
        ),
        out_specs=P("tile", "hid"),
        check_vma=False,
    )
```

```python
import functools

import jax
import jax.numpy as jnp
from jax import lax
from jax.experimental import pallas as pl
from jax.experimental.pallas import tpu as pltpu
from jax.sharding import PartitionSpec as P

HD = 64
BLOCK = 128
RUN = 4
NEG = -1e30
SCALE = 0.125 * 1.4426950408889634
AXES = ("tile", "hid")
BF = jnp.bfloat16
F32 = jnp.float32


def move(value, tile_mask, hid_mask):
    tiles, hids = lax.axis_size("tile"), lax.axis_size("hid")
    pairs = [
        (t * hids + h, (t ^ tile_mask) * hids + (h ^ hid_mask))
        for t in range(tiles)
        for h in range(hids)
    ]
    return lax.ppermute(value, AXES, pairs)


VMEM = pl.BlockSpec(memory_space=pltpu.VMEM)
SMEM = pl.BlockSpec(memory_space=pltpu.SMEM)
HBM = pl.BlockSpec(memory_space=pltpu.HBM)
TILE, HID, SPLIT, SLOTS = 0, 1, 2, 3
PAD = 16


def call(kernel, name, in_specs, outs, scratch=(), limit=24):
    return pl.pallas_call(
        kernel,
        in_specs=in_specs,
        out_specs=jax.tree.map(lambda _: VMEM, outs),
        out_shape=outs,
        scratch_shapes=list(scratch),
        name=name,
        compiler_params=pltpu.CompilerParams(vmem_limit_bytes=limit * 2**20),
    )


def shape(*dims, dtype=BF):
    return jax.ShapeDtypeStruct(dims, dtype)


def pieces(group, heads):
    pair = heads // 2 * 2
    single = heads - pair
    out = [(0, pl.multiple_of(group * (pair * HD), pair * HD), pair * HD)] if pair else []
    if single:
        start = RUN * pair * HD + group * HD
        out.append((pair * HD, pl.multiple_of(start, HD), HD))
    return out


def pack_queries_kernel(sc, q_ref, *refs):
    outs, (buf, turned, sems) = refs[:RUN], refs[RUN:]
    copy = pltpu.make_async_copy(q_ref, buf, sems.at[0])
    copy.start()
    copy.wait()
    turned[...] = buf[...].T
    for i in range(RUN):
        for at, start, size in pieces(sc[TILE] % RUN ^ i, outs[i].shape[0] // HD):
            outs[i][at : at + size, :] = turned[pl.ds(start, size), :]


def prefetch_kernel(sc, x_in, x_c, wk, wv, kc, vc, acc, later, caches, token, x_own, now, sems):
    hid = sc[HID]
    rows, width = x_own.shape
    token[...] = jnp.zeros(token.shape, F32)
    busy = sc[SLOTS] >= 0
    for n in range(1, rows // BLOCK):
        busy = busy | (sc[SLOTS + n] >= 0)

    def weights(n):
        w = (wk, wv)[n % 2]
        part = (0, 1, 2, 3)[n // 2]
        start = pl.multiple_of((hid ^ part) * width, width)
        target = now if part < 2 else later
        return pltpu.make_async_copy(w.at[pl.ds(start, width), :], target.at[n % 4], sems.at[n])

    rest = [
        pltpu.make_async_copy(kc, caches.at[0], sems.at[8]),
        pltpu.make_async_copy(vc, caches.at[1], sems.at[9]),
    ]
    own = pltpu.make_async_copy(x_in, x_own, sems.at[10])
    own.start()

    @pl.when(busy)
    def _():
        for n in range(8):
            weights(n).start()

    for copy in rest:
        copy.start()
    own.wait()

    @pl.when(busy)
    def _():
        for part, x in enumerate((x_own, x_c)):
            for n in range(2):
                weights(2 * part + n).wait()
                dots = jnp.dot(x[...], now[2 * part + n], preferred_element_type=F32)
                acc[n] = dots if part == 0 else acc[n] + dots
        for n in range(4, 8):
            weights(n).wait()

    for copy in rest:
        copy.wait()


def refresh_kernel(sc, x_y, x_cy, acc, later, caches, *refs):
    outs, mixed = refs[:RUN], refs[RUN]
    width = x_y.shape[1] // RUN
    blocks = x_y.shape[0] // BLOCK
    low = sc[TILE] % RUN
    fresh = []
    for b in range(blocks):
        hit = sc[SLOTS] == b
        for n in range(1, blocks):
            hit = hit | (sc[SLOTS + n] == b)
        fresh.append(hit)
    busy = fresh[0]
    for hit in fresh[1:]:
        busy = busy | hit

    mixed[...] = caches[...]

    @pl.when(busy)
    def _():
        for n in range(2):
            both = jnp.dot(x_y[...], later[n], preferred_element_type=F32)
            both = both + jnp.dot(x_cy[...], later[2 + n], preferred_element_type=F32)
            total = (acc[n] + both).astype(BF)
            for b in range(blocks):
                rows = slice(b * BLOCK, (b + 1) * BLOCK)
                mixed[n, rows, :] = jnp.where(fresh[b], total[rows, :], caches[n, rows, :])

    heads = width // HD
    pair = heads // 2 * 2 * HD
    upper = lax.broadcasted_iota(jnp.int32, (x_y.shape[0], 2 * HD), 1) >= HD
    for i in range(RUN):
        group = low ^ i
        cols = pl.ds(pl.multiple_of(group * pair, 2 * HD), pair)
        outs[i][:, :pair] = mixed[0, :, cols]
        outs[i][:, pair : 2 * pair] = mixed[1, :, cols]
        if heads % 2:
            cols = pl.ds(pl.multiple_of(RUN * pair + group // 2 * (2 * HD), 2 * HD), 2 * HD)
            keys, values = mixed[0, :, cols], mixed[1, :, cols]

            @pl.when(group % 2 == 0)
            def _():
                outs[i][:, 2 * pair :] = jnp.where(upper, pltpu.roll(values, HD, 1), keys)

            @pl.when(group % 2 == 1)
            def _():
                outs[i][:, 2 * pair :] = jnp.where(upper, values, pltpu.roll(keys, HD, 1))


def item_of(start, dims, axis, split):
    index = start + lax.broadcasted_iota(jnp.int32, dims, axis)
    return jnp.where(index < split, 0, 1)


def query_flags(start, count, split, mask_item=None):
    dims = (HD, count)
    item = item_of(start, dims, 1, split)
    zero, one = item == 0, item == 1
    if mask_item is not None:
        off = item != mask_item
        zero, one = zero | off, one | off
    row = lax.broadcasted_iota(jnp.int32, dims, 0)
    hit = ((row == 0) & zero) | ((row == 1) & one)
    return jnp.where(hit, 1.0, 0.0).astype(BF)


def key_flags(start, count, split):
    dims = (count, HD)
    item = item_of(start, dims, 0, split)
    lane = lax.broadcasted_iota(jnp.int32, dims, 1)
    hit = ((lane == 0) & (item == 1)) | ((lane == 1) & (item == 0))
    return jnp.where(hit, NEG, 0.0).astype(BF)


def head_cols(h, heads):
    pair = heads // 2 * 2
    if h < pair:
        return h * HD, (pair + h) * HD
    return 2 * pair * HD, (2 * pair + 1) * HD


def extend_keys(kv_refs, starts, split, kext, vext):
    heads = kext.shape[0]
    at = 0
    for kv, start in zip(kv_refs, starts):
        count = kv.shape[0]
        aux = key_flags(start, count, split)
        for h in range(heads):
            key_col, value_col = head_cols(h, heads)
            keys = kv[:, key_col : key_col + HD]
            kext[h, at : at + count, :] = jnp.concatenate([keys, aux], 1)
            vext[h, :HD, at : at + count] = kv[:, value_col : value_col + HD].T
            vext[h, HD:, at : at + count] = jnp.ones((PAD, count), BF)
        at += count


def scores_of(kext, h, q_ref, flags):
    q = jnp.concatenate([q_ref[h * HD : (h + 1) * HD, :], flags], 0)
    return jnp.dot(kext[h], q, preferred_element_type=F32)


def softmax_part(s, values):
    top = jnp.max(s, axis=0, keepdims=True)
    p = jnp.exp2((s - top) * SCALE).astype(BF)
    return top, jnp.dot(values, p, preferred_element_type=F32)


def places(sc, rows):
    tile = sc[TILE]
    cube = tile // RUN
    own = [(tile ^ i) * rows for i in range(RUN)]
    far = jnp.where(cube == 0, RUN, RUN - 1) * rows
    edge = (tile % RUN) ^ jnp.where(cube == 0, RUN - 1, 0)
    return cube, own, far, edge


def attend_guest_kernel(sc, q_ref, k0, k1, k2, k3, out, kext, vext):
    heads = kext.shape[0]
    count = q_ref.shape[1]
    cube, own, far, _ = places(sc, count)
    extend_keys((k0, k1, k2, k3), own, sc[SPLIT], kext, vext)
    flags = query_flags(far, count, sc[SPLIT], cube)
    row = lax.broadcasted_iota(jnp.int32, (PAD, count), 0)
    logs = jnp.zeros((PAD, count), F32)
    for h in range(heads):
        top, o = softmax_part(scores_of(kext, h, q_ref, flags), vext[h])
        total = o[HD : HD + 1, :]
        out[h * HD : (h + 1) * HD, :] = (o[:HD, :] / total).astype(BF)
        log = top * SCALE + jnp.log2(total)
        high = log.astype(BF).astype(F32)
        mid = (log - high).astype(BF).astype(F32)
        for n, piece in enumerate((high, mid, log - high - mid)):
            logs = jnp.where(row == 3 * h + n, piece, logs)
    out[heads * HD :, :] = logs.astype(BF)


def attend_own_kernel(sc, wo, q0, q1, q2, q3, k0, k1, k2, k3, out, out_w, kext, vext, sems):
    copy = pltpu.make_async_copy(wo, out_w, sems.at[0])
    copy.start()
    heads = kext.shape[0]
    count = q0.shape[1]
    _, own, _, _ = places(sc, count)
    extend_keys((k0, k1, k2, k3), own, sc[SPLIT], kext, vext)
    for i, q_ref in enumerate((q0, q1, q2, q3)):
        flags = query_flags(own[i], count, sc[SPLIT])
        for h in range(heads):
            top, o = softmax_part(scores_of(kext, h, q_ref, flags), vext[h])
            out[i, h, : HD + 8, :] = o[: HD + 8, :]
            out[i, h, HD + 8 :, :] = jnp.broadcast_to(top, (8, count))
    copy.wait()


def attend_merge_kernel(sc, q0, q1, q2, q3, part, kv, guest, o0, o1, o2, o3, kext, vext):
    heads = kext.shape[0]
    count = q0.shape[1]
    cube, own, far, edge = places(sc, count)
    extend_keys((kv,), (far,), sc[SPLIT], kext, vext)
    logs = guest[heads * HD :, :].astype(F32)
    for i, (q_ref, out) in enumerate(zip((q0, q1, q2, q3), (o0, o1, o2, o3))):
        flags = query_flags(own[i], count, sc[SPLIT], cube)
        for h in range(heads):
            at = slice(h * HD, (h + 1) * HD)
            s = scores_of(kext, h, q_ref, flags) * SCALE
            log = logs[3 * h : 3 * h + 1, :] + logs[3 * h + 1 : 3 * h + 2, :]
            log = log + logs[3 * h + 2 : 3 * h + 3, :]
            log = jnp.where(edge == i, log, NEG)
            own_log = part[i, h, HD + 8 : HD + 9, :] * SCALE
            top = jnp.maximum(own_log, jnp.max(s, axis=0, keepdims=True))
            top = jnp.maximum(top, log)
            p = jnp.exp2(s - top).astype(BF)
            near = jnp.exp2(own_log - top)
            share = jnp.exp2(log - top)
            o = jnp.dot(vext[h], p, preferred_element_type=F32)
            total = o[HD : HD + 1, :] + part[i, h, HD : HD + 1, :] * near + share
            o = o[:HD, :] + part[i, h, :HD, :] * near + guest[at, :].astype(F32) * share
            out[at, :] = (o / total).astype(BF)


def attend_items(scalars, tile, q_parts, kv_parts, out_weight):
    rows = kv_parts[0].shape[0]
    heads = q_parts[0].shape[0] // HD
    cube = tile // RUN
    edge = (tile % RUN) ^ jnp.where(cube == 0, RUN - 1, 0)

    def ext(keys):
        return [pltpu.VMEM((heads, keys, 2 * HD), BF), pltpu.VMEM((heads, HD + PAD, keys), BF)]

    guest_q = move(lax.select_n(edge, *q_parts), RUN, 0)
    guest_kv = move(lax.select_n(edge, *kv_parts), RUN, 0)
    guest = call(
        attend_guest_kernel,
        "attend_guest",
        [SMEM] + [VMEM] * 5,
        shape(heads * HD + PAD, rows),
        ext(RUN * rows),
    )(scalars, guest_q, *kv_parts)
    guest = move(guest, RUN, 0)
    own, out_w = call(
        attend_own_kernel,
        "attend_own",
        [SMEM, HBM] + [VMEM] * 8,
        [shape(RUN, heads, HD + PAD, rows, dtype=F32), shape(*out_weight.shape)],
        ext(RUN * rows) + [pltpu.SemaphoreType.DMA((1,))],
    )(scalars, out_weight, *q_parts, *kv_parts)
    return out_w, call(
        attend_merge_kernel,
        "attend_merge",
        [SMEM] + [VMEM] * 7,
        [shape(*q.shape) for q in q_parts],
        ext(rows),
    )(scalars, *q_parts, own, guest_kv, guest)


def attend_all_kernel(sc, starts, q_ref, kv_ref, out, kext, vext, kv_buf, sems, *, slot):
    heads = kext.shape[0]
    keys = kv_ref.shape[0]
    chunk = kv_buf.shape[0]
    flags = query_flags(starts[0], slot, sc[SPLIT])

    def step(j, state):
        rows = pl.ds(pl.multiple_of(j * chunk, chunk), chunk)
        copy = pltpu.make_async_copy(kv_ref.at[rows, :], kv_buf, sems.at[0])
        copy.start()
        copy.wait()
        parts = [kv_buf.at[slice(n * slot, (n + 1) * slot), :] for n in range(chunk // slot)]
        begin = [starts[1 + j * (chunk // slot) + n] for n in range(chunk // slot)]
        extend_keys(parts, begin, sc[SPLIT], kext, vext)
        after = []
        for h in range(heads):
            top, acc = state[h]
            s = scores_of(kext, h, q_ref, flags)
            new = jnp.maximum(top, jnp.max(s, axis=0, keepdims=True))
            p = jnp.exp2((s - new) * SCALE).astype(BF)
            acc = acc * jnp.exp2((top - new) * SCALE)
            after.append((new, acc + jnp.dot(vext[h], p, preferred_element_type=F32)))
        return tuple(after)

    start = jnp.full((1, slot), 2 * NEG, F32), jnp.zeros((HD + PAD, slot), F32)
    state = lax.fori_loop(0, keys // chunk, step, (start,) * heads)
    for h in range(heads):
        o = state[h][1]
        out[h * HD : (h + 1) * HD, :] = (o[:HD, :] / o[HD : HD + 1, :]).astype(BF)


def attend_gathered(scalars, tile, q_parts, kv_parts):
    rows = kv_parts[0].shape[0]
    heads = q_parts[0].shape[0] // HD
    masks = list(range(RUN))
    kv = jnp.concatenate(kv_parts, 0)
    bit = RUN
    while bit < lax.axis_size("tile"):
        kv = jnp.concatenate([kv, move(kv, bit, 0)], 0)
        masks = masks + [m ^ bit for m in masks]
        bit *= 2
    key_starts = (tile ^ jnp.array(masks, dtype=jnp.int32)) * rows
    chunk = RUN * rows
    outs = []
    for i, q in enumerate(q_parts):
        starts = jnp.concatenate([((tile ^ i) * rows)[None], key_starts]).astype(jnp.int32)
        outs.append(
            call(
                functools.partial(attend_all_kernel, slot=rows),
                "attend_all",
                [SMEM, SMEM, VMEM, HBM],
                shape(*q.shape),
                [
                    pltpu.VMEM((heads, chunk, 2 * HD), BF),
                    pltpu.VMEM((heads, HD + PAD, chunk), BF),
                    pltpu.VMEM((chunk, kv.shape[1]), BF),
                    pltpu.SemaphoreType.DMA((1,)),
                ],
            )(scalars, starts, q, kv)
        )
    return outs


def gather_lhs_kernel(sc, a0, a1, a2, a3, w, lhs, out, turned, *, block):
    for i, a in enumerate((a0, a1, a2, a3)):
        for at, start, size in pieces(sc[TILE] % RUN ^ i, a.shape[0] // HD):
            turned[pl.ds(start, size), :] = a[at : at + size, :]
    lhs[...] = turned[...].T
    out[...] = block_product(sc, lhs, w, block).astype(out.dtype)


def block_product(sc, lhs, w, block):
    width = w.shape[0]
    cols = pl.ds(pl.multiple_of((sc[HID] ^ block) * width, width), width)
    return jnp.dot(lhs[...], w[:, cols], preferred_element_type=F32)


def project_kernel(sc, lhs, w, out, *, block):
    out[...] = block_product(sc, lhs, w, block).astype(out.dtype)


def project(scalars, lhs, w, block, dtype):
    return call(
        functools.partial(project_kernel, block=block),
        "project",
        [SMEM, VMEM, VMEM],
        shape(lhs.shape[0], w.shape[0], dtype=dtype),
    )(scalars, lhs, w)


def body(
    item_lengths,
    refresh_slots,
    layer_input,
    key_weight,
    value_weight,
    queries,
    key_cache,
    value_cache,
    out_weight,
):
    rows, width = queries.shape
    tile = lax.axis_index("tile")
    hid = lax.axis_index("hid")
    scalars = jnp.concatenate([jnp.stack([tile, hid, item_lengths[0]]), refresh_slots])
    scalars = scalars.astype(jnp.int32)

    stay = functools.partial(pltpu.with_memory_space_constraint, memory_space=pltpu.HBM)
    x_y = move(layer_input, 0, 2)
    x_c = move(layer_input, 0, 1)
    part = width // RUN
    q_parts = call(
        pack_queries_kernel,
        "pack_queries",
        [SMEM, HBM],
        [shape(part, rows)] * RUN,
        [
            pltpu.VMEM((rows, width), BF),
            pltpu.VMEM((width, rows), BF),
            pltpu.SemaphoreType.DMA((1,)),
        ],
    )(scalars, stay(queries))
    q_parts = [q_parts[0]] + [move(q_parts[i], i, 0) for i in (3, 1, 2)]
    q_parts = [q_parts[0], q_parts[2], q_parts[3], q_parts[1]]
    ready = call(
        prefetch_kernel,
        "prefetch",
        [SMEM, HBM, VMEM] + [HBM] * 4,
        [
            shape(2, rows, width, dtype=F32),
            shape(4, width, width),
            shape(2, rows, width),
            shape(8, 128, dtype=F32),
        ],
        [
            pltpu.VMEM((rows, width), BF),
            pltpu.VMEM((4, width, width), BF),
            pltpu.SemaphoreType.DMA((11,)),
        ],
    )(
        scalars,
        stay(layer_input),
        x_c,
        stay(key_weight),
        stay(value_weight),
        stay(key_cache),
        stay(value_cache),
    )
    sums, later, caches, token = ready
    x_y, q_parts[3], token = lax.optimization_barrier((x_y, q_parts[3], token))
    x_cy = move(x_y, 0, 1)
    x_cy, q_parts[1], q_parts[2] = lax.optimization_barrier((x_cy, q_parts[1], q_parts[2]))
    kv = call(
        refresh_kernel,
        "refresh",
        [SMEM] + [VMEM] * 5,
        [shape(rows, 2 * part)] * RUN,
        [pltpu.VMEM((2, rows, width), BF)],
    )(scalars, x_y, x_cy, sums, later, caches)
    far = move(kv[3], 3, 0)
    kv_parts = [kv[0], move(kv[1], 1, 0), move(kv[2], 2, 0), far]
    if lax.axis_size("tile") == 2 * RUN:
        out_w, back = attend_items(scalars, tile, q_parts, kv_parts, stay(out_weight))
    else:
        out_w, back = out_weight, attend_gathered(scalars, tile, q_parts, kv_parts)
    parts = [back[0]] + [move(back[i], i, 0) for i in (1, 2, 3)]

    lhs, send_y = call(
        functools.partial(gather_lhs_kernel, block=3),
        "project_first",
        [SMEM] + [VMEM] * 5,
        [shape(rows, width), shape(rows, width)],
        [pltpu.VMEM((width, rows), BF)],
    )(scalars, *parts, out_w)
    got = move(send_y, 0, 1)
    keep_y = project(scalars, lhs, out_w, 2, F32)
    via_y = (keep_y + got.astype(F32)).astype(BF)
    via_y, lhs = lax.optimization_barrier((via_y, lhs))
    got_y = move(via_y, 0, 2)
    send = project(scalars, lhs, out_w, 1, BF)
    got = move(send, 0, 1)
    keep = project(scalars, lhs, out_w, 0, F32)
    return (keep + got.astype(F32) + got_y.astype(F32)).astype(BF)


def solution(mesh):
    return jax.shard_map(
        body,
        mesh=mesh,
        in_specs=(
            P(),
            P("tile"),
            P("tile", "hid"),
            P(None, "hid"),
            P(None, "hid"),
            P("tile", "hid"),
            P("tile", "hid"),
            P("tile", "hid"),
            P("hid", None),
        ),
        out_specs=P("tile", "hid"),
        check_vma=False,
    )
```

```python
import functools

import jax
import jax.numpy as jnp
from jax import lax
from jax.experimental import pallas as pl
from jax.experimental.pallas import tpu as pltpu
from jax.sharding import PartitionSpec as P

HD = 64
BLOCK = 128
RUN = 4
NEG = -1e30
SCALE = 0.125 * 1.4426950408889634
AXES = ("tile", "hid")
BF = jnp.bfloat16
F32 = jnp.float32


def move(value, tile_mask, hid_mask):
    tiles, hids = lax.axis_size("tile"), lax.axis_size("hid")
    pairs = [
        (t * hids + h, (t ^ tile_mask) * hids + (h ^ hid_mask))
        for t in range(tiles)
        for h in range(hids)
    ]
    return lax.ppermute(value, AXES, pairs)


VMEM = pl.BlockSpec(memory_space=pltpu.VMEM)
SMEM = pl.BlockSpec(memory_space=pltpu.SMEM)
HBM = pl.BlockSpec(memory_space=pltpu.HBM)
PAD = 16


def call(kernel, name, in_specs, outs, scratch=(), limit=24):
    return pl.pallas_call(
        kernel,
        in_specs=in_specs,
        out_specs=jax.tree.map(lambda _: VMEM, outs),
        out_shape=outs,
        scratch_shapes=list(scratch),
        name=name,
        compiler_params=pltpu.CompilerParams(vmem_limit_bytes=limit * 2**20),
    )


def shape(*dims, dtype=BF):
    return jax.ShapeDtypeStruct(dims, dtype)


def pieces(group, heads):
    pair = heads // 2 * 2
    single = heads - pair
    out = [(0, pl.multiple_of(group * (pair * HD), pair * HD), pair * HD)] if pair else []
    if single:
        start = RUN * pair * HD + group * HD
        out.append((pair * HD, pl.multiple_of(start, HD), HD))
    return out


def prefetch_kernel(sc, x_in, x_c, q_in, wk, wv, kc, vc, *refs):
    acc, caches, token = refs[:3]
    later, outs = refs[3:7], refs[7 : 7 + RUN]
    x_own, now, q_buf, turned, sems = refs[7 + RUN :]
    query = pltpu.make_async_copy(q_in, q_buf, sems.at[11])
    query.start()
    hid = lax.axis_index("hid")
    rows, width = x_own.shape
    token[...] = jnp.zeros(token.shape, F32)
    busy = sc[0] >= 0
    for n in range(1, rows // BLOCK):
        busy = busy | (sc[n] >= 0)

    def weights(n):
        w = (wk, wv)[n % 2]
        part = (0, 1, 2, 3)[n // 2]
        start = pl.multiple_of((hid ^ part) * width, width)
        target = now.at[n] if part < 2 else later[n % 4]
        return pltpu.make_async_copy(w.at[pl.ds(start, width), :], target, sems.at[n])

    rest = [
        pltpu.make_async_copy(kc, caches.at[0], sems.at[8]),
        pltpu.make_async_copy(vc, caches.at[1], sems.at[9]),
    ]
    own = pltpu.make_async_copy(x_in, x_own, sems.at[10])
    own.start()

    @pl.when(busy)
    def _():
        for n in range(8):
            weights(n).start()

    for copy in rest:
        copy.start()
    query.wait()
    turned[...] = q_buf[...].T
    for i in range(RUN):
        for at, start, size in pieces(lax.axis_index("tile") % RUN ^ i, outs[i].shape[0] // HD):
            outs[i][at : at + size, :] = turned[pl.ds(start, size), :]
    own.wait()

    @pl.when(busy)
    def _():
        for part, x in enumerate((x_own, x_c)):
            for n in range(2):
                weights(2 * part + n).wait()
                dots = jnp.dot(x[...], now[2 * part + n], preferred_element_type=F32)
                acc[n] = dots if part == 0 else acc[n] + dots
        for n in range(4, 8):
            weights(n).wait()

    for copy in rest:
        copy.wait()


def refresh_kernel(sc, x_y, x_cy, acc, caches, token, *refs):
    later, outs, mixed = refs[:4], refs[4 : 4 + RUN], refs[4 + RUN]
    width = x_y.shape[1] // RUN
    blocks = x_y.shape[0] // BLOCK
    low = lax.axis_index("tile") % RUN
    fresh = []
    for b in range(blocks):
        hit = sc[0] == b
        for n in range(1, blocks):
            hit = hit | (sc[n] == b)
        fresh.append(hit)
    busy = fresh[0]
    for hit in fresh[1:]:
        busy = busy | hit

    mixed[...] = caches[...]

    @pl.when(busy)
    def _():
        for n in range(2):
            both = jnp.dot(x_y[...], later[n][...], preferred_element_type=F32)
            both = both + jnp.dot(x_cy[...], later[2 + n][...], preferred_element_type=F32)
            total = (acc[n] + both).astype(BF)
            for b in range(blocks):
                rows = slice(b * BLOCK, (b + 1) * BLOCK)
                mixed[n, rows, :] = jnp.where(fresh[b], total[rows, :], caches[n, rows, :])

    heads = width // HD
    pair = heads // 2 * 2 * HD
    upper = lax.broadcasted_iota(jnp.int32, (x_y.shape[0], 2 * HD), 1) >= HD
    for i in range(RUN):
        group = low ^ i
        cols = pl.ds(pl.multiple_of(group * pair, 2 * HD), pair)
        outs[i][:, :pair] = mixed[0, :, cols]
        outs[i][:, pair : 2 * pair] = mixed[1, :, cols]
        if heads % 2:
            cols = pl.ds(pl.multiple_of(RUN * pair + group // 2 * (2 * HD), 2 * HD), 2 * HD)
            keys, values = mixed[0, :, cols], mixed[1, :, cols]

            @pl.when(group % 2 == 0)
            def _():
                outs[i][:, 2 * pair :] = jnp.where(upper, pltpu.roll(values, HD, 1), keys)

            @pl.when(group % 2 == 1)
            def _():
                outs[i][:, 2 * pair :] = jnp.where(upper, values, pltpu.roll(keys, HD, 1))


def item_of(start, dims, axis, split):
    index = start + lax.broadcasted_iota(jnp.int32, dims, axis)
    return jnp.where(index < split, 0, 1)


def query_flags(start, count, split, mask_item=None):
    dims = (HD, count)
    item = item_of(start, dims, 1, split)
    zero, one = item == 0, item == 1
    if mask_item is not None:
        off = item != mask_item
        zero, one = zero | off, one | off
    row = lax.broadcasted_iota(jnp.int32, dims, 0)
    hit = ((row == 0) & zero) | ((row == 1) & one)
    return jnp.where(hit, 1.0, 0.0).astype(BF)


def key_flags(start, count, split):
    dims = (count, HD)
    item = item_of(start, dims, 0, split)
    lane = lax.broadcasted_iota(jnp.int32, dims, 1)
    hit = ((lane == 0) & (item == 1)) | ((lane == 1) & (item == 0))
    return jnp.where(hit, NEG, 0.0).astype(BF)


def head_cols(h, heads):
    pair = heads // 2 * 2
    if h < pair:
        return h * HD, (pair + h) * HD
    return 2 * pair * HD, (2 * pair + 1) * HD


def extend_keys(kv_refs, starts, split, kext, vext):
    heads = kext.shape[0]
    at = 0
    for kv, start in zip(kv_refs, starts):
        count = kv.shape[0]
        aux = key_flags(start, count, split)
        for h in range(heads):
            key_col, value_col = head_cols(h, heads)
            keys = kv[:, key_col : key_col + HD]
            kext[h, at : at + count, :] = jnp.concatenate([keys, aux], 1)
            vext[h, :HD, at : at + count] = kv[:, value_col : value_col + HD].T
            vext[h, HD:, at : at + count] = jnp.ones((PAD, count), BF)
        at += count


def scores_of(kext, h, q_ref, flags):
    q = jnp.concatenate([q_ref[h * HD : (h + 1) * HD, :], flags], 0)
    return jnp.dot(kext[h], q, preferred_element_type=F32)


DEPTH = 3


def score_stream(units, score):
    ahead = [score(u) for u in units[:DEPTH]]
    for n, unit in enumerate(units):
        if n + DEPTH < len(units):
            ahead.append(score(units[n + DEPTH]))
        yield unit, ahead.pop(0)


def softmax_part(s, values):
    top = jnp.max(s, axis=0, keepdims=True)
    p = jnp.exp2((s - top) * SCALE).astype(BF)
    return top, jnp.dot(values, p, preferred_element_type=F32)


def places(rows):
    tile = lax.axis_index("tile")
    cube = tile // RUN
    own = [(tile ^ i) * rows for i in range(RUN)]
    far = jnp.where(cube == 0, RUN, RUN - 1) * rows
    edge = (tile % RUN) ^ jnp.where(cube == 0, RUN - 1, 0)
    return cube, own, far, edge


def pick_edge_kernel(q0, q1, q2, q3, out):
    edge = places(1)[3]
    for i, q in enumerate((q0, q1, q2, q3)):

        @pl.when(edge == i)
        def _(q=q):
            out[...] = q[...]


def attend_guest_kernel(sc, q_ref, k0, k1, k2, k3, out, kext, vext):
    heads = kext.shape[0]
    count = q_ref.shape[1]
    cube, own, far, _ = places(count)
    extend_keys((k0, k1, k2, k3), own, sc[0], kext, vext)
    flags = query_flags(far, count, sc[0], cube)
    row = lax.broadcasted_iota(jnp.int32, (PAD, count), 0)
    logs = jnp.zeros((PAD, count), F32)
    for h, s in score_stream(list(range(heads)), lambda h: scores_of(kext, h, q_ref, flags)):
        top, o = softmax_part(s, vext[h])
        total = o[HD : HD + 1, :]
        out[h * HD : (h + 1) * HD, :] = (o[:HD, :] / total).astype(BF)
        log = top * SCALE + jnp.log2(total)
        high = log.astype(BF).astype(F32)
        mid = (log - high).astype(BF).astype(F32)
        for n, piece in enumerate((high, mid, log - high - mid)):
            logs = jnp.where(row == 3 * h + n, piece, logs)
    out[heads * HD :, :] = logs.astype(BF)


def slot_scores(sc, q_refs, starts, kext, mask_item=None):
    heads = kext.shape[0]
    count = q_refs[0].shape[1]
    flags = [query_flags(start, count, sc[0], mask_item) for start in starts]
    units = [(i, h) for i in range(len(q_refs)) for h in range(heads)]
    return score_stream(units, lambda u: scores_of(kext, u[1], q_refs[u[0]], flags[u[0]]))


def attend_own_kernel(sc, wo, q0, q1, q2, q3, kext, vext, out, out_w, sems):
    copy = pltpu.make_async_copy(wo, out_w, sems.at[0])
    copy.start()
    count = q0.shape[1]
    _, own, _, _ = places(count)
    for (i, h), s in slot_scores(sc, (q0, q1, q2, q3), own, kext):
        top, o = softmax_part(s, vext[h])
        out[i, h, : HD + 8, :] = o[: HD + 8, :]
        out[i, h, HD + 8 :, :] = jnp.broadcast_to(top, (8, count))
    copy.wait()


def attend_merge_kernel(sc, q0, q1, q2, q3, part, b0, b1, b2, b3, guest, *refs):
    outs, (kv, kext, vext) = refs[:RUN], refs[RUN:]
    heads = kext.shape[0]
    count = q0.shape[1]
    cube, own, far, edge = places(count)
    kv[...] = (b0[...] + b1[...]) + (b2[...] + b3[...])
    extend_keys((kv,), (far,), sc[0], kext, vext)
    logs = guest[heads * HD :, :].astype(F32)
    for (i, h), s in slot_scores(sc, (q0, q1, q2, q3), own, kext, cube):
        at = slice(h * HD, (h + 1) * HD)
        log = logs[3 * h : 3 * h + 1, :] + logs[3 * h + 1 : 3 * h + 2, :]
        log = log + logs[3 * h + 2 : 3 * h + 3, :]
        log = jnp.where(edge == i, log, NEG)
        own_log = part[i, h, HD + 8 : HD + 9, :] * SCALE
        top = jnp.maximum(own_log, jnp.max(s, axis=0, keepdims=True) * SCALE)
        top = jnp.maximum(top, log)
        p = jnp.exp2(s * SCALE - top).astype(BF)
        near = jnp.exp2(own_log - top)
        share = jnp.exp2(log - top)
        o = jnp.dot(vext[h], p, preferred_element_type=F32)
        total = o[HD : HD + 1, :] + part[i, h, HD : HD + 1, :] * near + share
        o = o[:HD, :] + part[i, h, :HD, :] * near + guest[at, :].astype(F32) * share
        outs[i][at, :] = (o / total).astype(BF)


def send_tiles(value, tile_pairs):
    hids = lax.axis_size("hid")
    pairs = [(s * hids + h, d * hids + h) for s, d in tile_pairs for h in range(hids)]
    return lax.ppermute(value, AXES, pairs)


def attend_items(lengths, q_parts, kv, kv_parts, out_weight):
    rows = kv[0].shape[0]
    heads = q_parts[0].shape[0] // HD
    ext = [shape(heads, RUN * rows, 2 * HD), shape(heads, HD + PAD, RUN * rows)]

    guest_q = call(pick_edge_kernel, "pick_edge", [VMEM] * RUN, shape(*q_parts[0].shape))(*q_parts)
    guest_q = move(guest_q, RUN, 0)
    first, last = RUN - 1, RUN
    guest_kv = [
        send_tiles(kv[i], [(first, last + (first ^ i)), (last, i)]) for i in (0, 2, 3)
    ] + [send_tiles(kv_parts[1], [(first ^ 1, last + (first ^ 1)), (last ^ 1, 1)])]
    guest, kext, vext = call(
        attend_guest_kernel,
        "attend_guest",
        [SMEM] + [VMEM] * 5,
        [shape(heads * HD + PAD, rows)] + ext,
    )(lengths, guest_q, *kv_parts)
    guest = move(guest, RUN, 0)
    own, out_w = call(
        attend_own_kernel,
        "attend_own",
        [SMEM, HBM] + [VMEM] * 6,
        [shape(RUN, heads, HD + PAD, rows, dtype=F32), shape(*out_weight.shape)],
        [pltpu.SemaphoreType.DMA((1,))],
    )(lengths, out_weight, *q_parts, kext, vext)
    return out_w, call(
        attend_merge_kernel,
        "attend_merge",
        [SMEM] + [VMEM] * 10,
        [shape(*q.shape) for q in q_parts],
        [
            pltpu.VMEM(kv[0].shape, BF),
            pltpu.VMEM((heads, rows, 2 * HD), BF),
            pltpu.VMEM((heads, HD + PAD, rows), BF),
        ],
    )(lengths, *q_parts, own, *guest_kv, guest)


def attend_all_kernel(sc, starts, q_ref, kv_ref, out, kext, vext, kv_buf, sems, *, slot):
    heads = kext.shape[0]
    keys = kv_ref.shape[0]
    chunk = kv_buf.shape[0]
    flags = query_flags(starts[0], slot, sc[0])

    def step(j, state):
        rows = pl.ds(pl.multiple_of(j * chunk, chunk), chunk)
        copy = pltpu.make_async_copy(kv_ref.at[rows, :], kv_buf, sems.at[0])
        copy.start()
        copy.wait()
        parts = [kv_buf.at[slice(n * slot, (n + 1) * slot), :] for n in range(chunk // slot)]
        begin = [starts[1 + j * (chunk // slot) + n] for n in range(chunk // slot)]
        extend_keys(parts, begin, sc[0], kext, vext)
        after = []
        for h in range(heads):
            top, acc = state[h]
            s = scores_of(kext, h, q_ref, flags)
            new = jnp.maximum(top, jnp.max(s, axis=0, keepdims=True))
            p = jnp.exp2((s - new) * SCALE).astype(BF)
            acc = acc * jnp.exp2((top - new) * SCALE)
            after.append((new, acc + jnp.dot(vext[h], p, preferred_element_type=F32)))
        return tuple(after)

    start = jnp.full((1, slot), 2 * NEG, F32), jnp.zeros((HD + PAD, slot), F32)
    state = lax.fori_loop(0, keys // chunk, step, (start,) * heads)
    for h in range(heads):
        o = state[h][1]
        out[h * HD : (h + 1) * HD, :] = (o[:HD, :] / o[HD : HD + 1, :]).astype(BF)


def attend_gathered(lengths, tile, q_parts, kv_parts):
    rows = kv_parts[0].shape[0]
    heads = q_parts[0].shape[0] // HD
    masks = list(range(RUN))
    kv = jnp.concatenate(kv_parts, 0)
    bit = RUN
    while bit < lax.axis_size("tile"):
        kv = jnp.concatenate([kv, move(kv, bit, 0)], 0)
        masks = masks + [m ^ bit for m in masks]
        bit *= 2
    key_starts = (tile ^ jnp.array(masks, dtype=jnp.int32)) * rows
    chunk = RUN * rows
    outs = []
    for i, q in enumerate(q_parts):
        starts = jnp.concatenate([((tile ^ i) * rows)[None], key_starts]).astype(jnp.int32)
        outs.append(
            call(
                functools.partial(attend_all_kernel, slot=rows),
                "attend_all",
                [SMEM, SMEM, VMEM, HBM],
                shape(*q.shape),
                [
                    pltpu.VMEM((heads, chunk, 2 * HD), BF),
                    pltpu.VMEM((heads, HD + PAD, chunk), BF),
                    pltpu.VMEM((chunk, kv.shape[1]), BF),
                    pltpu.SemaphoreType.DMA((1,)),
                ],
            )(lengths, starts, q, kv)
        )
    return outs


def gather_lhs_kernel(a0, a1, a2, a3, w, lhs, out, turned, *, block):
    for i, a in enumerate((a0, a1, a2, a3)):
        for at, start, size in pieces(lax.axis_index("tile") % RUN ^ i, a.shape[0] // HD):
            turned[pl.ds(start, size), :] = a[at : at + size, :]
    lhs[...] = turned[...].T
    out[...] = block_product(lhs, w, block).astype(out.dtype)


def block_product(lhs, w, block):
    width = w.shape[0]
    cols = pl.ds(pl.multiple_of((lax.axis_index("hid") ^ block) * width, width), width)
    return jnp.dot(lhs[...], w[:, cols], preferred_element_type=F32)


def project_kernel(lhs, w, *outs, blocks):
    for out, block in zip(outs, blocks):
        out[...] = block_product(lhs, w, block).astype(out.dtype)


def project(lhs, w, blocks, dtypes):
    return call(
        functools.partial(project_kernel, blocks=blocks),
        "project",
        [VMEM, VMEM],
        [shape(lhs.shape[0], w.shape[0], dtype=dtype) for dtype in dtypes],
    )(lhs, w)


def body(
    item_lengths,
    refresh_slots,
    layer_input,
    key_weight,
    value_weight,
    queries,
    key_cache,
    value_cache,
    out_weight,
):
    rows, width = queries.shape
    tile = lax.axis_index("tile")
    stay = functools.partial(pltpu.with_memory_space_constraint, memory_space=pltpu.HBM)
    x_y = move(layer_input, 0, 2)
    x_c = move(layer_input, 0, 1)
    part = width // RUN
    ready = call(
        prefetch_kernel,
        "prefetch",
        [SMEM, HBM, VMEM] + [HBM] * 5,
        [
            shape(2, rows, width, dtype=F32),
            shape(2, rows, width),
            shape(8, 128, dtype=F32),
        ]
        + [shape(width, width)] * 4
        + [shape(part, rows)] * RUN,
        [
            pltpu.VMEM((rows, width), BF),
            pltpu.VMEM((4, width, width), BF),
            pltpu.VMEM((rows, width), BF),
            pltpu.VMEM((width, rows), BF),
            pltpu.SemaphoreType.DMA((12,)),
        ],
    )(
        refresh_slots,
        stay(layer_input),
        x_c,
        stay(queries),
        stay(key_weight),
        stay(value_weight),
        stay(key_cache),
        stay(value_cache),
    )
    (sums, caches, token), later = ready[:3], ready[3:7]
    q_parts = [ready[7]] + [move(ready[7 + i], i, 0) for i in (1, 2, 3)]
    x_y, token = lax.optimization_barrier((x_y, token))
    x_cy = move(x_y, 0, 1)
    kv = call(
        refresh_kernel,
        "refresh",
        [SMEM] + [VMEM] * 9,
        [shape(rows, 2 * part)] * RUN,
        [pltpu.VMEM((2, rows, width), BF)],
    )(refresh_slots, x_y, x_cy, sums, caches, token, *later)
    kv, q_parts = lax.optimization_barrier((kv, q_parts))
    kv_parts = [kv[0]] + [move(kv[i], i, 0) for i in (1, 2, 3)]
    if lax.axis_size("tile") == 2 * RUN:
        out_w, back = attend_items(item_lengths, q_parts, kv, kv_parts, stay(out_weight))
    else:
        out_w, back = out_weight, attend_gathered(item_lengths, tile, q_parts, kv_parts)
    parts = [back[0]] + [move(back[i], i, 0) for i in (1, 2, 3)]

    lhs, send_y = call(
        functools.partial(gather_lhs_kernel, block=3),
        "project_first",
        [VMEM] * 5,
        [shape(rows, width), shape(rows, width)],
        [pltpu.VMEM((width, rows), BF)],
    )(*parts, out_w)
    got = move(send_y, 0, 1)
    keep_y, send, keep = project(lhs, out_w, (2, 1, 0), (F32, BF, F32))
    got_y = move((keep_y + got.astype(F32)).astype(BF), 0, 2)
    got = move(send, 0, 1)
    return (keep + got.astype(F32) + got_y.astype(F32)).astype(BF)


def solution(mesh):
    return jax.shard_map(
        body,
        mesh=mesh,
        in_specs=(
            P(),
            P("tile"),
            P("tile", "hid"),
            P(None, "hid"),
            P(None, "hid"),
            P("tile", "hid"),
            P("tile", "hid"),
            P("tile", "hid"),
            P("hid", None),
        ),
        out_specs=P("tile", "hid"),
        check_vma=False,
    )
```

```python
import functools

import jax
import jax.numpy as jnp
from jax import lax
from jax.experimental import pallas as pl
from jax.experimental.pallas import tpu as pltpu
from jax.sharding import PartitionSpec as P

HD = 64
BLOCK = 128
RUN = 4
NEG = -1e30
SCALE = 0.125 * 1.4426950408889634
AXES = ("tile", "hid")
BF = jnp.bfloat16
F32 = jnp.float32


def move(value, tile_mask, hid_mask):
    tiles, hids = lax.axis_size("tile"), lax.axis_size("hid")
    pairs = [
        (t * hids + h, (t ^ tile_mask) * hids + (h ^ hid_mask))
        for t in range(tiles)
        for h in range(hids)
    ]
    return lax.ppermute(value, AXES, pairs)


VMEM = pl.BlockSpec(memory_space=pltpu.VMEM)
SMEM = pl.BlockSpec(memory_space=pltpu.SMEM)
HBM = pl.BlockSpec(memory_space=pltpu.HBM)
PAD = 16


def call(kernel, name, in_specs, outs, scratch=(), limit=24):
    return pl.pallas_call(
        kernel,
        in_specs=in_specs,
        out_specs=jax.tree.map(lambda _: VMEM, outs),
        out_shape=outs,
        scratch_shapes=list(scratch),
        name=name,
        compiler_params=pltpu.CompilerParams(vmem_limit_bytes=limit * 2**20),
    )


def shape(*dims, dtype=BF):
    return jax.ShapeDtypeStruct(dims, dtype)


def pieces(group, heads):
    pair = heads // 2 * 2
    single = heads - pair
    out = [(0, pl.multiple_of(group * (pair * HD), pair * HD), pair * HD)] if pair else []
    if single:
        start = RUN * pair * HD + group * HD
        out.append((pair * HD, pl.multiple_of(start, HD), HD))
    return out


def any_fresh(slots, count):
    busy = slots[0] >= 0
    for n in range(1, count):
        busy = busy | (slots[n] >= 0)
    return busy


def weight_copy(w, part, target, sem):
    width = target.shape[0]
    start = pl.multiple_of((lax.axis_index("hid") ^ part) * width, width)
    return pltpu.make_async_copy(w.at[pl.ds(start, width), :], target, sem)


def begin_kernel(slots, x_in, x_c, q_in, wk, wv, acc, *refs):
    outs, (x_own, now, q_buf, turned, sems) = refs[:RUN], refs[RUN:]
    rows = x_own.shape[0]
    busy = any_fresh(slots, rows // BLOCK)
    query = pltpu.make_async_copy(q_in, q_buf, sems.at[0])
    own = pltpu.make_async_copy(x_in, x_own, sems.at[1])
    copies = [
        weight_copy((wk, wv)[n], part, now.at[2 * part + n], sems.at[2 + 2 * part + n])
        for part in range(2)
        for n in range(2)
    ]
    query.start()

    @pl.when(busy)
    def _():
        own.start()
        for copy in copies:
            copy.start()

    query.wait()
    turned[...] = q_buf[...].T
    low = lax.axis_index("tile") % RUN
    for i in range(RUN):
        for at, start, size in pieces(low ^ i, outs[i].shape[0] // HD):
            outs[i][at : at + size, :] = turned[pl.ds(start, size), :]

    @pl.when(busy)
    def _():
        own.wait()
        for part, x in enumerate((x_own, x_c)):
            for n in range(2):
                copies[2 * part + n].wait()
                dots = jnp.dot(x[...], now[2 * part + n], preferred_element_type=F32)
                acc[n] = dots if part == 0 else acc[n] + dots


def prefetch_kernel(slots, wk, wv, kc, vc, caches, token, *refs):
    later, sems = refs[:4], refs[4]
    token[...] = jnp.zeros(token.shape, F32)
    busy = any_fresh(slots, caches.shape[1] // BLOCK)
    copies = [
        weight_copy((wk, wv)[n % 2], 2 + n // 2, later[n], sems.at[n]) for n in range(4)
    ]
    rest = [
        pltpu.make_async_copy(kc, caches.at[0], sems.at[4]),
        pltpu.make_async_copy(vc, caches.at[1], sems.at[5]),
    ]
    for copy in rest:
        copy.start()

    @pl.when(busy)
    def _():
        for copy in copies:
            copy.start()
        for copy in copies:
            copy.wait()

    for copy in rest:
        copy.wait()


def refresh_kernel(sc, x_y, x_cy, acc, caches, token, *refs):
    later, outs, mixed = refs[:4], refs[4 : 4 + RUN], refs[4 + RUN]
    width = x_y.shape[1] // RUN
    blocks = x_y.shape[0] // BLOCK
    low = lax.axis_index("tile") % RUN
    fresh = []
    for b in range(blocks):
        hit = sc[0] == b
        for n in range(1, blocks):
            hit = hit | (sc[n] == b)
        fresh.append(hit)
    busy = fresh[0]
    for hit in fresh[1:]:
        busy = busy | hit

    mixed[...] = caches[...]

    @pl.when(busy)
    def _():
        for n in range(2):
            both = jnp.dot(x_y[...], later[n][...], preferred_element_type=F32)
            both = both + jnp.dot(x_cy[...], later[2 + n][...], preferred_element_type=F32)
            total = (acc[n] + both).astype(BF)
            for b in range(blocks):
                rows = slice(b * BLOCK, (b + 1) * BLOCK)
                mixed[n, rows, :] = jnp.where(fresh[b], total[rows, :], caches[n, rows, :])

    heads = width // HD
    pair = heads // 2 * 2 * HD
    upper = lax.broadcasted_iota(jnp.int32, (x_y.shape[0], 2 * HD), 1) >= HD
    for i in range(RUN):
        group = low ^ i
        cols = pl.ds(pl.multiple_of(group * pair, 2 * HD), pair)
        outs[i][:, :pair] = mixed[0, :, cols]
        outs[i][:, pair : 2 * pair] = mixed[1, :, cols]
        if heads % 2:
            cols = pl.ds(pl.multiple_of(RUN * pair + group // 2 * (2 * HD), 2 * HD), 2 * HD)
            keys, values = mixed[0, :, cols], mixed[1, :, cols]

            @pl.when(group % 2 == 0)
            def _():
                outs[i][:, 2 * pair :] = jnp.where(upper, pltpu.roll(values, HD, 1), keys)

            @pl.when(group % 2 == 1)
            def _():
                outs[i][:, 2 * pair :] = jnp.where(upper, values, pltpu.roll(keys, HD, 1))


def item_of(start, dims, axis, split):
    index = start + lax.broadcasted_iota(jnp.int32, dims, axis)
    return jnp.where(index < split, 0, 1)


def query_flags(start, count, split, mask_item=None):
    dims = (HD, count)
    item = item_of(start, dims, 1, split)
    zero, one = item == 0, item == 1
    if mask_item is not None:
        off = item != mask_item
        zero, one = zero | off, one | off
    row = lax.broadcasted_iota(jnp.int32, dims, 0)
    hit = ((row == 0) & zero) | ((row == 1) & one)
    return jnp.where(hit, 1.0, 0.0).astype(BF)


def key_flags(start, count, split):
    dims = (count, HD)
    item = item_of(start, dims, 0, split)
    lane = lax.broadcasted_iota(jnp.int32, dims, 1)
    hit = ((lane == 0) & (item == 1)) | ((lane == 1) & (item == 0))
    return jnp.where(hit, NEG, 0.0).astype(BF)


def head_cols(h, heads):
    pair = heads // 2 * 2
    if h < pair:
        return h * HD, (pair + h) * HD
    return 2 * pair * HD, (2 * pair + 1) * HD


def extend_keys(kv_refs, starts, split, kext, vext):
    heads = kext.shape[0]
    at = 0
    for kv, start in zip(kv_refs, starts):
        count = kv.shape[0]
        aux = key_flags(start, count, split)
        for h in range(heads):
            key_col, value_col = head_cols(h, heads)
            keys = kv[:, key_col : key_col + HD]
            kext[h, at : at + count, :] = jnp.concatenate([keys, aux], 1)
            vext[h, :HD, at : at + count] = kv[:, value_col : value_col + HD].T
            vext[h, HD:, at : at + count] = jnp.ones((PAD, count), BF)
        at += count


def scores_of(kext, h, q_ref, flags):
    q = jnp.concatenate([q_ref[h * HD : (h + 1) * HD, :], flags], 0)
    return jnp.dot(kext[h], q, preferred_element_type=F32)


DEPTH = 3


def score_stream(units, score):
    ahead = [score(u) for u in units[:DEPTH]]
    for n, unit in enumerate(units):
        if n + DEPTH < len(units):
            ahead.append(score(units[n + DEPTH]))
        yield unit, ahead.pop(0)


def softmax_part(s, values):
    top = jnp.max(s, axis=0, keepdims=True)
    p = jnp.exp2((s - top) * SCALE).astype(BF)
    return top, jnp.dot(values, p, preferred_element_type=F32)


def places(rows):
    tile = lax.axis_index("tile")
    cube = tile // RUN
    own = [(tile ^ i) * rows for i in range(RUN)]
    far = jnp.where(cube == 0, RUN, RUN - 1) * rows
    edge = (tile % RUN) ^ jnp.where(cube == 0, RUN - 1, 0)
    return cube, own, far, edge


def pick_edge_kernel(q0, q1, q2, q3, out):
    edge = places(1)[3]
    for i, q in enumerate((q0, q1, q2, q3)):

        @pl.when(edge == i)
        def _(q=q):
            out[...] = q[...]


def attend_guest_kernel(sc, q_ref, k0, k1, k2, k3, out, kext, vext):
    heads = kext.shape[0]
    count = q_ref.shape[1]
    cube, own, far, _ = places(count)
    extend_keys((k0, k1, k2, k3), own, sc[0], kext, vext)
    flags = query_flags(far, count, sc[0], cube)
    row = lax.broadcasted_iota(jnp.int32, (PAD, count), 0)
    logs = jnp.zeros((PAD, count), F32)
    for h, s in score_stream(list(range(heads)), lambda h: scores_of(kext, h, q_ref, flags)):
        top, o = softmax_part(s, vext[h])
        total = o[HD : HD + 1, :]
        out[h * HD : (h + 1) * HD, :] = (o[:HD, :] / total).astype(BF)
        log = top * SCALE + jnp.log2(total)
        high = log.astype(BF).astype(F32)
        mid = (log - high).astype(BF).astype(F32)
        for n, piece in enumerate((high, mid, log - high - mid)):
            logs = jnp.where(row == 3 * h + n, piece, logs)
    out[heads * HD :, :] = logs.astype(BF)


def slot_scores(sc, q_refs, starts, kext, mask_item=None):
    heads = kext.shape[0]
    count = q_refs[0].shape[1]
    flags = [query_flags(start, count, sc[0], mask_item) for start in starts]
    units = [(i, h) for i in range(len(q_refs)) for h in range(heads)]
    return score_stream(units, lambda u: scores_of(kext, u[1], q_refs[u[0]], flags[u[0]]))


def attend_own_kernel(sc, wo, q0, q1, q2, q3, kext, vext, out, out_w, sems):
    copy = pltpu.make_async_copy(wo, out_w, sems.at[0])
    copy.start()
    count = q0.shape[1]
    _, own, _, _ = places(count)
    for (i, h), s in slot_scores(sc, (q0, q1, q2, q3), own, kext):
        top, o = softmax_part(s, vext[h])
        out[i, h, : HD + 8, :] = o[: HD + 8, :]
        out[i, h, HD + 8 :, :] = jnp.broadcast_to(top, (8, count))
    copy.wait()


def attend_merge_kernel(sc, q0, q1, q2, q3, part, b0, b1, b2, b3, guest, *refs):
    outs, (kv, kext, vext) = refs[:RUN], refs[RUN:]
    heads = kext.shape[0]
    count = q0.shape[1]
    cube, own, far, edge = places(count)
    kv[...] = (b0[...] + b1[...]) + (b2[...] + b3[...])
    extend_keys((kv,), (far,), sc[0], kext, vext)
    logs = guest[heads * HD :, :].astype(F32)
    for (i, h), s in slot_scores(sc, (q0, q1, q2, q3), own, kext, cube):
        at = slice(h * HD, (h + 1) * HD)
        log = logs[3 * h : 3 * h + 1, :] + logs[3 * h + 1 : 3 * h + 2, :]
        log = log + logs[3 * h + 2 : 3 * h + 3, :]
        log = jnp.where(edge == i, log, NEG)
        own_log = part[i, h, HD + 8 : HD + 9, :] * SCALE
        top = jnp.maximum(own_log, jnp.max(s, axis=0, keepdims=True) * SCALE)
        top = jnp.maximum(top, log)
        p = jnp.exp2(s * SCALE - top).astype(BF)
        near = jnp.exp2(own_log - top)
        share = jnp.exp2(log - top)
        o = jnp.dot(vext[h], p, preferred_element_type=F32)
        total = o[HD : HD + 1, :] + part[i, h, HD : HD + 1, :] * near + share
        o = o[:HD, :] + part[i, h, :HD, :] * near + guest[at, :].astype(F32) * share
        outs[i][at, :] = (o / total).astype(BF)


def send_tiles(value, tile_pairs):
    hids = lax.axis_size("hid")
    pairs = [(s * hids + h, d * hids + h) for s, d in tile_pairs for h in range(hids)]
    return lax.ppermute(value, AXES, pairs)


def guest_queries(q_parts):
    picked = call(pick_edge_kernel, "pick_edge", [VMEM] * RUN, shape(*q_parts[0].shape))(*q_parts)
    return move(picked, RUN, 0)


def attend_items(lengths, guest_q, q_parts, kv, kv_parts, out_weight):
    rows = kv[0].shape[0]
    heads = q_parts[0].shape[0] // HD
    ext = [shape(heads, RUN * rows, 2 * HD), shape(heads, HD + PAD, RUN * rows)]

    first, last = RUN - 1, RUN
    guest_kv = [
        send_tiles(kv[i], [(first, last + (first ^ i)), (last, i)]) for i in (0, 2, 3)
    ] + [send_tiles(kv_parts[1], [(first ^ 1, last + (first ^ 1)), (last ^ 1, 1)])]
    guest, kext, vext = call(
        attend_guest_kernel,
        "attend_guest",
        [SMEM] + [VMEM] * 5,
        [shape(heads * HD + PAD, rows)] + ext,
    )(lengths, guest_q, *kv_parts)
    guest = move(guest, RUN, 0)
    own, out_w = call(
        attend_own_kernel,
        "attend_own",
        [SMEM, HBM] + [VMEM] * 6,
        [shape(RUN, heads, HD + PAD, rows, dtype=F32), shape(*out_weight.shape)],
        [pltpu.SemaphoreType.DMA((1,))],
    )(lengths, out_weight, *q_parts, kext, vext)
    return out_w, call(
        attend_merge_kernel,
        "attend_merge",
        [SMEM] + [VMEM] * 10,
        [shape(*q.shape) for q in q_parts],
        [
            pltpu.VMEM(kv[0].shape, BF),
            pltpu.VMEM((heads, rows, 2 * HD), BF),
            pltpu.VMEM((heads, HD + PAD, rows), BF),
        ],
    )(lengths, *q_parts, own, *guest_kv, guest)


def attend_all_kernel(sc, starts, q_ref, kv_ref, out, kext, vext, kv_buf, sems, *, slot):
    heads = kext.shape[0]
    keys = kv_ref.shape[0]
    chunk = kv_buf.shape[0]
    flags = query_flags(starts[0], slot, sc[0])

    def step(j, state):
        rows = pl.ds(pl.multiple_of(j * chunk, chunk), chunk)
        copy = pltpu.make_async_copy(kv_ref.at[rows, :], kv_buf, sems.at[0])
        copy.start()
        copy.wait()
        parts = [kv_buf.at[slice(n * slot, (n + 1) * slot), :] for n in range(chunk // slot)]
        begin = [starts[1 + j * (chunk // slot) + n] for n in range(chunk // slot)]
        extend_keys(parts, begin, sc[0], kext, vext)
        after = []
        for h in range(heads):
            top, acc = state[h]
            s = scores_of(kext, h, q_ref, flags)
            new = jnp.maximum(top, jnp.max(s, axis=0, keepdims=True))
            p = jnp.exp2((s - new) * SCALE).astype(BF)
            acc = acc * jnp.exp2((top - new) * SCALE)
            after.append((new, acc + jnp.dot(vext[h], p, preferred_element_type=F32)))
        return tuple(after)

    start = jnp.full((1, slot), 2 * NEG, F32), jnp.zeros((HD + PAD, slot), F32)
    state = lax.fori_loop(0, keys // chunk, step, (start,) * heads)
    for h in range(heads):
        o = state[h][1]
        out[h * HD : (h + 1) * HD, :] = (o[:HD, :] / o[HD : HD + 1, :]).astype(BF)


def attend_gathered(lengths, tile, q_parts, kv_parts):
    rows = kv_parts[0].shape[0]
    heads = q_parts[0].shape[0] // HD
    masks = list(range(RUN))
    kv = jnp.concatenate(kv_parts, 0)
    bit = RUN
    while bit < lax.axis_size("tile"):
        kv = jnp.concatenate([kv, move(kv, bit, 0)], 0)
        masks = masks + [m ^ bit for m in masks]
        bit *= 2
    key_starts = (tile ^ jnp.array(masks, dtype=jnp.int32)) * rows
    chunk = RUN * rows
    outs = []
    for i, q in enumerate(q_parts):
        starts = jnp.concatenate([((tile ^ i) * rows)[None], key_starts]).astype(jnp.int32)
        outs.append(
            call(
                functools.partial(attend_all_kernel, slot=rows),
                "attend_all",
                [SMEM, SMEM, VMEM, HBM],
                shape(*q.shape),
                [
                    pltpu.VMEM((heads, chunk, 2 * HD), BF),
                    pltpu.VMEM((heads, HD + PAD, chunk), BF),
                    pltpu.VMEM((chunk, kv.shape[1]), BF),
                    pltpu.SemaphoreType.DMA((1,)),
                ],
            )(lengths, starts, q, kv)
        )
    return outs


def gather_lhs_kernel(a0, a1, a2, a3, w, lhs, out, turned, *, block):
    for i, a in enumerate((a0, a1, a2, a3)):
        for at, start, size in pieces(lax.axis_index("tile") % RUN ^ i, a.shape[0] // HD):
            turned[pl.ds(start, size), :] = a[at : at + size, :]
    lhs[...] = turned[...].T
    out[...] = block_product(lhs, w, block).astype(out.dtype)


def block_product(lhs, w, block):
    width = w.shape[0]
    cols = pl.ds(pl.multiple_of((lax.axis_index("hid") ^ block) * width, width), width)
    return jnp.dot(lhs[...], w[:, cols], preferred_element_type=F32)


def project_kernel(lhs, w, *outs, blocks):
    for out, block in zip(outs, blocks):
        out[...] = block_product(lhs, w, block).astype(out.dtype)


def project(lhs, w, blocks, dtypes):
    return call(
        functools.partial(project_kernel, blocks=blocks),
        "project",
        [VMEM, VMEM],
        [shape(lhs.shape[0], w.shape[0], dtype=dtype) for dtype in dtypes],
    )(lhs, w)


def body(
    item_lengths,
    refresh_slots,
    layer_input,
    key_weight,
    value_weight,
    queries,
    key_cache,
    value_cache,
    out_weight,
):
    rows, width = queries.shape
    tile = lax.axis_index("tile")
    stay = functools.partial(pltpu.with_memory_space_constraint, memory_space=pltpu.HBM)
    x_y = move(layer_input, 0, 2)
    x_c = move(layer_input, 0, 1)
    part = width // RUN
    sums, *q_packed = call(
        begin_kernel,
        "begin",
        [SMEM, HBM, VMEM] + [HBM] * 3,
        [shape(2, rows, width, dtype=F32)] + [shape(part, rows)] * RUN,
        [
            pltpu.VMEM((rows, width), BF),
            pltpu.VMEM((4, width, width), BF),
            pltpu.VMEM((rows, width), BF),
            pltpu.VMEM((width, rows), BF),
            pltpu.SemaphoreType.DMA((6,)),
        ],
    )(
        refresh_slots,
        stay(layer_input),
        x_c,
        stay(queries),
        stay(key_weight),
        stay(value_weight),
    )
    q_parts = q_packed[:1] + [move(q_packed[i], i, 0) for i in (1, 2, 3)]
    caches, token, *later = call(
        prefetch_kernel,
        "prefetch",
        [SMEM] + [HBM] * 4,
        [shape(2, rows, width), shape(8, 128, dtype=F32)] + [shape(width, width)] * 4,
        [pltpu.SemaphoreType.DMA((6,))],
    )(
        refresh_slots,
        stay(key_weight),
        stay(value_weight),
        stay(key_cache),
        stay(value_cache),
    )
    x_y, token, q_parts = lax.optimization_barrier((x_y, token, q_parts))
    x_cy = move(x_y, 0, 1)
    kv = call(
        refresh_kernel,
        "refresh",
        [SMEM] + [VMEM] * 9,
        [shape(rows, 2 * part)] * RUN,
        [pltpu.VMEM((2, rows, width), BF)],
    )(refresh_slots, x_y, x_cy, sums, caches, token, *later)
    items = lax.axis_size("tile") == 2 * RUN
    if items:
        kv, guest_q = lax.optimization_barrier((kv, guest_queries(q_parts)))
    kv_parts = [kv[0]] + [move(kv[i], i, 0) for i in (1, 2, 3)]
    if items:
        out_w, back = attend_items(item_lengths, guest_q, q_parts, kv, kv_parts, stay(out_weight))
    else:
        out_w, back = out_weight, attend_gathered(item_lengths, tile, q_parts, kv_parts)
    parts = [back[0]] + [move(back[i], i, 0) for i in (1, 2, 3)]

    lhs, send_y = call(
        functools.partial(gather_lhs_kernel, block=3),
        "project_first",
        [VMEM] * 5,
        [shape(rows, width), shape(rows, width)],
        [pltpu.VMEM((width, rows), BF)],
    )(*parts, out_w)
    got = move(send_y, 0, 1)
    keep_y, send, keep = project(lhs, out_w, (2, 1, 0), (F32, BF, F32))
    got_y = move((keep_y + got.astype(F32)).astype(BF), 0, 2)
    got = move(send, 0, 1)
    return (keep + got.astype(F32) + got_y.astype(F32)).astype(BF)


def solution(mesh):
    return jax.shard_map(
        body,
        mesh=mesh,
        in_specs=(
            P(),
            P("tile"),
            P("tile", "hid"),
            P(None, "hid"),
            P(None, "hid"),
            P("tile", "hid"),
            P("tile", "hid"),
            P("tile", "hid"),
            P("hid", None),
        ),
        out_specs=P("tile", "hid"),
        check_vma=False,
    )
```

```python
import functools

import jax
import jax.numpy as jnp
from jax import lax
from jax.experimental import pallas as pl
from jax.experimental.pallas import tpu as pltpu
from jax.sharding import PartitionSpec as P

HD = 64
BLOCK = 128
RUN = 4
NEG = -1e30
SCALE = 0.125 * 1.4426950408889634
AXES = ("tile", "hid")
BF = jnp.bfloat16
F32 = jnp.float32


def move(value, tile_mask, hid_mask):
    tiles, hids = lax.axis_size("tile"), lax.axis_size("hid")
    pairs = [
        (t * hids + h, (t ^ tile_mask) * hids + (h ^ hid_mask))
        for t in range(tiles)
        for h in range(hids)
    ]
    return lax.ppermute(value, AXES, pairs)


VMEM = pl.BlockSpec(memory_space=pltpu.VMEM)
SMEM = pl.BlockSpec(memory_space=pltpu.SMEM)
HBM = pl.BlockSpec(memory_space=pltpu.HBM)
PAD = 16


def call(kernel, name, in_specs, outs, scratch=(), limit=24):
    return pl.pallas_call(
        kernel,
        in_specs=in_specs,
        out_specs=jax.tree.map(lambda _: VMEM, outs),
        out_shape=outs,
        scratch_shapes=list(scratch),
        name=name,
        compiler_params=pltpu.CompilerParams(vmem_limit_bytes=limit * 2**20),
    )


def shape(*dims, dtype=BF):
    return jax.ShapeDtypeStruct(dims, dtype)


def pieces(group, heads):
    pair = heads // 2 * 2
    single = heads - pair
    out = [(0, pl.multiple_of(group * (pair * HD), pair * HD), pair * HD)] if pair else []
    if single:
        start = RUN * pair * HD + group * HD
        out.append((pair * HD, pl.multiple_of(start, HD), HD))
    return out


def any_fresh(slots, count):
    busy = slots[0] >= 0
    for n in range(1, count):
        busy = busy | (slots[n] >= 0)
    return busy


def weight_copy(w, part, target, sem):
    width = target.shape[0]
    start = pl.multiple_of((lax.axis_index("hid") ^ part) * width, width)
    return pltpu.make_async_copy(w.at[pl.ds(start, width), :], target, sem)


def pack_queries_kernel(q_in, *refs):
    outs, (q_buf, turned, sems) = refs[:RUN], refs[RUN:]
    copy = pltpu.make_async_copy(q_in, q_buf, sems.at[0])
    copy.start()
    copy.wait()
    turned[...] = q_buf[...].T
    low = lax.axis_index("tile") % RUN
    for i in range(RUN):
        for at, start, size in pieces(low ^ i, outs[i].shape[0] // HD):
            outs[i][at : at + size, :] = turned[pl.ds(start, size), :]


def prefetch_kernel(slots, x_in, x_c, wk, wv, kc, vc, acc, caches, token, *refs):
    later, (x_own, now, sems) = refs[:4], refs[4:]
    token[...] = jnp.zeros(token.shape, F32)
    busy = any_fresh(slots, caches.shape[1] // BLOCK)
    own = pltpu.make_async_copy(x_in, x_own, sems.at[0])
    rest = [
        pltpu.make_async_copy(kc, caches.at[0], sems.at[1]),
        pltpu.make_async_copy(vc, caches.at[1], sems.at[2]),
    ]
    copies = [
        weight_copy((wk, wv)[n % 2], n // 2, now.at[n] if n < 4 else later[n - 4], sems.at[3 + n])
        for n in range(8)
    ]

    @pl.when(busy)
    def _():
        own.start()
        for copy in copies:
            copy.start()

    for copy in rest:
        copy.start()

    @pl.when(busy)
    def _():
        own.wait()
        for n in range(4):
            x = (x_own, x_c)[n // 2]
            copies[n].wait()
            dots = jnp.dot(x[...], now[n], preferred_element_type=F32)
            acc[n % 2] = dots if n < 2 else acc[n % 2] + dots
        for copy in copies[4:]:
            copy.wait()

    for copy in rest:
        copy.wait()


def refresh_kernel(sc, x_y, x_cy, acc, caches, token, *refs):
    later, outs, mixed = refs[:4], refs[4 : 4 + RUN], refs[4 + RUN]
    width = x_y.shape[1] // RUN
    blocks = x_y.shape[0] // BLOCK
    low = lax.axis_index("tile") % RUN
    fresh = []
    for b in range(blocks):
        hit = sc[0] == b
        for n in range(1, blocks):
            hit = hit | (sc[n] == b)
        fresh.append(hit)
    busy = fresh[0]
    for hit in fresh[1:]:
        busy = busy | hit

    mixed[...] = caches[...]

    @pl.when(busy)
    def _():
        for n in range(2):
            both = jnp.dot(x_y[...], later[n][...], preferred_element_type=F32)
            both = both + jnp.dot(x_cy[...], later[2 + n][...], preferred_element_type=F32)
            total = (acc[n] + both).astype(BF)
            for b in range(blocks):
                rows = slice(b * BLOCK, (b + 1) * BLOCK)
                mixed[n, rows, :] = jnp.where(fresh[b], total[rows, :], caches[n, rows, :])

    heads = width // HD
    pair = heads // 2 * 2 * HD
    upper = lax.broadcasted_iota(jnp.int32, (x_y.shape[0], 2 * HD), 1) >= HD
    for i in range(RUN):
        group = low ^ i
        cols = pl.ds(pl.multiple_of(group * pair, 2 * HD), pair)
        outs[i][:, :pair] = mixed[0, :, cols]
        outs[i][:, pair : 2 * pair] = mixed[1, :, cols]
        if heads % 2:
            cols = pl.ds(pl.multiple_of(RUN * pair + group // 2 * (2 * HD), 2 * HD), 2 * HD)
            keys, values = mixed[0, :, cols], mixed[1, :, cols]

            @pl.when(group % 2 == 0)
            def _():
                outs[i][:, 2 * pair :] = jnp.where(upper, pltpu.roll(values, HD, 1), keys)

            @pl.when(group % 2 == 1)
            def _():
                outs[i][:, 2 * pair :] = jnp.where(upper, values, pltpu.roll(keys, HD, 1))


def item_of(start, dims, axis, split):
    index = start + lax.broadcasted_iota(jnp.int32, dims, axis)
    return jnp.where(index < split, 0, 1)


def query_flags(start, count, split, mask_item=None):
    dims = (HD, count)
    item = item_of(start, dims, 1, split)
    zero, one = item == 0, item == 1
    if mask_item is not None:
        off = item != mask_item
        zero, one = zero | off, one | off
    row = lax.broadcasted_iota(jnp.int32, dims, 0)
    hit = ((row == 0) & zero) | ((row == 1) & one)
    return jnp.where(hit, 1.0, 0.0).astype(BF)


def key_flags(start, count, split):
    dims = (count, HD)
    item = item_of(start, dims, 0, split)
    lane = lax.broadcasted_iota(jnp.int32, dims, 1)
    hit = ((lane == 0) & (item == 1)) | ((lane == 1) & (item == 0))
    return jnp.where(hit, NEG, 0.0).astype(BF)


def head_cols(h, heads):
    pair = heads // 2 * 2
    if h < pair:
        return h * HD, (pair + h) * HD
    return 2 * pair * HD, (2 * pair + 1) * HD


def extend_keys(kv_refs, starts, split, kext, vext):
    heads = kext.shape[0]
    at = 0
    for kv, start in zip(kv_refs, starts):
        count = kv.shape[0]
        aux = key_flags(start, count, split)
        for h in range(heads):
            key_col, value_col = head_cols(h, heads)
            keys = kv[:, key_col : key_col + HD]
            kext[h, at : at + count, :] = jnp.concatenate([keys, aux], 1)
            vext[h, :HD, at : at + count] = kv[:, value_col : value_col + HD].T
            vext[h, HD:, at : at + count] = jnp.ones((PAD, count), BF)
        at += count


def scores_of(kext, h, q_ref, flags):
    q = jnp.concatenate([q_ref[h * HD : (h + 1) * HD, :], flags], 0)
    return jnp.dot(kext[h], q, preferred_element_type=F32)


DEPTH = 3


def score_stream(units, score):
    ahead = [score(u) for u in units[:DEPTH]]
    for n, unit in enumerate(units):
        if n + DEPTH < len(units):
            ahead.append(score(units[n + DEPTH]))
        yield unit, ahead.pop(0)


def softmax_part(s, values):
    top = jnp.max(s, axis=0, keepdims=True)
    p = jnp.exp2((s - top) * SCALE).astype(BF)
    return top, jnp.dot(values, p, preferred_element_type=F32)


def places(rows):
    tile = lax.axis_index("tile")
    cube = tile // RUN
    own = [(tile ^ i) * rows for i in range(RUN)]
    far = jnp.where(cube == 0, RUN, RUN - 1) * rows
    edge = (tile % RUN) ^ jnp.where(cube == 0, RUN - 1, 0)
    return cube, own, far, edge


def pick_edge_kernel(q0, q1, q2, q3, out):
    edge = places(1)[3]
    for i, q in enumerate((q0, q1, q2, q3)):

        @pl.when(edge == i)
        def _(q=q):
            out[...] = q[...]


def attend_guest_kernel(sc, q_ref, k0, k1, k2, k3, out, kext, vext):
    heads = kext.shape[0]
    count = q_ref.shape[1]
    cube, own, far, _ = places(count)
    extend_keys((k0, k1, k2, k3), own, sc[0], kext, vext)
    flags = query_flags(far, count, sc[0], cube)
    row = lax.broadcasted_iota(jnp.int32, (PAD, count), 0)
    logs = jnp.zeros((PAD, count), F32)
    for h, s in score_stream(list(range(heads)), lambda h: scores_of(kext, h, q_ref, flags)):
        top, o = softmax_part(s, vext[h])
        total = o[HD : HD + 1, :]
        out[h * HD : (h + 1) * HD, :] = (o[:HD, :] / total).astype(BF)
        log = top * SCALE + jnp.log2(total)
        high = log.astype(BF).astype(F32)
        mid = (log - high).astype(BF).astype(F32)
        for n, piece in enumerate((high, mid, log - high - mid)):
            logs = jnp.where(row == 3 * h + n, piece, logs)
    out[heads * HD :, :] = logs.astype(BF)


def slot_scores(sc, q_refs, starts, kext, mask_item=None):
    heads = kext.shape[0]
    count = q_refs[0].shape[1]
    flags = [query_flags(start, count, sc[0], mask_item) for start in starts]
    units = [(i, h) for i in range(len(q_refs)) for h in range(heads)]
    return score_stream(units, lambda u: scores_of(kext, u[1], q_refs[u[0]], flags[u[0]]))


def attend_own_kernel(sc, wo, q0, q1, q2, q3, kext, vext, out, out_w, sems):
    copy = pltpu.make_async_copy(wo, out_w, sems.at[0])
    copy.start()
    count = q0.shape[1]
    _, own, _, _ = places(count)
    for (i, h), s in slot_scores(sc, (q0, q1, q2, q3), own, kext):
        top, o = softmax_part(s, vext[h])
        out[i, h, : HD + 8, :] = o[: HD + 8, :]
        out[i, h, HD + 8 :, :] = jnp.broadcast_to(top, (8, count))
    copy.wait()


def attend_merge_kernel(sc, q0, q1, q2, q3, part, b0, b1, b2, b3, guest, *refs):
    outs, (kv, kext, vext) = refs[:RUN], refs[RUN:]
    heads = kext.shape[0]
    count = q0.shape[1]
    cube, own, far, edge = places(count)
    kv[...] = (b0[...] + b1[...]) + (b2[...] + b3[...])
    extend_keys((kv,), (far,), sc[0], kext, vext)
    logs = guest[heads * HD :, :].astype(F32)
    for (i, h), s in slot_scores(sc, (q0, q1, q2, q3), own, kext, cube):
        at = slice(h * HD, (h + 1) * HD)
        log = logs[3 * h : 3 * h + 1, :] + logs[3 * h + 1 : 3 * h + 2, :]
        log = log + logs[3 * h + 2 : 3 * h + 3, :]
        log = jnp.where(edge == i, log, NEG)
        own_log = part[i, h, HD + 8 : HD + 9, :] * SCALE
        top = jnp.maximum(own_log, jnp.max(s, axis=0, keepdims=True) * SCALE)
        top = jnp.maximum(top, log)
        p = jnp.exp2(s * SCALE - top).astype(BF)
        near = jnp.exp2(own_log - top)
        share = jnp.exp2(log - top)
        o = jnp.dot(vext[h], p, preferred_element_type=F32)
        total = o[HD : HD + 1, :] + part[i, h, HD : HD + 1, :] * near + share
        o = o[:HD, :] + part[i, h, :HD, :] * near + guest[at, :].astype(F32) * share
        outs[i][at, :] = (o / total).astype(BF)


def send_tiles(value, tile_pairs):
    hids = lax.axis_size("hid")
    pairs = [(s * hids + h, d * hids + h) for s, d in tile_pairs for h in range(hids)]
    return lax.ppermute(value, AXES, pairs)


def guest_queries(q_parts):
    picked = call(pick_edge_kernel, "pick_edge", [VMEM] * RUN, shape(*q_parts[0].shape))(*q_parts)
    return move(picked, RUN, 0)


def attend_items(lengths, guest_q, q_parts, kv, kv_parts, out_weight):
    rows = kv[0].shape[0]
    heads = q_parts[0].shape[0] // HD
    ext = [shape(heads, RUN * rows, 2 * HD), shape(heads, HD + PAD, RUN * rows)]

    first, last = RUN - 1, RUN
    guest_kv = [
        send_tiles(kv[i], [(first, last + (first ^ i)), (last, i)]) for i in (0, 2, 3)
    ] + [send_tiles(kv_parts[1], [(first ^ 1, last + (first ^ 1)), (last ^ 1, 1)])]
    guest, kext, vext = call(
        attend_guest_kernel,
        "attend_guest",
        [SMEM] + [VMEM] * 5,
        [shape(heads * HD + PAD, rows)] + ext,
    )(lengths, guest_q, *kv_parts)
    guest = move(guest, RUN, 0)
    own, out_w = call(
        attend_own_kernel,
        "attend_own",
        [SMEM, HBM] + [VMEM] * 6,
        [shape(RUN, heads, HD + PAD, rows, dtype=F32), shape(*out_weight.shape)],
        [pltpu.SemaphoreType.DMA((1,))],
    )(lengths, out_weight, *q_parts, kext, vext)
    return out_w, call(
        attend_merge_kernel,
        "attend_merge",
        [SMEM] + [VMEM] * 10,
        [shape(*q.shape) for q in q_parts],
        [
            pltpu.VMEM(kv[0].shape, BF),
            pltpu.VMEM((heads, rows, 2 * HD), BF),
            pltpu.VMEM((heads, HD + PAD, rows), BF),
        ],
    )(lengths, *q_parts, own, *guest_kv, guest)


def attend_all_kernel(sc, starts, q_ref, kv_ref, out, kext, vext, kv_buf, sems, *, slot):
    heads = kext.shape[0]
    keys = kv_ref.shape[0]
    chunk = kv_buf.shape[0]
    flags = query_flags(starts[0], slot, sc[0])

    def step(j, state):
        rows = pl.ds(pl.multiple_of(j * chunk, chunk), chunk)
        copy = pltpu.make_async_copy(kv_ref.at[rows, :], kv_buf, sems.at[0])
        copy.start()
        copy.wait()
        parts = [kv_buf.at[slice(n * slot, (n + 1) * slot), :] for n in range(chunk // slot)]
        begin = [starts[1 + j * (chunk // slot) + n] for n in range(chunk // slot)]
        extend_keys(parts, begin, sc[0], kext, vext)
        after = []
        for h in range(heads):
            top, acc = state[h]
            s = scores_of(kext, h, q_ref, flags)
            new = jnp.maximum(top, jnp.max(s, axis=0, keepdims=True))
            p = jnp.exp2((s - new) * SCALE).astype(BF)
            acc = acc * jnp.exp2((top - new) * SCALE)
            after.append((new, acc + jnp.dot(vext[h], p, preferred_element_type=F32)))
        return tuple(after)

    start = jnp.full((1, slot), 2 * NEG, F32), jnp.zeros((HD + PAD, slot), F32)
    state = lax.fori_loop(0, keys // chunk, step, (start,) * heads)
    for h in range(heads):
        o = state[h][1]
        out[h * HD : (h + 1) * HD, :] = (o[:HD, :] / o[HD : HD + 1, :]).astype(BF)


def attend_gathered(lengths, tile, q_parts, kv_parts):
    rows = kv_parts[0].shape[0]
    heads = q_parts[0].shape[0] // HD
    masks = list(range(RUN))
    kv = jnp.concatenate(kv_parts, 0)
    bit = RUN
    while bit < lax.axis_size("tile"):
        kv = jnp.concatenate([kv, move(kv, bit, 0)], 0)
        masks = masks + [m ^ bit for m in masks]
        bit *= 2
    key_starts = (tile ^ jnp.array(masks, dtype=jnp.int32)) * rows
    chunk = RUN * rows
    outs = []
    for i, q in enumerate(q_parts):
        starts = jnp.concatenate([((tile ^ i) * rows)[None], key_starts]).astype(jnp.int32)
        outs.append(
            call(
                functools.partial(attend_all_kernel, slot=rows),
                "attend_all",
                [SMEM, SMEM, VMEM, HBM],
                shape(*q.shape),
                [
                    pltpu.VMEM((heads, chunk, 2 * HD), BF),
                    pltpu.VMEM((heads, HD + PAD, chunk), BF),
                    pltpu.VMEM((chunk, kv.shape[1]), BF),
                    pltpu.SemaphoreType.DMA((1,)),
                ],
            )(lengths, starts, q, kv)
        )
    return outs


def gather_lhs_kernel(a0, a1, a2, a3, w, lhs, out, turned, *, block):
    for i, a in enumerate((a0, a1, a2, a3)):
        for at, start, size in pieces(lax.axis_index("tile") % RUN ^ i, a.shape[0] // HD):
            turned[pl.ds(start, size), :] = a[at : at + size, :]
    lhs[...] = turned[...].T
    out[...] = block_product(lhs, w, block).astype(out.dtype)


def block_product(lhs, w, block):
    width = w.shape[0]
    cols = pl.ds(pl.multiple_of((lax.axis_index("hid") ^ block) * width, width), width)
    return jnp.dot(lhs[...], w[:, cols], preferred_element_type=F32)


def project_kernel(lhs, w, *outs, blocks):
    for out, block in zip(outs, blocks):
        out[...] = block_product(lhs, w, block).astype(out.dtype)


def project(lhs, w, blocks, dtypes):
    return call(
        functools.partial(project_kernel, blocks=blocks),
        "project",
        [VMEM, VMEM],
        [shape(lhs.shape[0], w.shape[0], dtype=dtype) for dtype in dtypes],
    )(lhs, w)


def body(
    item_lengths,
    refresh_slots,
    layer_input,
    key_weight,
    value_weight,
    queries,
    key_cache,
    value_cache,
    out_weight,
):
    rows, width = queries.shape
    tile = lax.axis_index("tile")
    stay = functools.partial(pltpu.with_memory_space_constraint, memory_space=pltpu.HBM)
    x_y = move(layer_input, 0, 2)
    x_c = move(layer_input, 0, 1)
    part = width // RUN
    q_packed = call(
        pack_queries_kernel,
        "pack_queries",
        [HBM],
        [shape(part, rows)] * RUN,
        [
            pltpu.VMEM((rows, width), BF),
            pltpu.VMEM((width, rows), BF),
            pltpu.SemaphoreType.DMA((1,)),
        ],
    )(stay(queries))
    q_parts = [q_packed[0]] + [move(q_packed[i], i, 0) for i in (1, 2, 3)]
    sums, caches, token, *later = call(
        prefetch_kernel,
        "prefetch",
        [SMEM, HBM, VMEM] + [HBM] * 4,
        [
            shape(2, rows, width, dtype=F32),
            shape(2, rows, width),
            shape(8, 128, dtype=F32),
        ]
        + [shape(width, width)] * 4,
        [
            pltpu.VMEM((rows, width), BF),
            pltpu.VMEM((4, width, width), BF),
            pltpu.SemaphoreType.DMA((11,)),
        ],
    )(
        refresh_slots,
        stay(layer_input),
        x_c,
        stay(key_weight),
        stay(value_weight),
        stay(key_cache),
        stay(value_cache),
    )
    x_y, token, q_parts = lax.optimization_barrier((x_y, token, q_parts))
    x_cy = move(x_y, 0, 1)
    kv = call(
        refresh_kernel,
        "refresh",
        [SMEM] + [VMEM] * 9,
        [shape(rows, 2 * part)] * RUN,
        [pltpu.VMEM((2, rows, width), BF)],
    )(refresh_slots, x_y, x_cy, sums, caches, token, *later)
    items = lax.axis_size("tile") == 2 * RUN
    if items:
        guest_q = guest_queries(q_parts)
        far_part, guest_q = lax.optimization_barrier((kv[3], guest_q))
        kv = [kv[0], kv[1], kv[2], far_part]
    moved = {i: move(kv[i], i, 0) for i in (1, 2, 3)}
    kv_parts = [kv[0], moved[1], moved[2], moved[3]]
    if items:
        out_w, back = attend_items(item_lengths, guest_q, q_parts, kv, kv_parts, stay(out_weight))
    else:
        out_w, back = out_weight, attend_gathered(item_lengths, tile, q_parts, kv_parts)
    parts = [back[0]] + [move(back[i], i, 0) for i in (1, 2, 3)]

    lhs, send_y = call(
        functools.partial(gather_lhs_kernel, block=3),
        "project_first",
        [VMEM] * 5,
        [shape(rows, width), shape(rows, width)],
        [pltpu.VMEM((width, rows), BF)],
    )(*parts, out_w)
    got = move(send_y, 0, 1)
    keep_y, send, keep = project(lhs, out_w, (2, 1, 0), (F32, BF, F32))
    via_y, send = lax.optimization_barrier(((keep_y + got.astype(F32)).astype(BF), send))
    got_y = move(via_y, 0, 2)
    got = move(send, 0, 1)
    return (keep + got.astype(F32) + got_y.astype(F32)).astype(BF)


def solution(mesh):
    return jax.shard_map(
        body,
        mesh=mesh,
        in_specs=(
            P(),
            P("tile"),
            P("tile", "hid"),
            P(None, "hid"),
            P(None, "hid"),
            P("tile", "hid"),
            P("tile", "hid"),
            P("tile", "hid"),
            P("hid", None),
        ),
        out_specs=P("tile", "hid"),
        check_vma=False,
    )
```

```python
import functools

import jax
import jax.numpy as jnp
from jax import lax
from jax.experimental import pallas as pl
from jax.experimental.pallas import tpu as pltpu
from jax.sharding import PartitionSpec as P

HD = 64
BLOCK = 128
RUN = 4
NEG = -1e30
SCALE = 0.125 * 1.4426950408889634
AXES = ("tile", "hid")
BF = jnp.bfloat16
F32 = jnp.float32


def move(value, tile_mask, hid_mask):
    tiles, hids = lax.axis_size("tile"), lax.axis_size("hid")
    pairs = [
        (t * hids + h, (t ^ tile_mask) * hids + (h ^ hid_mask))
        for t in range(tiles)
        for h in range(hids)
    ]
    return lax.ppermute(value, AXES, pairs)


VMEM = pl.BlockSpec(memory_space=pltpu.VMEM)
SMEM = pl.BlockSpec(memory_space=pltpu.SMEM)
HBM = pl.BlockSpec(memory_space=pltpu.HBM)
PAD = 16


def call(kernel, name, in_specs, outs, scratch=(), limit=24):
    return pl.pallas_call(
        kernel,
        in_specs=in_specs,
        out_specs=jax.tree.map(lambda _: VMEM, outs),
        out_shape=outs,
        scratch_shapes=list(scratch),
        name=name,
        compiler_params=pltpu.CompilerParams(vmem_limit_bytes=limit * 2**20),
    )


def shape(*dims, dtype=BF):
    return jax.ShapeDtypeStruct(dims, dtype)


def pieces(group, heads):
    pair = heads // 2 * 2
    single = heads - pair
    out = [(0, pl.multiple_of(group * (pair * HD), pair * HD), pair * HD)] if pair else []
    if single:
        start = RUN * pair * HD + group * HD
        out.append((pair * HD, pl.multiple_of(start, HD), HD))
    return out


def any_fresh(slots, count):
    busy = slots[0] >= 0
    for n in range(1, count):
        busy = busy | (slots[n] >= 0)
    return busy


def weight_copy(w, part, target, sem):
    width = target.shape[0]
    start = pl.multiple_of((lax.axis_index("hid") ^ part) * width, width)
    return pltpu.make_async_copy(w.at[pl.ds(start, width), :], target, sem)


def pack_queries_kernel(q_in, *refs):
    outs, (q_buf, turned, sems) = refs[:RUN], refs[RUN:]
    copy = pltpu.make_async_copy(q_in, q_buf, sems.at[0])
    copy.start()
    copy.wait()
    turned[...] = q_buf[...].T
    low = lax.axis_index("tile") % RUN
    for i in range(RUN):
        for at, start, size in pieces(low ^ i, outs[i].shape[0] // HD):
            outs[i][at : at + size, :] = turned[pl.ds(start, size), :]


def prefetch_kernel(slots, x_in, x_c, wk, wv, kc, vc, acc, caches, token, *refs):
    later, (x_own, now, sems) = refs[:4], refs[4:]
    token[...] = jnp.zeros(token.shape, F32)
    busy = any_fresh(slots, caches.shape[1] // BLOCK)
    own = pltpu.make_async_copy(x_in, x_own, sems.at[0])
    rest = [
        pltpu.make_async_copy(kc, caches.at[0], sems.at[1]),
        pltpu.make_async_copy(vc, caches.at[1], sems.at[2]),
    ]
    copies = [
        weight_copy((wk, wv)[n % 2], n // 2, now.at[n] if n < 4 else later[n - 4], sems.at[3 + n])
        for n in range(8)
    ]

    @pl.when(busy)
    def _():
        own.start()
        for copy in copies:
            copy.start()

    for copy in rest:
        copy.start()

    @pl.when(busy)
    def _():
        own.wait()
        for n in range(4):
            x = (x_own, x_c)[n // 2]
            copies[n].wait()
            dots = jnp.dot(x[...], now[n], preferred_element_type=F32)
            acc[n % 2] = dots if n < 2 else acc[n % 2] + dots
        for copy in copies[4:]:
            copy.wait()

    for copy in rest:
        copy.wait()


def refresh_kernel(sc, x_y, x_cy, acc, caches, token, *refs):
    later, outs, mixed = refs[:4], refs[4 : 4 + RUN], refs[4 + RUN]
    width = x_y.shape[1] // RUN
    blocks = x_y.shape[0] // BLOCK
    low = lax.axis_index("tile") % RUN
    fresh = []
    for b in range(blocks):
        hit = sc[0] == b
        for n in range(1, blocks):
            hit = hit | (sc[n] == b)
        fresh.append(hit)
    busy = fresh[0]
    for hit in fresh[1:]:
        busy = busy | hit

    mixed[...] = caches[...]

    @pl.when(busy)
    def _():
        for n in range(2):
            both = jnp.dot(x_y[...], later[n][...], preferred_element_type=F32)
            both = both + jnp.dot(x_cy[...], later[2 + n][...], preferred_element_type=F32)
            total = (acc[n] + both).astype(BF)
            for b in range(blocks):
                rows = slice(b * BLOCK, (b + 1) * BLOCK)
                mixed[n, rows, :] = jnp.where(fresh[b], total[rows, :], caches[n, rows, :])

    heads = width // HD
    pair = heads // 2 * 2 * HD
    upper = lax.broadcasted_iota(jnp.int32, (x_y.shape[0], 2 * HD), 1) >= HD
    for i in range(RUN):
        group = low ^ i
        cols = pl.ds(pl.multiple_of(group * pair, 2 * HD), pair)
        outs[i][:, :pair] = mixed[0, :, cols]
        outs[i][:, pair : 2 * pair] = mixed[1, :, cols]
        if heads % 2:
            cols = pl.ds(pl.multiple_of(RUN * pair + group // 2 * (2 * HD), 2 * HD), 2 * HD)
            keys, values = mixed[0, :, cols], mixed[1, :, cols]

            @pl.when(group % 2 == 0)
            def _():
                outs[i][:, 2 * pair :] = jnp.where(upper, pltpu.roll(values, HD, 1), keys)

            @pl.when(group % 2 == 1)
            def _():
                outs[i][:, 2 * pair :] = jnp.where(upper, values, pltpu.roll(keys, HD, 1))


def item_of(start, dims, axis, split):
    index = start + lax.broadcasted_iota(jnp.int32, dims, axis)
    return jnp.where(index < split, 0, 1)


def query_flags(start, count, split, mask_item=None):
    dims = (HD, count)
    item = item_of(start, dims, 1, split)
    zero, one = item == 0, item == 1
    if mask_item is not None:
        off = item != mask_item
        zero, one = zero | off, one | off
    row = lax.broadcasted_iota(jnp.int32, dims, 0)
    hit = ((row == 0) & zero) | ((row == 1) & one)
    return jnp.where(hit, 1.0, 0.0).astype(BF)


def key_flags(start, count, split):
    dims = (count, HD)
    item = item_of(start, dims, 0, split)
    lane = lax.broadcasted_iota(jnp.int32, dims, 1)
    hit = ((lane == 0) & (item == 1)) | ((lane == 1) & (item == 0))
    return jnp.where(hit, NEG, 0.0).astype(BF)


def head_cols(h, heads):
    pair = heads // 2 * 2
    if h < pair:
        return h * HD, (pair + h) * HD
    return 2 * pair * HD, (2 * pair + 1) * HD


def extend_keys(kv_refs, starts, split, kext, vext):
    heads = kext.shape[0]
    at = 0
    for kv, start in zip(kv_refs, starts):
        count = kv.shape[0]
        aux = key_flags(start, count, split)
        for h in range(heads):
            key_col, value_col = head_cols(h, heads)
            keys = kv[:, key_col : key_col + HD]
            kext[h, at : at + count, :] = jnp.concatenate([keys, aux], 1)
            vext[h, :HD, at : at + count] = kv[:, value_col : value_col + HD].T
            vext[h, HD:, at : at + count] = jnp.ones((PAD, count), BF)
        at += count


def scores_of(kext, h, q_ref, flags):
    q = jnp.concatenate([q_ref[h * HD : (h + 1) * HD, :], flags], 0)
    return jnp.dot(kext[h], q, preferred_element_type=F32)


DEPTH = 3


def score_stream(units, score):
    ahead = [score(u) for u in units[:DEPTH]]
    for n, unit in enumerate(units):
        if n + DEPTH < len(units):
            ahead.append(score(units[n + DEPTH]))
        yield unit, ahead.pop(0)


def softmax_part(s, values):
    top = jnp.max(s, axis=0, keepdims=True)
    p = jnp.exp2((s - top) * SCALE).astype(BF)
    return top, jnp.dot(values, p, preferred_element_type=F32)


def places(rows):
    tile = lax.axis_index("tile")
    cube = tile // RUN
    own = [(tile ^ i) * rows for i in range(RUN)]
    far = jnp.where(cube == 0, RUN, RUN - 1) * rows
    edge = (tile % RUN) ^ jnp.where(cube == 0, RUN - 1, 0)
    return cube, own, far, edge


def pick_edge_kernel(q0, q1, q2, q3, out):
    edge = places(1)[3]
    for i, q in enumerate((q0, q1, q2, q3)):

        @pl.when(edge == i)
        def _(q=q):
            out[...] = q[...]


def attend_guest_kernel(sc, q_ref, k0, k1, k2, k3, out, kext, vext):
    heads = kext.shape[0]
    count = q_ref.shape[1]
    cube, own, far, _ = places(count)
    extend_keys((k0, k1, k2, k3), own, sc[0], kext, vext)
    flags = query_flags(far, count, sc[0], cube)
    row = lax.broadcasted_iota(jnp.int32, (PAD, count), 0)
    logs = jnp.zeros((PAD, count), F32)
    for h, s in score_stream(list(range(heads)), lambda h: scores_of(kext, h, q_ref, flags)):
        top, o = softmax_part(s, vext[h])
        total = o[HD : HD + 1, :]
        out[h * HD : (h + 1) * HD, :] = (o[:HD, :] / total).astype(BF)
        log = top * SCALE + jnp.log2(total)
        high = log.astype(BF).astype(F32)
        mid = (log - high).astype(BF).astype(F32)
        for n, piece in enumerate((high, mid, log - high - mid)):
            logs = jnp.where(row == 3 * h + n, piece, logs)
    out[heads * HD :, :] = logs.astype(BF)


def slot_scores(sc, q_refs, starts, kext, mask_item=None):
    heads = kext.shape[0]
    count = q_refs[0].shape[1]
    flags = [query_flags(start, count, sc[0], mask_item) for start in starts]
    units = [(i, h) for i in range(len(q_refs)) for h in range(heads)]
    return score_stream(units, lambda u: scores_of(kext, u[1], q_refs[u[0]], flags[u[0]]))


def attend_own_kernel(sc, wo, q0, q1, q2, q3, kext, vext, out, out_w, sems):
    copy = pltpu.make_async_copy(wo, out_w, sems.at[0])
    copy.start()
    count = q0.shape[1]
    _, own, _, _ = places(count)
    for (i, h), s in slot_scores(sc, (q0, q1, q2, q3), own, kext):
        top, o = softmax_part(s, vext[h])
        out[i, h, : HD + 8, :] = o[: HD + 8, :]
        out[i, h, HD + 8 :, :] = jnp.broadcast_to(top, (8, count))
    copy.wait()


def attend_merge_kernel(sc, q0, q1, q2, q3, part, b0, b1, b2, b3, guest, *refs):
    outs, (kv, kext, vext) = refs[:RUN], refs[RUN:]
    heads = kext.shape[0]
    count = q0.shape[1]
    cube, own, far, edge = places(count)
    kv[...] = (b0[...] + b1[...]) + (b2[...] + b3[...])
    extend_keys((kv,), (far,), sc[0], kext, vext)
    logs = guest[heads * HD :, :].astype(F32)
    for (i, h), s in slot_scores(sc, (q0, q1, q2, q3), own, kext, cube):
        at = slice(h * HD, (h + 1) * HD)
        log = logs[3 * h : 3 * h + 1, :] + logs[3 * h + 1 : 3 * h + 2, :]
        log = log + logs[3 * h + 2 : 3 * h + 3, :]
        log = jnp.where(edge == i, log, NEG)
        own_log = part[i, h, HD + 8 : HD + 9, :] * SCALE
        top = jnp.maximum(own_log, jnp.max(s, axis=0, keepdims=True) * SCALE)
        top = jnp.maximum(top, log)
        p = jnp.exp2(s * SCALE - top).astype(BF)
        near = jnp.exp2(own_log - top)
        share = jnp.exp2(log - top)
        o = jnp.dot(vext[h], p, preferred_element_type=F32)
        total = o[HD : HD + 1, :] + part[i, h, HD : HD + 1, :] * near + share
        o = o[:HD, :] + part[i, h, :HD, :] * near + guest[at, :].astype(F32) * share
        outs[i][at, :] = (o / total).astype(BF)


def send_tiles(value, tile_pairs):
    hids = lax.axis_size("hid")
    pairs = [(s * hids + h, d * hids + h) for s, d in tile_pairs for h in range(hids)]
    return lax.ppermute(value, AXES, pairs)


def guest_queries(q_parts):
    picked = call(pick_edge_kernel, "pick_edge", [VMEM] * RUN, shape(*q_parts[0].shape))(*q_parts)
    return move(picked, RUN, 0)


def attend_items(lengths, guest_q, q_parts, kv, kv_parts, out_weight):
    rows = kv[0].shape[0]
    heads = q_parts[0].shape[0] // HD
    ext = [shape(heads, RUN * rows, 2 * HD), shape(heads, HD + PAD, RUN * rows)]

    first, last = RUN - 1, RUN
    guest_kv = [send_tiles(kv[i], [(first, last + (first ^ i)), (last, i)]) for i in (0, 2)]
    guest_kv += [
        send_tiles(kv_parts[i], [(first ^ i, last + (first ^ i)), (last ^ i, i)]) for i in (1, 3)
    ]
    guest, kext, vext = call(
        attend_guest_kernel,
        "attend_guest",
        [SMEM] + [VMEM] * 5,
        [shape(heads * HD + PAD, rows)] + ext,
    )(lengths, guest_q, *kv_parts)
    guest = move(guest, RUN, 0)
    own, out_w = call(
        attend_own_kernel,
        "attend_own",
        [SMEM, HBM] + [VMEM] * 6,
        [shape(RUN, heads, HD + PAD, rows, dtype=F32), shape(*out_weight.shape)],
        [pltpu.SemaphoreType.DMA((1,))],
    )(lengths, out_weight, *q_parts, kext, vext)
    return out_w, call(
        attend_merge_kernel,
        "attend_merge",
        [SMEM] + [VMEM] * 10,
        [shape(*q.shape) for q in q_parts],
        [
            pltpu.VMEM(kv[0].shape, BF),
            pltpu.VMEM((heads, rows, 2 * HD), BF),
            pltpu.VMEM((heads, HD + PAD, rows), BF),
        ],
    )(lengths, *q_parts, own, *guest_kv, guest)


def attend_all_kernel(sc, starts, q_ref, kv_ref, out, kext, vext, kv_buf, sems, *, slot):
    heads = kext.shape[0]
    keys = kv_ref.shape[0]
    chunk = kv_buf.shape[0]
    flags = query_flags(starts[0], slot, sc[0])

    def step(j, state):
        rows = pl.ds(pl.multiple_of(j * chunk, chunk), chunk)
        copy = pltpu.make_async_copy(kv_ref.at[rows, :], kv_buf, sems.at[0])
        copy.start()
        copy.wait()
        parts = [kv_buf.at[slice(n * slot, (n + 1) * slot), :] for n in range(chunk // slot)]
        begin = [starts[1 + j * (chunk // slot) + n] for n in range(chunk // slot)]
        extend_keys(parts, begin, sc[0], kext, vext)
        after = []
        for h in range(heads):
            top, acc = state[h]
            s = scores_of(kext, h, q_ref, flags)
            new = jnp.maximum(top, jnp.max(s, axis=0, keepdims=True))
            p = jnp.exp2((s - new) * SCALE).astype(BF)
            acc = acc * jnp.exp2((top - new) * SCALE)
            after.append((new, acc + jnp.dot(vext[h], p, preferred_element_type=F32)))
        return tuple(after)

    start = jnp.full((1, slot), 2 * NEG, F32), jnp.zeros((HD + PAD, slot), F32)
    state = lax.fori_loop(0, keys // chunk, step, (start,) * heads)
    for h in range(heads):
        o = state[h][1]
        out[h * HD : (h + 1) * HD, :] = (o[:HD, :] / o[HD : HD + 1, :]).astype(BF)


def attend_gathered(lengths, tile, q_parts, kv_parts):
    rows = kv_parts[0].shape[0]
    heads = q_parts[0].shape[0] // HD
    masks = list(range(RUN))
    kv = jnp.concatenate(kv_parts, 0)
    bit = RUN
    while bit < lax.axis_size("tile"):
        kv = jnp.concatenate([kv, move(kv, bit, 0)], 0)
        masks = masks + [m ^ bit for m in masks]
        bit *= 2
    key_starts = (tile ^ jnp.array(masks, dtype=jnp.int32)) * rows
    chunk = RUN * rows
    outs = []
    for i, q in enumerate(q_parts):
        starts = jnp.concatenate([((tile ^ i) * rows)[None], key_starts]).astype(jnp.int32)
        outs.append(
            call(
                functools.partial(attend_all_kernel, slot=rows),
                "attend_all",
                [SMEM, SMEM, VMEM, HBM],
                shape(*q.shape),
                [
                    pltpu.VMEM((heads, chunk, 2 * HD), BF),
                    pltpu.VMEM((heads, HD + PAD, chunk), BF),
                    pltpu.VMEM((chunk, kv.shape[1]), BF),
                    pltpu.SemaphoreType.DMA((1,)),
                ],
            )(lengths, starts, q, kv)
        )
    return outs


def gather_lhs_kernel(a0, a1, a2, a3, w, lhs, out, turned, *, block):
    for i, a in enumerate((a0, a1, a2, a3)):
        for at, start, size in pieces(lax.axis_index("tile") % RUN ^ i, a.shape[0] // HD):
            turned[pl.ds(start, size), :] = a[at : at + size, :]
    lhs[...] = turned[...].T
    out[...] = block_product(lhs, w, block).astype(out.dtype)


def block_product(lhs, w, block):
    width = w.shape[0]
    cols = pl.ds(pl.multiple_of((lax.axis_index("hid") ^ block) * width, width), width)
    return jnp.dot(lhs[...], w[:, cols], preferred_element_type=F32)


def project_kernel(lhs, w, *outs, blocks):
    for out, block in zip(outs, blocks):
        out[...] = block_product(lhs, w, block).astype(out.dtype)


def project(lhs, w, blocks, dtypes):
    return call(
        functools.partial(project_kernel, blocks=blocks),
        "project",
        [VMEM, VMEM],
        [shape(lhs.shape[0], w.shape[0], dtype=dtype) for dtype in dtypes],
    )(lhs, w)


def body(
    item_lengths,
    refresh_slots,
    layer_input,
    key_weight,
    value_weight,
    queries,
    key_cache,
    value_cache,
    out_weight,
):
    rows, width = queries.shape
    tile = lax.axis_index("tile")
    stay = functools.partial(pltpu.with_memory_space_constraint, memory_space=pltpu.HBM)
    x_y = move(layer_input, 0, 2)
    x_c = move(layer_input, 0, 1)
    part = width // RUN
    q_packed = call(
        pack_queries_kernel,
        "pack_queries",
        [HBM],
        [shape(part, rows)] * RUN,
        [
            pltpu.VMEM((rows, width), BF),
            pltpu.VMEM((width, rows), BF),
            pltpu.SemaphoreType.DMA((1,)),
        ],
    )(stay(queries))
    q_parts = [q_packed[0]] + [move(q_packed[i], i, 0) for i in (1, 2, 3)]
    sums, caches, token, *later = call(
        prefetch_kernel,
        "prefetch",
        [SMEM, HBM, VMEM] + [HBM] * 4,
        [
            shape(2, rows, width, dtype=F32),
            shape(2, rows, width),
            shape(8, 128, dtype=F32),
        ]
        + [shape(width, width)] * 4,
        [
            pltpu.VMEM((rows, width), BF),
            pltpu.VMEM((4, width, width), BF),
            pltpu.SemaphoreType.DMA((11,)),
        ],
    )(
        refresh_slots,
        stay(layer_input),
        x_c,
        stay(key_weight),
        stay(value_weight),
        stay(key_cache),
        stay(value_cache),
    )
    x_y, token, q_parts = lax.optimization_barrier((x_y, token, q_parts))
    x_cy = move(x_y, 0, 1)
    kv = call(
        refresh_kernel,
        "refresh",
        [SMEM] + [VMEM] * 9,
        [shape(rows, 2 * part)] * RUN,
        [pltpu.VMEM((2, rows, width), BF)],
    )(refresh_slots, x_y, x_cy, sums, caches, token, *later)
    items = lax.axis_size("tile") == 2 * RUN
    if items:
        guest_q = guest_queries(q_parts)
        z_part, guest_q = lax.optimization_barrier((kv[2], guest_q))
        kv = [kv[0], kv[1], z_part, kv[3]]
    moved = {i: move(kv[i], i, 0) for i in (1, 2, 3)}
    kv_parts = [kv[0], moved[1], moved[2], moved[3]]
    if items:
        out_w, back = attend_items(item_lengths, guest_q, q_parts, kv, kv_parts, stay(out_weight))
    else:
        out_w, back = out_weight, attend_gathered(item_lengths, tile, q_parts, kv_parts)
    parts = [back[0]] + [move(back[i], i, 0) for i in (1, 2, 3)]

    lhs, send_y = call(
        functools.partial(gather_lhs_kernel, block=3),
        "project_first",
        [VMEM] * 5,
        [shape(rows, width), shape(rows, width)],
        [pltpu.VMEM((width, rows), BF)],
    )(*parts, out_w)
    got = move(send_y, 0, 1)
    keep_y, send, keep = project(lhs, out_w, (2, 1, 0), (F32, BF, F32))
    via_y, send = lax.optimization_barrier(((keep_y + got.astype(F32)).astype(BF), send))
    got_y = move(via_y, 0, 2)
    got = move(send, 0, 1)
    return (keep + got.astype(F32) + got_y.astype(F32)).astype(BF)


def solution(mesh):
    return jax.shard_map(
        body,
        mesh=mesh,
        in_specs=(
            P(),
            P("tile"),
            P("tile", "hid"),
            P(None, "hid"),
            P(None, "hid"),
            P("tile", "hid"),
            P("tile", "hid"),
            P("tile", "hid"),
            P("hid", None),
        ),
        out_specs=P("tile", "hid"),
        check_vma=False,
    )
```

```python
import functools

import jax
import jax.numpy as jnp
from jax import lax
from jax.experimental import pallas as pl
from jax.experimental.pallas import tpu as pltpu
from jax.sharding import PartitionSpec as P

HD = 64
BLOCK = 128
RUN = 4
NEG = -1e30
SCALE = 0.125 * 1.4426950408889634
AXES = ("tile", "hid")
BF = jnp.bfloat16
F32 = jnp.float32


def move(value, tile_mask, hid_mask):
    tiles, hids = lax.axis_size("tile"), lax.axis_size("hid")
    pairs = [
        (t * hids + h, (t ^ tile_mask) * hids + (h ^ hid_mask))
        for t in range(tiles)
        for h in range(hids)
    ]
    return lax.ppermute(value, AXES, pairs)


VMEM = pl.BlockSpec(memory_space=pltpu.VMEM)
SMEM = pl.BlockSpec(memory_space=pltpu.SMEM)
HBM = pl.BlockSpec(memory_space=pltpu.HBM)
PAD = 16


def call(kernel, name, in_specs, outs, scratch=(), limit=24):
    return pl.pallas_call(
        kernel,
        in_specs=in_specs,
        out_specs=jax.tree.map(lambda _: VMEM, outs),
        out_shape=outs,
        scratch_shapes=list(scratch),
        name=name,
        compiler_params=pltpu.CompilerParams(vmem_limit_bytes=limit * 2**20),
    )


def shape(*dims, dtype=BF):
    return jax.ShapeDtypeStruct(dims, dtype)


def pieces(group, heads):
    pair = heads // 2 * 2
    single = heads - pair
    out = [(0, pl.multiple_of(group * (pair * HD), pair * HD), pair * HD)] if pair else []
    if single:
        start = RUN * pair * HD + group * HD
        out.append((pair * HD, pl.multiple_of(start, HD), HD))
    return out


def any_fresh(slots, count):
    busy = slots[0] >= 0
    for n in range(1, count):
        busy = busy | (slots[n] >= 0)
    return busy


def weight_copy(w, part, target, sem):
    width = target.shape[0]
    start = pl.multiple_of((lax.axis_index("hid") ^ part) * width, width)
    return pltpu.make_async_copy(w.at[pl.ds(start, width), :], target, sem)


def pack_queries_kernel(q_in, *refs):
    outs, (q_buf, turned, sems) = refs[:RUN], refs[RUN:]
    copy = pltpu.make_async_copy(q_in, q_buf, sems.at[0])
    copy.start()
    copy.wait()
    turned[...] = q_buf[...].T
    low = lax.axis_index("tile") % RUN
    for i in range(RUN):
        for at, start, size in pieces(low ^ i, outs[i].shape[0] // HD):
            outs[i][at : at + size, :] = turned[pl.ds(start, size), :]


def prefetch_kernel(slots, x_in, x_c, wk, wv, kc, vc, acc, caches, token, *refs):
    later, (x_own, now, sems) = refs[:4], refs[4:]
    token[...] = jnp.zeros(token.shape, F32)
    busy = any_fresh(slots, caches.shape[1] // BLOCK)
    own = pltpu.make_async_copy(x_in, x_own, sems.at[0])
    rest = [
        pltpu.make_async_copy(kc, caches.at[0], sems.at[1]),
        pltpu.make_async_copy(vc, caches.at[1], sems.at[2]),
    ]
    copies = [
        weight_copy((wk, wv)[n % 2], n // 2, now.at[n] if n < 4 else later[n - 4], sems.at[3 + n])
        for n in range(8)
    ]

    @pl.when(busy)
    def _():
        own.start()
        for copy in copies:
            copy.start()

    for copy in rest:
        copy.start()

    @pl.when(busy)
    def _():
        own.wait()
        for n in range(4):
            x = (x_own, x_c)[n // 2]
            copies[n].wait()
            dots = jnp.dot(x[...], now[n], preferred_element_type=F32)
            acc[n % 2] = dots if n < 2 else acc[n % 2] + dots
        for copy in copies[4:]:
            copy.wait()

    for copy in rest:
        copy.wait()


def refresh_kernel(sc, x_y, x_cy, acc, caches, token, *refs):
    later, outs, mixed = refs[:4], refs[4 : 4 + RUN], refs[4 + RUN]
    width = x_y.shape[1] // RUN
    blocks = x_y.shape[0] // BLOCK
    low = lax.axis_index("tile") % RUN
    fresh = []
    for b in range(blocks):
        hit = sc[0] == b
        for n in range(1, blocks):
            hit = hit | (sc[n] == b)
        fresh.append(hit)
    busy = fresh[0]
    for hit in fresh[1:]:
        busy = busy | hit

    mixed[...] = caches[...]

    @pl.when(busy)
    def _():
        for n in range(2):
            both = jnp.dot(x_y[...], later[n][...], preferred_element_type=F32)
            both = both + jnp.dot(x_cy[...], later[2 + n][...], preferred_element_type=F32)
            total = (acc[n] + both).astype(BF)
            for b in range(blocks):
                rows = slice(b * BLOCK, (b + 1) * BLOCK)
                mixed[n, rows, :] = jnp.where(fresh[b], total[rows, :], caches[n, rows, :])

    heads = width // HD
    pair = heads // 2 * 2 * HD
    upper = lax.broadcasted_iota(jnp.int32, (x_y.shape[0], 2 * HD), 1) >= HD
    for i in range(RUN):
        group = low ^ i
        cols = pl.ds(pl.multiple_of(group * pair, 2 * HD), pair)
        outs[i][:, :pair] = mixed[0, :, cols]
        outs[i][:, pair : 2 * pair] = mixed[1, :, cols]
        if heads % 2:
            cols = pl.ds(pl.multiple_of(RUN * pair + group // 2 * (2 * HD), 2 * HD), 2 * HD)
            keys, values = mixed[0, :, cols], mixed[1, :, cols]

            @pl.when(group % 2 == 0)
            def _():
                outs[i][:, 2 * pair :] = jnp.where(upper, pltpu.roll(values, HD, 1), keys)

            @pl.when(group % 2 == 1)
            def _():
                outs[i][:, 2 * pair :] = jnp.where(upper, values, pltpu.roll(keys, HD, 1))


def item_of(start, dims, axis, split):
    index = start + lax.broadcasted_iota(jnp.int32, dims, axis)
    return jnp.where(index < split, 0, 1)


def query_flags(start, count, split, mask_item=None):
    dims = (HD, count)
    item = item_of(start, dims, 1, split)
    zero, one = item == 0, item == 1
    if mask_item is not None:
        off = item != mask_item
        zero, one = zero | off, one | off
    row = lax.broadcasted_iota(jnp.int32, dims, 0)
    hit = ((row == 0) & zero) | ((row == 1) & one)
    return jnp.where(hit, 1.0, 0.0).astype(BF)


def key_flags(start, count, split):
    dims = (count, HD)
    item = item_of(start, dims, 0, split)
    lane = lax.broadcasted_iota(jnp.int32, dims, 1)
    hit = ((lane == 0) & (item == 1)) | ((lane == 1) & (item == 0))
    return jnp.where(hit, NEG, 0.0).astype(BF)


def head_cols(h, heads):
    pair = heads // 2 * 2
    if h < pair:
        return h * HD, (pair + h) * HD
    return 2 * pair * HD, (2 * pair + 1) * HD


def extend_keys(kv_refs, starts, split, kext, vext):
    heads = kext.shape[0]
    at = 0
    for kv, start in zip(kv_refs, starts):
        count = kv.shape[0]
        aux = key_flags(start, count, split)
        for h in range(heads):
            key_col, value_col = head_cols(h, heads)
            keys = kv[:, key_col : key_col + HD]
            kext[h, at : at + count, :] = jnp.concatenate([keys, aux], 1)
            vext[h, :HD, at : at + count] = kv[:, value_col : value_col + HD].T
            vext[h, HD:, at : at + count] = jnp.ones((PAD, count), BF)
        at += count


def scores_of(kext, h, q_ref, flags):
    q = jnp.concatenate([q_ref[h * HD : (h + 1) * HD, :], flags], 0)
    return jnp.dot(kext[h], q, preferred_element_type=F32)


DEPTH = 3


def score_stream(units, score):
    ahead = [score(u) for u in units[:DEPTH]]
    for n, unit in enumerate(units):
        if n + DEPTH < len(units):
            ahead.append(score(units[n + DEPTH]))
        yield unit, ahead.pop(0)


def softmax_part(s, values):
    top = jnp.max(s, axis=0, keepdims=True)
    p = jnp.exp2((s - top) * SCALE).astype(BF)
    return top, jnp.dot(values, p, preferred_element_type=F32)


def places(rows):
    tile = lax.axis_index("tile")
    cube = tile // RUN
    own = [(tile ^ i) * rows for i in range(RUN)]
    far = jnp.where(cube == 0, RUN, RUN - 1) * rows
    edge = (tile % RUN) ^ jnp.where(cube == 0, RUN - 1, 0)
    return cube, own, far, edge


def pick_edge_kernel(q0, q1, q2, q3, out):
    edge = places(1)[3]
    for i, q in enumerate((q0, q1, q2, q3)):

        @pl.when(edge == i)
        def _(q=q):
            out[...] = q[...]


def attend_guest_kernel(sc, q_ref, k0, k1, k2, k3, out, kext, vext):
    heads = kext.shape[0]
    count = q_ref.shape[1]
    cube, own, far, _ = places(count)
    extend_keys((k0, k1, k2, k3), own, sc[0], kext, vext)
    flags = query_flags(far, count, sc[0], cube)
    row = lax.broadcasted_iota(jnp.int32, (PAD, count), 0)
    logs = jnp.zeros((PAD, count), F32)
    for h, s in score_stream(list(range(heads)), lambda h: scores_of(kext, h, q_ref, flags)):
        top, o = softmax_part(s, vext[h])
        total = o[HD : HD + 1, :]
        out[h * HD : (h + 1) * HD, :] = (o[:HD, :] / total).astype(BF)
        log = top * SCALE + jnp.log2(total)
        high = log.astype(BF).astype(F32)
        mid = (log - high).astype(BF).astype(F32)
        for n, piece in enumerate((high, mid, log - high - mid)):
            logs = jnp.where(row == 3 * h + n, piece, logs)
    out[heads * HD :, :] = logs.astype(BF)


def slot_scores(sc, q_refs, starts, kext, mask_item=None):
    heads = kext.shape[0]
    count = q_refs[0].shape[1]
    flags = [query_flags(start, count, sc[0], mask_item) for start in starts]
    units = [(i, h) for i in range(len(q_refs)) for h in range(heads)]
    return score_stream(units, lambda u: scores_of(kext, u[1], q_refs[u[0]], flags[u[0]]))


def attend_own_kernel(sc, wo, q0, q1, q2, q3, kext, vext, out, out_w, sems):
    copy = pltpu.make_async_copy(wo, out_w, sems.at[0])
    copy.start()
    count = q0.shape[1]
    _, own, _, _ = places(count)
    for (i, h), s in slot_scores(sc, (q0, q1, q2, q3), own, kext):
        top, o = softmax_part(s, vext[h])
        out[i, h, : HD + 8, :] = o[: HD + 8, :]
        out[i, h, HD + 8 :, :] = jnp.broadcast_to(top, (8, count))
    copy.wait()


def attend_merge_kernel(sc, q0, q1, q2, q3, part, b0, b1, b2, b3, guest, *refs, taker):
    outs, (kv, kext, vext) = refs[:RUN], refs[RUN:]
    heads = kext.shape[0]
    count = q0.shape[1]
    cube, own, far, edge = places(count)
    kv[...] = (b0[...] + b1[...]) + (b2[...] + b3[...])
    extend_keys((kv,), (far,), sc[0], kext, vext)
    logs = guest[heads * HD :, :].astype(F32)
    for (i, h), s in slot_scores(sc, (q0, q1, q2, q3), own, kext, cube):
        at = slice(h * HD, (h + 1) * HD)
        log = logs[3 * h : 3 * h + 1, :] + logs[3 * h + 1 : 3 * h + 2, :]
        log = log + logs[3 * h + 2 : 3 * h + 3, :]
        log = jnp.where((edge == i) & (cube == taker), log, NEG)
        own_log = part[i, h, HD + 8 : HD + 9, :] * SCALE
        top = jnp.maximum(own_log, jnp.max(s, axis=0, keepdims=True) * SCALE)
        top = jnp.maximum(top, log)
        p = jnp.exp2(s * SCALE - top).astype(BF)
        near = jnp.exp2(own_log - top)
        share = jnp.exp2(log - top)
        o = jnp.dot(vext[h], p, preferred_element_type=F32)
        total = o[HD : HD + 1, :] + part[i, h, HD : HD + 1, :] * near + share
        o = o[:HD, :] + part[i, h, :HD, :] * near + guest[at, :].astype(F32) * share
        outs[i][at, :] = (o / total).astype(BF)


def send_tiles(value, tile_pairs):
    hids = lax.axis_size("hid")
    pairs = [(s * hids + h, d * hids + h) for s, d in tile_pairs for h in range(hids)]
    return lax.ppermute(value, AXES, pairs)


def guest_queries(q_parts, up):
    picked = call(pick_edge_kernel, "pick_edge", [VMEM] * RUN, shape(*q_parts[0].shape))(*q_parts)
    return across(picked, not up)


def across(value, up):
    return send_tiles(value, [(t, t + RUN) if up else (t + RUN, t) for t in range(RUN)])


def attend_items(lengths, guest_q, q_parts, kv, kv_parts, out_weight, up):
    rows = kv[0].shape[0]
    heads = q_parts[0].shape[0] // HD
    ext = [shape(heads, RUN * rows, 2 * HD), shape(heads, HD + PAD, RUN * rows)]

    first, last = RUN - 1, RUN
    guest_kv = [
        send_tiles(kv[i], [(last, i) if up else (first, last + (first ^ i))]) for i in (0, 2, 3)
    ]
    relay = (last ^ 1, 1) if up else (first ^ 1, last + (first ^ 1))
    guest_kv.append(send_tiles(kv_parts[1], [relay]))
    guest, kext, vext = call(
        attend_guest_kernel,
        "attend_guest",
        [SMEM] + [VMEM] * 5,
        [shape(heads * HD + PAD, rows)] + ext,
    )(lengths, guest_q, *kv_parts)
    guest = across(guest, up)
    own, out_w = call(
        attend_own_kernel,
        "attend_own",
        [SMEM, HBM] + [VMEM] * 6,
        [shape(RUN, heads, HD + PAD, rows, dtype=F32), shape(*out_weight.shape)],
        [pltpu.SemaphoreType.DMA((1,))],
    )(lengths, out_weight, *q_parts, kext, vext)
    return out_w, call(
        functools.partial(attend_merge_kernel, taker=1 if up else 0),
        "attend_merge",
        [SMEM] + [VMEM] * 10,
        [shape(*q.shape) for q in q_parts],
        [
            pltpu.VMEM(kv[0].shape, BF),
            pltpu.VMEM((heads, rows, 2 * HD), BF),
            pltpu.VMEM((heads, HD + PAD, rows), BF),
        ],
    )(lengths, *q_parts, own, *guest_kv, guest)


def attend_all_kernel(sc, starts, q_ref, kv_ref, out, kext, vext, kv_buf, sems, *, slot):
    heads = kext.shape[0]
    keys = kv_ref.shape[0]
    chunk = kv_buf.shape[0]
    flags = query_flags(starts[0], slot, sc[0])

    def step(j, state):
        rows = pl.ds(pl.multiple_of(j * chunk, chunk), chunk)
        copy = pltpu.make_async_copy(kv_ref.at[rows, :], kv_buf, sems.at[0])
        copy.start()
        copy.wait()
        parts = [kv_buf.at[slice(n * slot, (n + 1) * slot), :] for n in range(chunk // slot)]
        begin = [starts[1 + j * (chunk // slot) + n] for n in range(chunk // slot)]
        extend_keys(parts, begin, sc[0], kext, vext)
        after = []
        for h in range(heads):
            top, acc = state[h]
            s = scores_of(kext, h, q_ref, flags)
            new = jnp.maximum(top, jnp.max(s, axis=0, keepdims=True))
            p = jnp.exp2((s - new) * SCALE).astype(BF)
            acc = acc * jnp.exp2((top - new) * SCALE)
            after.append((new, acc + jnp.dot(vext[h], p, preferred_element_type=F32)))
        return tuple(after)

    start = jnp.full((1, slot), 2 * NEG, F32), jnp.zeros((HD + PAD, slot), F32)
    state = lax.fori_loop(0, keys // chunk, step, (start,) * heads)
    for h in range(heads):
        o = state[h][1]
        out[h * HD : (h + 1) * HD, :] = (o[:HD, :] / o[HD : HD + 1, :]).astype(BF)


def attend_gathered(lengths, tile, q_parts, kv_parts):
    rows = kv_parts[0].shape[0]
    heads = q_parts[0].shape[0] // HD
    masks = list(range(RUN))
    kv = jnp.concatenate(kv_parts, 0)
    bit = RUN
    while bit < lax.axis_size("tile"):
        kv = jnp.concatenate([kv, move(kv, bit, 0)], 0)
        masks = masks + [m ^ bit for m in masks]
        bit *= 2
    key_starts = (tile ^ jnp.array(masks, dtype=jnp.int32)) * rows
    chunk = RUN * rows
    outs = []
    for i, q in enumerate(q_parts):
        starts = jnp.concatenate([((tile ^ i) * rows)[None], key_starts]).astype(jnp.int32)
        outs.append(
            call(
                functools.partial(attend_all_kernel, slot=rows),
                "attend_all",
                [SMEM, SMEM, VMEM, HBM],
                shape(*q.shape),
                [
                    pltpu.VMEM((heads, chunk, 2 * HD), BF),
                    pltpu.VMEM((heads, HD + PAD, chunk), BF),
                    pltpu.VMEM((chunk, kv.shape[1]), BF),
                    pltpu.SemaphoreType.DMA((1,)),
                ],
            )(lengths, starts, q, kv)
        )
    return outs


def gather_lhs_kernel(a0, a1, a2, a3, w, lhs, out, turned, *, block):
    for i, a in enumerate((a0, a1, a2, a3)):
        for at, start, size in pieces(lax.axis_index("tile") % RUN ^ i, a.shape[0] // HD):
            turned[pl.ds(start, size), :] = a[at : at + size, :]
    lhs[...] = turned[...].T
    out[...] = block_product(lhs, w, block).astype(out.dtype)


def block_product(lhs, w, block):
    width = w.shape[0]
    cols = pl.ds(pl.multiple_of((lax.axis_index("hid") ^ block) * width, width), width)
    return jnp.dot(lhs[...], w[:, cols], preferred_element_type=F32)


def project_kernel(lhs, w, *outs, blocks):
    for out, block in zip(outs, blocks):
        out[...] = block_product(lhs, w, block).astype(out.dtype)


def project(lhs, w, blocks, dtypes):
    return call(
        functools.partial(project_kernel, blocks=blocks),
        "project",
        [VMEM, VMEM],
        [shape(lhs.shape[0], w.shape[0], dtype=dtype) for dtype in dtypes],
    )(lhs, w)


def layer(
    up,
    item_lengths,
    refresh_slots,
    layer_input,
    key_weight,
    value_weight,
    queries,
    key_cache,
    value_cache,
    out_weight,
):
    rows, width = queries.shape
    tile = lax.axis_index("tile")
    stay = functools.partial(pltpu.with_memory_space_constraint, memory_space=pltpu.HBM)
    x_y = move(layer_input, 0, 2)
    x_c = move(layer_input, 0, 1)
    part = width // RUN
    q_packed = call(
        pack_queries_kernel,
        "pack_queries",
        [HBM],
        [shape(part, rows)] * RUN,
        [
            pltpu.VMEM((rows, width), BF),
            pltpu.VMEM((width, rows), BF),
            pltpu.SemaphoreType.DMA((1,)),
        ],
    )(stay(queries))
    q_parts = [q_packed[0]] + [move(q_packed[i], i, 0) for i in (1, 2, 3)]
    sums, caches, token, *later = call(
        prefetch_kernel,
        "prefetch",
        [SMEM, HBM, VMEM] + [HBM] * 4,
        [
            shape(2, rows, width, dtype=F32),
            shape(2, rows, width),
            shape(8, 128, dtype=F32),
        ]
        + [shape(width, width)] * 4,
        [
            pltpu.VMEM((rows, width), BF),
            pltpu.VMEM((4, width, width), BF),
            pltpu.SemaphoreType.DMA((11,)),
        ],
    )(
        refresh_slots,
        stay(layer_input),
        x_c,
        stay(key_weight),
        stay(value_weight),
        stay(key_cache),
        stay(value_cache),
    )
    x_y, token, q_parts = lax.optimization_barrier((x_y, token, q_parts))
    x_cy = move(x_y, 0, 1)
    kv = call(
        refresh_kernel,
        "refresh",
        [SMEM] + [VMEM] * 9,
        [shape(rows, 2 * part)] * RUN,
        [pltpu.VMEM((2, rows, width), BF)],
    )(refresh_slots, x_y, x_cy, sums, caches, token, *later)
    items = up is not None
    if items:
        guest_q = guest_queries(q_parts, up)
        far_part, guest_q = lax.optimization_barrier((kv[3], guest_q))
        kv = [kv[0], kv[1], kv[2], far_part]
    moved = {i: move(kv[i], i, 0) for i in (1, 2, 3)}
    kv_parts = [kv[0], moved[1], moved[2], moved[3]]
    if items:
        out_w, back = attend_items(item_lengths, guest_q, q_parts, kv, kv_parts, stay(out_weight), up)
    else:
        out_w, back = out_weight, attend_gathered(item_lengths, tile, q_parts, kv_parts)
    parts = [back[0]] + [move(back[i], i, 0) for i in (1, 2, 3)]

    lhs, send_y = call(
        functools.partial(gather_lhs_kernel, block=3),
        "project_first",
        [VMEM] * 5,
        [shape(rows, width), shape(rows, width)],
        [pltpu.VMEM((width, rows), BF)],
    )(*parts, out_w)
    got = move(send_y, 0, 1)
    keep_y, send, keep = project(lhs, out_w, (2, 1, 0), (F32, BF, F32))
    via_y, send = lax.optimization_barrier(((keep_y + got.astype(F32)).astype(BF), send))
    got_y = move(via_y, 0, 2)
    got = move(send, 0, 1)
    return (keep + got.astype(F32) + got_y.astype(F32)).astype(BF)


def body(item_lengths, refresh_slots, layer_input, *rest):
    args = (item_lengths, refresh_slots, layer_input) + rest
    if lax.axis_size("tile") != 2 * RUN:
        return layer(None, *args)
    half = RUN * layer_input.shape[0]
    branches = [functools.partial(layer, up) for up in (True, False)]
    return lax.cond(item_lengths[0] > half, *branches, *args)


def solution(mesh):
    return jax.shard_map(
        body,
        mesh=mesh,
        in_specs=(
            P(),
            P("tile"),
            P("tile", "hid"),
            P(None, "hid"),
            P(None, "hid"),
            P("tile", "hid"),
            P("tile", "hid"),
            P("tile", "hid"),
            P("hid", None),
        ),
        out_specs=P("tile", "hid"),
        check_vma=False,
    )
```

```python
import functools

import jax
import jax.numpy as jnp
from jax import lax
from jax.experimental import pallas as pl
from jax.experimental.pallas import tpu as pltpu
from jax.sharding import PartitionSpec as P

HD = 64
BLOCK = 128
RUN = 4
NEG = -1e30
SCALE = 0.125 * 1.4426950408889634
AXES = ("tile", "hid")
BF = jnp.bfloat16
F32 = jnp.float32


def move(value, tile_mask, hid_mask):
    tiles, hids = lax.axis_size("tile"), lax.axis_size("hid")
    pairs = [
        (t * hids + h, (t ^ tile_mask) * hids + (h ^ hid_mask))
        for t in range(tiles)
        for h in range(hids)
    ]
    return lax.ppermute(value, AXES, pairs)


VMEM = pl.BlockSpec(memory_space=pltpu.VMEM)
SMEM = pl.BlockSpec(memory_space=pltpu.SMEM)
HBM = pl.BlockSpec(memory_space=pltpu.HBM)
PAD = 16


def call(kernel, name, in_specs, outs, scratch=(), limit=24):
    return pl.pallas_call(
        kernel,
        in_specs=in_specs,
        out_specs=jax.tree.map(lambda _: VMEM, outs),
        out_shape=outs,
        scratch_shapes=list(scratch),
        name=name,
        compiler_params=pltpu.CompilerParams(vmem_limit_bytes=limit * 2**20),
    )


def shape(*dims, dtype=BF):
    return jax.ShapeDtypeStruct(dims, dtype)


def pieces(group, heads):
    pair = heads // 2 * 2
    single = heads - pair
    out = [(0, pl.multiple_of(group * (pair * HD), pair * HD), pair * HD)] if pair else []
    if single:
        start = RUN * pair * HD + group * HD
        out.append((pair * HD, pl.multiple_of(start, HD), HD))
    return out


def any_fresh(slots, count):
    busy = slots[0] >= 0
    for n in range(1, count):
        busy = busy | (slots[n] >= 0)
    return busy


def weight_copy(w, part, target, sem):
    width = target.shape[0]
    start = pl.multiple_of((lax.axis_index("hid") ^ part) * width, width)
    return pltpu.make_async_copy(w.at[pl.ds(start, width), :], target, sem)


def pack_queries_kernel(q_in, *refs):
    outs, (q_buf, turned, sems) = refs[:RUN], refs[RUN:]
    copy = pltpu.make_async_copy(q_in, q_buf, sems.at[0])
    copy.start()
    copy.wait()
    turned[...] = q_buf[...].T
    low = lax.axis_index("tile") % RUN
    for i in range(RUN):
        for at, start, size in pieces(low ^ i, outs[i].shape[0] // HD):
            outs[i][at : at + size, :] = turned[pl.ds(start, size), :]


def prefetch_kernel(slots, x_in, x_c, wk, wv, kc, vc, acc, caches, token, *refs):
    later, (x_own, now, sems) = refs[:4], refs[4:]
    token[...] = jnp.zeros(token.shape, F32)
    busy = any_fresh(slots, caches.shape[1] // BLOCK)
    own = pltpu.make_async_copy(x_in, x_own, sems.at[0])
    rest = [
        pltpu.make_async_copy(kc, caches.at[0], sems.at[1]),
        pltpu.make_async_copy(vc, caches.at[1], sems.at[2]),
    ]
    copies = [
        weight_copy((wk, wv)[n % 2], n // 2, now.at[n] if n < 4 else later[n - 4], sems.at[3 + n])
        for n in range(8)
    ]

    @pl.when(busy)
    def _():
        own.start()
        for copy in copies:
            copy.start()

    for copy in rest:
        copy.start()

    @pl.when(busy)
    def _():
        own.wait()
        for n in range(4):
            x = (x_own, x_c)[n // 2]
            copies[n].wait()
            dots = jnp.dot(x[...], now[n], preferred_element_type=F32)
            acc[n % 2] = dots if n < 2 else acc[n % 2] + dots
        for copy in copies[4:]:
            copy.wait()

    for copy in rest:
        copy.wait()


def refresh_kernel(sc, x_y, x_cy, acc, caches, token, *refs):
    later, outs, mixed = refs[:4], refs[4 : 4 + RUN], refs[4 + RUN]
    width = x_y.shape[1] // RUN
    blocks = x_y.shape[0] // BLOCK
    low = lax.axis_index("tile") % RUN
    fresh = []
    for b in range(blocks):
        hit = sc[0] == b
        for n in range(1, blocks):
            hit = hit | (sc[n] == b)
        fresh.append(hit)
    busy = fresh[0]
    for hit in fresh[1:]:
        busy = busy | hit

    mixed[...] = caches[...]

    @pl.when(busy)
    def _():
        for n in range(2):
            both = jnp.dot(x_y[...], later[n][...], preferred_element_type=F32)
            both = both + jnp.dot(x_cy[...], later[2 + n][...], preferred_element_type=F32)
            total = (acc[n] + both).astype(BF)
            for b in range(blocks):
                rows = slice(b * BLOCK, (b + 1) * BLOCK)
                mixed[n, rows, :] = jnp.where(fresh[b], total[rows, :], caches[n, rows, :])

    heads = width // HD
    pair = heads // 2 * 2 * HD
    upper = lax.broadcasted_iota(jnp.int32, (x_y.shape[0], 2 * HD), 1) >= HD
    for i in range(RUN):
        group = low ^ i
        cols = pl.ds(pl.multiple_of(group * pair, 2 * HD), pair)
        outs[i][:, :pair] = mixed[0, :, cols]
        outs[i][:, pair : 2 * pair] = mixed[1, :, cols]
        if heads % 2:
            cols = pl.ds(pl.multiple_of(RUN * pair + group // 2 * (2 * HD), 2 * HD), 2 * HD)
            keys, values = mixed[0, :, cols], mixed[1, :, cols]

            @pl.when(group % 2 == 0)
            def _():
                outs[i][:, 2 * pair :] = jnp.where(upper, pltpu.roll(values, HD, 1), keys)

            @pl.when(group % 2 == 1)
            def _():
                outs[i][:, 2 * pair :] = jnp.where(upper, values, pltpu.roll(keys, HD, 1))


def item_of(start, dims, axis, split):
    index = start + lax.broadcasted_iota(jnp.int32, dims, axis)
    return jnp.where(index < split, 0, 1)


def query_flags(start, count, split, mask_item=None):
    dims = (HD, count)
    item = item_of(start, dims, 1, split)
    zero, one = item == 0, item == 1
    if mask_item is not None:
        off = item != mask_item
        zero, one = zero | off, one | off
    row = lax.broadcasted_iota(jnp.int32, dims, 0)
    hit = ((row == 0) & zero) | ((row == 1) & one)
    return jnp.where(hit, 1.0, 0.0).astype(BF)


def key_flags(start, count, split):
    dims = (count, HD)
    item = item_of(start, dims, 0, split)
    lane = lax.broadcasted_iota(jnp.int32, dims, 1)
    hit = ((lane == 0) & (item == 1)) | ((lane == 1) & (item == 0))
    return jnp.where(hit, NEG, 0.0).astype(BF)


def head_cols(h, heads):
    pair = heads // 2 * 2
    if h < pair:
        return h * HD, (pair + h) * HD
    return 2 * pair * HD, (2 * pair + 1) * HD


def extend_keys(kv_refs, starts, split, kext, vext):
    heads = kext.shape[0]
    at = 0
    for kv, start in zip(kv_refs, starts):
        count = kv.shape[0]
        aux = key_flags(start, count, split)
        for h in range(heads):
            key_col, value_col = head_cols(h, heads)
            keys = kv[:, key_col : key_col + HD]
            kext[h, at : at + count, :] = jnp.concatenate([keys, aux], 1)
            vext[h, :HD, at : at + count] = kv[:, value_col : value_col + HD].T
            vext[h, HD:, at : at + count] = jnp.ones((PAD, count), BF)
        at += count


def scores_of(kext, h, q_ref, flags):
    q = jnp.concatenate([q_ref[h * HD : (h + 1) * HD, :], flags], 0)
    return jnp.dot(kext[h], q, preferred_element_type=F32)


DEPTH = 3


def score_stream(units, score):
    ahead = [score(u) for u in units[:DEPTH]]
    for n, unit in enumerate(units):
        if n + DEPTH < len(units):
            ahead.append(score(units[n + DEPTH]))
        yield unit, ahead.pop(0)


def softmax_part(s, values):
    top = jnp.max(s, axis=0, keepdims=True)
    p = jnp.exp2((s - top) * SCALE).astype(BF)
    return top, jnp.dot(values, p, preferred_element_type=F32)


def places(rows):
    tile = lax.axis_index("tile")
    cube = tile // RUN
    own = [(tile ^ i) * rows for i in range(RUN)]
    far = jnp.where(cube == 0, RUN, RUN - 1) * rows
    edge = (tile % RUN) ^ jnp.where(cube == 0, RUN - 1, 0)
    return cube, own, far, edge


def pick_edge_kernel(q0, q1, q2, q3, out):
    edge = places(1)[3]
    for i, q in enumerate((q0, q1, q2, q3)):

        @pl.when(edge == i)
        def _(q=q):
            out[...] = q[...]


def attend_guest_kernel(sc, q_ref, k0, k1, k2, k3, out, kext, vext):
    heads = kext.shape[0]
    count = q_ref.shape[1]
    cube, own, far, _ = places(count)
    extend_keys((k0, k1, k2, k3), own, sc[0], kext, vext)
    flags = query_flags(far, count, sc[0], cube)
    row = lax.broadcasted_iota(jnp.int32, (PAD, count), 0)
    logs = jnp.zeros((PAD, count), F32)
    for h, s in score_stream(list(range(heads)), lambda h: scores_of(kext, h, q_ref, flags)):
        top, o = softmax_part(s, vext[h])
        total = o[HD : HD + 1, :]
        out[h * HD : (h + 1) * HD, :] = (o[:HD, :] / total).astype(BF)
        log = top * SCALE + jnp.log2(total)
        high = log.astype(BF).astype(F32)
        mid = (log - high).astype(BF).astype(F32)
        for n, piece in enumerate((high, mid, log - high - mid)):
            logs = jnp.where(row == 3 * h + n, piece, logs)
    out[heads * HD :, :] = logs.astype(BF)


def slot_scores(sc, q_refs, starts, kext, mask_item=None):
    heads = kext.shape[0]
    count = q_refs[0].shape[1]
    flags = [query_flags(start, count, sc[0], mask_item) for start in starts]
    units = [(i, h) for i in range(len(q_refs)) for h in range(heads)]
    return score_stream(units, lambda u: scores_of(kext, u[1], q_refs[u[0]], flags[u[0]]))


def attend_own_kernel(sc, q0, q1, kext, vext, out, *, slots):
    count = q0.shape[1]
    _, own, _, _ = places(count)
    own = [own[i] for i in slots]
    for (i, h), s in slot_scores(sc, (q0, q1), own, kext):
        top, o = softmax_part(s, vext[h])
        out[i, h, : HD + 8, :] = o[: HD + 8, :]
        out[i, h, HD + 8 :, :] = jnp.broadcast_to(top, (8, count))


def attend_own_fetch_kernel(sc, q0, q1, kext, vext, wo, out, out_w, sems, *, slots):
    copy = pltpu.make_async_copy(wo, out_w, sems.at[0])
    copy.start()
    attend_own_kernel(sc, q0, q1, kext, vext, out, slots=slots)
    copy.wait()


def attend_merge_kernel(sc, q0, q1, q2, q3, early, late, b0, b1, b2, b3, guest, *refs, taker):
    outs, (kv, kext, vext) = refs[:RUN], refs[RUN:]
    heads = kext.shape[0]
    count = q0.shape[1]
    cube, own, far, edge = places(count)
    kv[...] = (b0[...] + b1[...]) + (b2[...] + b3[...])
    extend_keys((kv,), (far,), sc[0], kext, vext)
    logs = guest[heads * HD :, :].astype(F32)
    for (i, h), s in slot_scores(sc, (q0, q1, q2, q3), own, kext, cube):
        at = slice(h * HD, (h + 1) * HD)
        part = (early, late)[i // 2].at[i % 2, h]
        log = logs[3 * h : 3 * h + 1, :] + logs[3 * h + 1 : 3 * h + 2, :]
        log = log + logs[3 * h + 2 : 3 * h + 3, :]
        log = jnp.where((edge == i) & (cube == taker), log, NEG)
        own_log = part[HD + 8 : HD + 9, :] * SCALE
        top = jnp.maximum(own_log, jnp.max(s, axis=0, keepdims=True) * SCALE)
        top = jnp.maximum(top, log)
        p = jnp.exp2(s * SCALE - top).astype(BF)
        near = jnp.exp2(own_log - top)
        share = jnp.exp2(log - top)
        o = jnp.dot(vext[h], p, preferred_element_type=F32)
        total = o[HD : HD + 1, :] + part[HD : HD + 1, :] * near + share
        o = o[:HD, :] + part[:HD, :] * near + guest[at, :].astype(F32) * share
        outs[i][at, :] = (o / total).astype(BF)


def send_tiles(value, tile_pairs):
    hids = lax.axis_size("hid")
    pairs = [(s * hids + h, d * hids + h) for s, d in tile_pairs for h in range(hids)]
    return lax.ppermute(value, AXES, pairs)


def guest_queries(q_parts, up):
    picked = call(pick_edge_kernel, "pick_edge", [VMEM] * RUN, shape(*q_parts[0].shape))(*q_parts)
    return across(picked, not up)


def across(value, up):
    return send_tiles(value, [(t, t + RUN) if up else (t + RUN, t) for t in range(RUN)])


def attend_items(lengths, guest_q, q_parts, kv, kv_parts, out_weight, up):
    rows = kv[0].shape[0]
    heads = q_parts[0].shape[0] // HD
    ext = [shape(heads, RUN * rows, 2 * HD), shape(heads, HD + PAD, RUN * rows)]

    first, last = RUN - 1, RUN
    guest_kv = [
        send_tiles(kv[i], [(last, i) if up else (first, last + (first ^ i))]) for i in (0, 2, 3)
    ]
    relay = (last ^ 1, 1) if up else (first ^ 1, last + (first ^ 1))
    guest_kv.append(send_tiles(kv_parts[1], [relay]))
    guest, kext, vext = call(
        attend_guest_kernel,
        "attend_guest",
        [SMEM] + [VMEM] * 5,
        [shape(heads * HD + PAD, rows)] + ext,
    )(lengths, guest_q, *kv_parts)
    own_shape = shape(2, heads, HD + PAD, rows, dtype=F32)
    early = call(
        functools.partial(attend_own_kernel, slots=(0, 1)),
        "attend_own",
        [SMEM] + [VMEM] * 4,
        own_shape,
    )(lengths, *q_parts[:2], kext, vext)
    guest, early = lax.optimization_barrier((guest, early))
    guest = across(guest, up)
    late, out_w = call(
        functools.partial(attend_own_fetch_kernel, slots=(2, 3)),
        "attend_own_fetch",
        [SMEM] + [VMEM] * 4 + [HBM],
        [own_shape, shape(*out_weight.shape)],
        [pltpu.SemaphoreType.DMA((1,))],
    )(lengths, *q_parts[2:], kext, vext, out_weight)
    return out_w, call(
        functools.partial(attend_merge_kernel, taker=1 if up else 0),
        "attend_merge",
        [SMEM] + [VMEM] * 11,
        [shape(*q.shape) for q in q_parts],
        [
            pltpu.VMEM(kv[0].shape, BF),
            pltpu.VMEM((heads, rows, 2 * HD), BF),
            pltpu.VMEM((heads, HD + PAD, rows), BF),
        ],
    )(lengths, *q_parts, early, late, *guest_kv, guest)


def attend_all_kernel(sc, starts, q_ref, kv_ref, out, kext, vext, kv_buf, sems, *, slot):
    heads = kext.shape[0]
    keys = kv_ref.shape[0]
    chunk = kv_buf.shape[0]
    flags = query_flags(starts[0], slot, sc[0])

    def step(j, state):
        rows = pl.ds(pl.multiple_of(j * chunk, chunk), chunk)
        copy = pltpu.make_async_copy(kv_ref.at[rows, :], kv_buf, sems.at[0])
        copy.start()
        copy.wait()
        parts = [kv_buf.at[slice(n * slot, (n + 1) * slot), :] for n in range(chunk // slot)]
        begin = [starts[1 + j * (chunk // slot) + n] for n in range(chunk // slot)]
        extend_keys(parts, begin, sc[0], kext, vext)
        after = []
        for h in range(heads):
            top, acc = state[h]
            s = scores_of(kext, h, q_ref, flags)
            new = jnp.maximum(top, jnp.max(s, axis=0, keepdims=True))
            p = jnp.exp2((s - new) * SCALE).astype(BF)
            acc = acc * jnp.exp2((top - new) * SCALE)
            after.append((new, acc + jnp.dot(vext[h], p, preferred_element_type=F32)))
        return tuple(after)

    start = jnp.full((1, slot), 2 * NEG, F32), jnp.zeros((HD + PAD, slot), F32)
    state = lax.fori_loop(0, keys // chunk, step, (start,) * heads)
    for h in range(heads):
        o = state[h][1]
        out[h * HD : (h + 1) * HD, :] = (o[:HD, :] / o[HD : HD + 1, :]).astype(BF)


def attend_gathered(lengths, tile, q_parts, kv_parts):
    rows = kv_parts[0].shape[0]
    heads = q_parts[0].shape[0] // HD
    masks = list(range(RUN))
    kv = jnp.concatenate(kv_parts, 0)
    bit = RUN
    while bit < lax.axis_size("tile"):
        kv = jnp.concatenate([kv, move(kv, bit, 0)], 0)
        masks = masks + [m ^ bit for m in masks]
        bit *= 2
    key_starts = (tile ^ jnp.array(masks, dtype=jnp.int32)) * rows
    chunk = RUN * rows
    outs = []
    for i, q in enumerate(q_parts):
        starts = jnp.concatenate([((tile ^ i) * rows)[None], key_starts]).astype(jnp.int32)
        outs.append(
            call(
                functools.partial(attend_all_kernel, slot=rows),
                "attend_all",
                [SMEM, SMEM, VMEM, HBM],
                shape(*q.shape),
                [
                    pltpu.VMEM((heads, chunk, 2 * HD), BF),
                    pltpu.VMEM((heads, HD + PAD, chunk), BF),
                    pltpu.VMEM((chunk, kv.shape[1]), BF),
                    pltpu.SemaphoreType.DMA((1,)),
                ],
            )(lengths, starts, q, kv)
        )
    return outs


def gather_lhs_kernel(a0, a1, a2, a3, w, lhs, out, turned, *, block):
    for i, a in enumerate((a0, a1, a2, a3)):
        for at, start, size in pieces(lax.axis_index("tile") % RUN ^ i, a.shape[0] // HD):
            turned[pl.ds(start, size), :] = a[at : at + size, :]
    lhs[...] = turned[...].T
    out[...] = block_product(lhs, w, block).astype(out.dtype)


def block_product(lhs, w, block):
    width = w.shape[0]
    cols = pl.ds(pl.multiple_of((lax.axis_index("hid") ^ block) * width, width), width)
    return jnp.dot(lhs[...], w[:, cols], preferred_element_type=F32)


def project_kernel(lhs, w, *outs, blocks):
    for out, block in zip(outs, blocks):
        out[...] = block_product(lhs, w, block).astype(out.dtype)


def project(lhs, w, blocks, dtypes):
    return call(
        functools.partial(project_kernel, blocks=blocks),
        "project",
        [VMEM, VMEM],
        [shape(lhs.shape[0], w.shape[0], dtype=dtype) for dtype in dtypes],
    )(lhs, w)


def layer(
    up,
    item_lengths,
    refresh_slots,
    layer_input,
    key_weight,
    value_weight,
    queries,
    key_cache,
    value_cache,
    out_weight,
):
    rows, width = queries.shape
    tile = lax.axis_index("tile")
    stay = functools.partial(pltpu.with_memory_space_constraint, memory_space=pltpu.HBM)
    x_y = move(layer_input, 0, 2)
    x_c = move(layer_input, 0, 1)
    part = width // RUN
    q_packed = call(
        pack_queries_kernel,
        "pack_queries",
        [HBM],
        [shape(part, rows)] * RUN,
        [
            pltpu.VMEM((rows, width), BF),
            pltpu.VMEM((width, rows), BF),
            pltpu.SemaphoreType.DMA((1,)),
        ],
    )(stay(queries))
    q_parts = [q_packed[0]] + [move(q_packed[i], i, 0) for i in (1, 2, 3)]
    sums, caches, token, *later = call(
        prefetch_kernel,
        "prefetch",
        [SMEM, HBM, VMEM] + [HBM] * 4,
        [
            shape(2, rows, width, dtype=F32),
            shape(2, rows, width),
            shape(8, 128, dtype=F32),
        ]
        + [shape(width, width)] * 4,
        [
            pltpu.VMEM((rows, width), BF),
            pltpu.VMEM((4, width, width), BF),
            pltpu.SemaphoreType.DMA((11,)),
        ],
    )(
        refresh_slots,
        stay(layer_input),
        x_c,
        stay(key_weight),
        stay(value_weight),
        stay(key_cache),
        stay(value_cache),
    )
    x_y, token, q_parts = lax.optimization_barrier((x_y, token, q_parts))
    x_cy = move(x_y, 0, 1)
    kv = call(
        refresh_kernel,
        "refresh",
        [SMEM] + [VMEM] * 9,
        [shape(rows, 2 * part)] * RUN,
        [pltpu.VMEM((2, rows, width), BF)],
    )(refresh_slots, x_y, x_cy, sums, caches, token, *later)
    items = up is not None
    if items:
        guest_q = guest_queries(q_parts, up)
        far_part, guest_q = lax.optimization_barrier((kv[3], guest_q))
        kv = [kv[0], kv[1], kv[2], far_part]
    moved = {i: move(kv[i], i, 0) for i in (1, 2, 3)}
    kv_parts = [kv[0], moved[1], moved[2], moved[3]]
    if items:
        out_w, back = attend_items(item_lengths, guest_q, q_parts, kv, kv_parts, stay(out_weight), up)
    else:
        out_w, back = out_weight, attend_gathered(item_lengths, tile, q_parts, kv_parts)
    parts = [back[0]] + [move(back[i], i, 0) for i in (1, 2, 3)]

    lhs, send_y = call(
        functools.partial(gather_lhs_kernel, block=3),
        "project_first",
        [VMEM] * 5,
        [shape(rows, width), shape(rows, width)],
        [pltpu.VMEM((width, rows), BF)],
    )(*parts, out_w)
    got = move(send_y, 0, 1)
    keep_y, send, keep = project(lhs, out_w, (2, 1, 0), (F32, BF, F32))
    via_y, send = lax.optimization_barrier(((keep_y + got.astype(F32)).astype(BF), send))
    got_y = move(via_y, 0, 2)
    got = move(send, 0, 1)
    return keep, got, got_y


def body(item_lengths, refresh_slots, layer_input, *rest):
    args = (item_lengths, refresh_slots, layer_input) + rest
    if lax.axis_size("tile") == 2 * RUN:
        half = RUN * layer_input.shape[0]
        branches = [functools.partial(layer, up) for up in (True, False)]
        keep, got, got_y = lax.cond(item_lengths[0] > half, *branches, *args)
    else:
        keep, got, got_y = layer(None, *args)
    return (keep + got.astype(F32) + got_y.astype(F32)).astype(BF)


def solution(mesh):
    return jax.shard_map(
        body,
        mesh=mesh,
        in_specs=(
            P(),
            P("tile"),
            P("tile", "hid"),
            P(None, "hid"),
            P(None, "hid"),
            P("tile", "hid"),
            P("tile", "hid"),
            P("tile", "hid"),
            P("hid", None),
        ),
        out_specs=P("tile", "hid"),
        check_vma=False,
    )
```

```python
import functools

import jax
import jax.numpy as jnp
from jax import lax
from jax.experimental import pallas as pl
from jax.experimental.pallas import tpu as pltpu
from jax.sharding import PartitionSpec as P

HD = 64
BLOCK = 128
RUN = 4
NEG = -1e30
SCALE = 0.125 * 1.4426950408889634
AXES = ("tile", "hid")
BF = jnp.bfloat16
F32 = jnp.float32


def move(value, tile_mask, hid_mask):
    tiles, hids = lax.axis_size("tile"), lax.axis_size("hid")
    pairs = [
        (t * hids + h, (t ^ tile_mask) * hids + (h ^ hid_mask))
        for t in range(tiles)
        for h in range(hids)
    ]
    return lax.ppermute(value, AXES, pairs)


VMEM = pl.BlockSpec(memory_space=pltpu.VMEM)
SMEM = pl.BlockSpec(memory_space=pltpu.SMEM)
HBM = pl.BlockSpec(memory_space=pltpu.HBM)
PAD = 16


def call(kernel, name, in_specs, outs, scratch=(), limit=24):
    return pl.pallas_call(
        kernel,
        in_specs=in_specs,
        out_specs=jax.tree.map(lambda _: VMEM, outs),
        out_shape=outs,
        scratch_shapes=list(scratch),
        name=name,
        compiler_params=pltpu.CompilerParams(vmem_limit_bytes=limit * 2**20),
    )


def shape(*dims, dtype=BF):
    return jax.ShapeDtypeStruct(dims, dtype)


def pieces(group, heads):
    pair = heads // 2 * 2
    single = heads - pair
    out = [(0, pl.multiple_of(group * (pair * HD), pair * HD), pair * HD)] if pair else []
    if single:
        start = RUN * pair * HD + group * HD
        out.append((pair * HD, pl.multiple_of(start, HD), HD))
    return out


def any_fresh(slots, count):
    busy = slots[0] >= 0
    for n in range(1, count):
        busy = busy | (slots[n] >= 0)
    return busy


def weight_copy(w, part, target, sem):
    width = target.shape[0]
    start = pl.multiple_of((lax.axis_index("hid") ^ part) * width, width)
    return pltpu.make_async_copy(w.at[pl.ds(start, width), :], target, sem)


def pack_queries_kernel(q_in, *refs):
    outs, (q_buf, turned, sems) = refs[:RUN], refs[RUN:]
    copy = pltpu.make_async_copy(q_in, q_buf, sems.at[0])
    copy.start()
    copy.wait()
    turned[...] = q_buf[...].T
    low = lax.axis_index("tile") % RUN
    for i in range(RUN):
        for at, start, size in pieces(low ^ i, outs[i].shape[0] // HD):
            outs[i][at : at + size, :] = turned[pl.ds(start, size), :]


def prefetch_kernel(slots, x_in, x_c, wk, wv, kc, vc, acc, caches, token, *refs):
    later, (x_own, now, sems) = refs[:4], refs[4:]
    token[...] = jnp.zeros(token.shape, F32)
    busy = any_fresh(slots, caches.shape[1] // BLOCK)
    own = pltpu.make_async_copy(x_in, x_own, sems.at[0])
    rest = [
        pltpu.make_async_copy(kc, caches.at[0], sems.at[1]),
        pltpu.make_async_copy(vc, caches.at[1], sems.at[2]),
    ]
    copies = [
        weight_copy((wk, wv)[n % 2], n // 2, now.at[n] if n < 4 else later[n - 4], sems.at[3 + n])
        for n in range(8)
    ]

    @pl.when(busy)
    def _():
        own.start()
        for copy in copies:
            copy.start()

    for copy in rest:
        copy.start()

    @pl.when(busy)
    def _():
        own.wait()
        for n in range(4):
            x = (x_own, x_c)[n // 2]
            copies[n].wait()
            dots = jnp.dot(x[...], now[n], preferred_element_type=F32)
            acc[n % 2] = dots if n < 2 else acc[n % 2] + dots
        for copy in copies[4:]:
            copy.wait()

    for copy in rest:
        copy.wait()


def refresh_kernel(sc, x_y, x_cy, acc, caches, token, *refs):
    later, outs, mixed = refs[:4], refs[4 : 4 + RUN], refs[4 + RUN]
    width = x_y.shape[1] // RUN
    blocks = x_y.shape[0] // BLOCK
    low = lax.axis_index("tile") % RUN
    fresh = []
    for b in range(blocks):
        hit = sc[0] == b
        for n in range(1, blocks):
            hit = hit | (sc[n] == b)
        fresh.append(hit)
    busy = fresh[0]
    for hit in fresh[1:]:
        busy = busy | hit

    mixed[...] = caches[...]

    @pl.when(busy)
    def _():
        for n in range(2):
            both = jnp.dot(x_y[...], later[n][...], preferred_element_type=F32)
            both = both + jnp.dot(x_cy[...], later[2 + n][...], preferred_element_type=F32)
            total = (acc[n] + both).astype(BF)
            for b in range(blocks):
                rows = slice(b * BLOCK, (b + 1) * BLOCK)
                mixed[n, rows, :] = jnp.where(fresh[b], total[rows, :], caches[n, rows, :])

    heads = width // HD
    pair = heads // 2 * 2 * HD
    upper = lax.broadcasted_iota(jnp.int32, (x_y.shape[0], 2 * HD), 1) >= HD
    for i in range(RUN):
        group = low ^ i
        cols = pl.ds(pl.multiple_of(group * pair, 2 * HD), pair)
        outs[i][:, :pair] = mixed[0, :, cols]
        outs[i][:, pair : 2 * pair] = mixed[1, :, cols]
        if heads % 2:
            cols = pl.ds(pl.multiple_of(RUN * pair + group // 2 * (2 * HD), 2 * HD), 2 * HD)
            keys, values = mixed[0, :, cols], mixed[1, :, cols]

            @pl.when(group % 2 == 0)
            def _():
                outs[i][:, 2 * pair :] = jnp.where(upper, pltpu.roll(values, HD, 1), keys)

            @pl.when(group % 2 == 1)
            def _():
                outs[i][:, 2 * pair :] = jnp.where(upper, values, pltpu.roll(keys, HD, 1))


def item_of(start, dims, axis, split):
    index = start + lax.broadcasted_iota(jnp.int32, dims, axis)
    return jnp.where(index < split, 0, 1)


def query_flags(start, count, split, mask_item=None):
    dims = (HD, count)
    item = item_of(start, dims, 1, split)
    zero, one = item == 0, item == 1
    if mask_item is not None:
        off = item != mask_item
        zero, one = zero | off, one | off
    row = lax.broadcasted_iota(jnp.int32, dims, 0)
    hit = ((row == 0) & zero) | ((row == 1) & one)
    return jnp.where(hit, 1.0, 0.0).astype(BF)


def key_flags(start, count, split):
    dims = (count, HD)
    item = item_of(start, dims, 0, split)
    lane = lax.broadcasted_iota(jnp.int32, dims, 1)
    hit = ((lane == 0) & (item == 1)) | ((lane == 1) & (item == 0))
    return jnp.where(hit, NEG, 0.0).astype(BF)


def head_cols(h, heads):
    pair = heads // 2 * 2
    if h < pair:
        return h * HD, (pair + h) * HD
    return 2 * pair * HD, (2 * pair + 1) * HD


def extend_keys(kv_refs, starts, split, kext, vext):
    heads = kext.shape[0]
    at = 0
    for kv, start in zip(kv_refs, starts):
        count = kv.shape[0]
        aux = key_flags(start, count, split)
        for h in range(heads):
            key_col, value_col = head_cols(h, heads)
            keys = kv[:, key_col : key_col + HD]
            kext[h, at : at + count, :] = jnp.concatenate([keys, aux], 1)
            vext[h, :HD, at : at + count] = kv[:, value_col : value_col + HD].T
            vext[h, HD:, at : at + count] = jnp.ones((PAD, count), BF)
        at += count


def scores_of(kext, h, q_ref, flags):
    q = jnp.concatenate([q_ref[h * HD : (h + 1) * HD, :], flags], 0)
    return jnp.dot(kext[h], q, preferred_element_type=F32)


DEPTH = 3


def score_stream(units, score):
    ahead = [score(u) for u in units[:DEPTH]]
    for n, unit in enumerate(units):
        if n + DEPTH < len(units):
            ahead.append(score(units[n + DEPTH]))
        yield unit, ahead.pop(0)


def softmax_part(s, values):
    top = jnp.max(s, axis=0, keepdims=True)
    p = jnp.exp2((s - top) * SCALE).astype(BF)
    return top, jnp.dot(values, p, preferred_element_type=F32)


def places(rows, span):
    tile = lax.axis_index("tile")
    cube = tile // RUN
    own = [(tile ^ i) * rows for i in range(RUN)]
    far = jnp.where(cube == 0, RUN * rows, RUN * rows - span)
    edge = (tile % RUN) ^ jnp.where(cube == 0, RUN - 1, 0)
    return cube, own, far, edge


def window(rows, span):
    cube = lax.axis_index("tile") // RUN
    start = jnp.where(cube == 0, rows - span, 0)
    return pl.ds(pl.multiple_of(start, span), span)


def window_kernel(*refs):
    half = len(refs) // 2
    for value, out in zip(refs[:half], refs[half:]):
        out[...] = value[window(value.shape[0], out.shape[0]), :]


def windows(values, span):
    rows, width = values[0].shape
    if span == rows:
        return values
    return call(
        window_kernel, "window", [VMEM] * len(values), [shape(span, width)] * len(values)
    )(*values)


def pick_edge_kernel(q0, q1, q2, q3, out):
    rows, span = q0.shape[1], out.shape[1]
    edge = places(rows, span)[3]
    for i, q in enumerate((q0, q1, q2, q3)):

        @pl.when(edge == i)
        def _(q=q):
            out[...] = q[:, window(rows, span)]


def attend_guest_kernel(sc, q_ref, k0, k1, k2, k3, out, kext, vext):
    heads = kext.shape[0]
    count = q_ref.shape[1]
    cube, own, far, _ = places(k0.shape[0], count)
    extend_keys((k0, k1, k2, k3), own, sc[0], kext, vext)
    flags = query_flags(far, count, sc[0], cube)
    row = lax.broadcasted_iota(jnp.int32, (PAD, count), 0)
    logs = jnp.zeros((PAD, count), F32)
    for h, s in score_stream(list(range(heads)), lambda h: scores_of(kext, h, q_ref, flags)):
        top, o = softmax_part(s, vext[h])
        total = o[HD : HD + 1, :]
        out[h * HD : (h + 1) * HD, :] = (o[:HD, :] / total).astype(BF)
        log = top * SCALE + jnp.log2(total)
        high = log.astype(BF).astype(F32)
        mid = (log - high).astype(BF).astype(F32)
        for n, piece in enumerate((high, mid, log - high - mid)):
            logs = jnp.where(row == 3 * h + n, piece, logs)
    out[heads * HD :, :] = logs.astype(BF)


def slot_scores(sc, q_refs, starts, kext, mask_item=None):
    heads = kext.shape[0]
    count = q_refs[0].shape[1]
    flags = [query_flags(start, count, sc[0], mask_item) for start in starts]
    units = [(i, h) for i in range(len(q_refs)) for h in range(heads)]
    return score_stream(units, lambda u: scores_of(kext, u[1], q_refs[u[0]], flags[u[0]]))


def attend_own_kernel(sc, wo, q0, q1, q2, q3, kext, vext, out, out_w, sems):
    copy = pltpu.make_async_copy(wo, out_w, sems.at[0])
    copy.start()
    count = q0.shape[1]
    _, own, _, _ = places(count, count)
    for (i, h), s in slot_scores(sc, (q0, q1, q2, q3), own, kext):
        top, o = softmax_part(s, vext[h])
        out[i, h, : HD + 8, :] = o[: HD + 8, :]
        out[i, h, HD + 8 :, :] = jnp.broadcast_to(top, (8, count))
    copy.wait()


def attend_merge_kernel(sc, q0, q1, q2, q3, part, b0, b1, b2, b3, guest, *refs):
    outs, (kv, kext, vext, placed) = refs[:RUN], refs[RUN:]
    heads = kext.shape[0]
    count = q0.shape[1]
    span = kv.shape[0]
    cube, own, far, edge = places(count, span)
    placed[...] = jnp.zeros(placed.shape, BF)
    placed[:, window(count, span)] = guest[...]
    shift = lax.broadcasted_iota(jnp.int32, (1, count), 1) - jnp.where(cube == 0, count - span, 0)
    held = (shift >= 0) & (shift < span)
    kv[...] = (b0[...] + b1[...]) + (b2[...] + b3[...])
    extend_keys((kv,), (far,), sc[0], kext, vext)
    logs = placed[heads * HD :, :].astype(F32)
    for (i, h), s in slot_scores(sc, (q0, q1, q2, q3), own, kext, cube):
        at = slice(h * HD, (h + 1) * HD)
        log = logs[3 * h : 3 * h + 1, :] + logs[3 * h + 1 : 3 * h + 2, :]
        log = log + logs[3 * h + 2 : 3 * h + 3, :]
        log = jnp.where((edge == i) & held, log, NEG)
        own_log = part[i, h, HD + 8 : HD + 9, :] * SCALE
        top = jnp.maximum(own_log, jnp.max(s, axis=0, keepdims=True) * SCALE)
        top = jnp.maximum(top, log)
        p = jnp.exp2(s * SCALE - top).astype(BF)
        near = jnp.exp2(own_log - top)
        share = jnp.exp2(log - top)
        o = jnp.dot(vext[h], p, preferred_element_type=F32)
        total = o[HD : HD + 1, :] + part[i, h, HD : HD + 1, :] * near + share
        o = o[:HD, :] + part[i, h, :HD, :] * near + placed[at, :].astype(F32) * share
        outs[i][at, :] = (o / total).astype(BF)


def send_tiles(value, tile_pairs):
    hids = lax.axis_size("hid")
    pairs = [(s * hids + h, d * hids + h) for s, d in tile_pairs for h in range(hids)]
    return lax.ppermute(value, AXES, pairs)


def guest_queries(q_parts, span):
    out = shape(q_parts[0].shape[0], span)
    picked = call(pick_edge_kernel, "pick_edge", [VMEM] * RUN, out)(*q_parts)
    return move(picked, RUN, 0)


def attend_items(lengths, guest_q, q_parts, kv, kv_parts, out_weight, span):
    rows = kv[0].shape[0]
    heads = q_parts[0].shape[0] // HD
    ext = [shape(heads, RUN * rows, 2 * HD), shape(heads, HD + PAD, RUN * rows)]

    first, last = RUN - 1, RUN
    near = windows([kv[i] for i in (0, 2, 3)], span)
    guest_kv = [
        send_tiles(near[n], [(first, last + (first ^ i)), (last, i)])
        for n, i in enumerate((0, 2, 3))
    ]
    (relay,) = windows([kv_parts[1]], span)
    guest_kv.append(send_tiles(relay, [(first ^ 1, last + (first ^ 1)), (last ^ 1, 1)]))
    guest, kext, vext = call(
        attend_guest_kernel,
        "attend_guest",
        [SMEM] + [VMEM] * 5,
        [shape(heads * HD + PAD, span)] + ext,
    )(lengths, guest_q, *kv_parts)
    guest = move(guest, RUN, 0)
    own, out_w = call(
        attend_own_kernel,
        "attend_own",
        [SMEM, HBM] + [VMEM] * 6,
        [shape(RUN, heads, HD + PAD, rows, dtype=F32), shape(*out_weight.shape)],
        [pltpu.SemaphoreType.DMA((1,))],
    )(lengths, out_weight, *q_parts, kext, vext)
    return out_w, call(
        attend_merge_kernel,
        "attend_merge",
        [SMEM] + [VMEM] * 10,
        [shape(*q.shape) for q in q_parts],
        [
            pltpu.VMEM((span, kv[0].shape[1]), BF),
            pltpu.VMEM((heads, span, 2 * HD), BF),
            pltpu.VMEM((heads, HD + PAD, span), BF),
            pltpu.VMEM((heads * HD + PAD, rows), BF),
        ],
    )(lengths, *q_parts, own, *guest_kv, guest)


def attend_all_kernel(sc, starts, q_ref, kv_ref, out, kext, vext, kv_buf, sems, *, slot):
    heads = kext.shape[0]
    keys = kv_ref.shape[0]
    chunk = kv_buf.shape[0]
    flags = query_flags(starts[0], slot, sc[0])

    def step(j, state):
        rows = pl.ds(pl.multiple_of(j * chunk, chunk), chunk)
        copy = pltpu.make_async_copy(kv_ref.at[rows, :], kv_buf, sems.at[0])
        copy.start()
        copy.wait()
        parts = [kv_buf.at[slice(n * slot, (n + 1) * slot), :] for n in range(chunk // slot)]
        begin = [starts[1 + j * (chunk // slot) + n] for n in range(chunk // slot)]
        extend_keys(parts, begin, sc[0], kext, vext)
        after = []
        for h in range(heads):
            top, acc = state[h]
            s = scores_of(kext, h, q_ref, flags)
            new = jnp.maximum(top, jnp.max(s, axis=0, keepdims=True))
            p = jnp.exp2((s - new) * SCALE).astype(BF)
            acc = acc * jnp.exp2((top - new) * SCALE)
            after.append((new, acc + jnp.dot(vext[h], p, preferred_element_type=F32)))
        return tuple(after)

    start = jnp.full((1, slot), 2 * NEG, F32), jnp.zeros((HD + PAD, slot), F32)
    state = lax.fori_loop(0, keys // chunk, step, (start,) * heads)
    for h in range(heads):
        o = state[h][1]
        out[h * HD : (h + 1) * HD, :] = (o[:HD, :] / o[HD : HD + 1, :]).astype(BF)


def attend_gathered(lengths, tile, q_parts, kv_parts):
    rows = kv_parts[0].shape[0]
    heads = q_parts[0].shape[0] // HD
    masks = list(range(RUN))
    kv = jnp.concatenate(kv_parts, 0)
    bit = RUN
    while bit < lax.axis_size("tile"):
        kv = jnp.concatenate([kv, move(kv, bit, 0)], 0)
        masks = masks + [m ^ bit for m in masks]
        bit *= 2
    key_starts = (tile ^ jnp.array(masks, dtype=jnp.int32)) * rows
    chunk = RUN * rows
    outs = []
    for i, q in enumerate(q_parts):
        starts = jnp.concatenate([((tile ^ i) * rows)[None], key_starts]).astype(jnp.int32)
        outs.append(
            call(
                functools.partial(attend_all_kernel, slot=rows),
                "attend_all",
                [SMEM, SMEM, VMEM, HBM],
                shape(*q.shape),
                [
                    pltpu.VMEM((heads, chunk, 2 * HD), BF),
                    pltpu.VMEM((heads, HD + PAD, chunk), BF),
                    pltpu.VMEM((chunk, kv.shape[1]), BF),
                    pltpu.SemaphoreType.DMA((1,)),
                ],
            )(lengths, starts, q, kv)
        )
    return outs


def gather_lhs_kernel(a0, a1, a2, a3, w, lhs, out, turned, *, block):
    for i, a in enumerate((a0, a1, a2, a3)):
        for at, start, size in pieces(lax.axis_index("tile") % RUN ^ i, a.shape[0] // HD):
            turned[pl.ds(start, size), :] = a[at : at + size, :]
    lhs[...] = turned[...].T
    out[...] = block_product(lhs, w, block).astype(out.dtype)


def block_product(lhs, w, block):
    width = w.shape[0]
    cols = pl.ds(pl.multiple_of((lax.axis_index("hid") ^ block) * width, width), width)
    return jnp.dot(lhs[...], w[:, cols], preferred_element_type=F32)


def project_kernel(lhs, w, *outs, blocks):
    for out, block in zip(outs, blocks):
        out[...] = block_product(lhs, w, block).astype(out.dtype)


def project(lhs, w, blocks, dtypes):
    return call(
        functools.partial(project_kernel, blocks=blocks),
        "project",
        [VMEM, VMEM],
        [shape(lhs.shape[0], w.shape[0], dtype=dtype) for dtype in dtypes],
    )(lhs, w)


def layer(
    parts_of_edge,
    item_lengths,
    refresh_slots,
    layer_input,
    key_weight,
    value_weight,
    queries,
    key_cache,
    value_cache,
    out_weight,
):
    rows, width = queries.shape
    tile = lax.axis_index("tile")
    stay = functools.partial(pltpu.with_memory_space_constraint, memory_space=pltpu.HBM)
    x_y = move(layer_input, 0, 2)
    x_c = move(layer_input, 0, 1)
    part = width // RUN
    q_packed = call(
        pack_queries_kernel,
        "pack_queries",
        [HBM],
        [shape(part, rows)] * RUN,
        [
            pltpu.VMEM((rows, width), BF),
            pltpu.VMEM((width, rows), BF),
            pltpu.SemaphoreType.DMA((1,)),
        ],
    )(stay(queries))
    q_parts = [q_packed[0]] + [move(q_packed[i], i, 0) for i in (1, 2, 3)]
    sums, caches, token, *later = call(
        prefetch_kernel,
        "prefetch",
        [SMEM, HBM, VMEM] + [HBM] * 4,
        [
            shape(2, rows, width, dtype=F32),
            shape(2, rows, width),
            shape(8, 128, dtype=F32),
        ]
        + [shape(width, width)] * 4,
        [
            pltpu.VMEM((rows, width), BF),
            pltpu.VMEM((4, width, width), BF),
            pltpu.SemaphoreType.DMA((11,)),
        ],
    )(
        refresh_slots,
        stay(layer_input),
        x_c,
        stay(key_weight),
        stay(value_weight),
        stay(key_cache),
        stay(value_cache),
    )
    x_y, token, q_parts = lax.optimization_barrier((x_y, token, q_parts))
    x_cy = move(x_y, 0, 1)
    kv = call(
        refresh_kernel,
        "refresh",
        [SMEM] + [VMEM] * 9,
        [shape(rows, 2 * part)] * RUN,
        [pltpu.VMEM((2, rows, width), BF)],
    )(refresh_slots, x_y, x_cy, sums, caches, token, *later)
    items = parts_of_edge > 0
    if items:
        span = rows // parts_of_edge
        guest_q = guest_queries(q_parts, span)
        far_part, guest_q = lax.optimization_barrier((kv[3], guest_q))
        kv = [kv[0], kv[1], kv[2], far_part]
    moved = {i: move(kv[i], i, 0) for i in (1, 2, 3)}
    kv_parts = [kv[0], moved[1], moved[2], moved[3]]
    if items:
        out_w, back = attend_items(item_lengths, guest_q, q_parts, kv, kv_parts, stay(out_weight), span)
    else:
        out_w, back = out_weight, attend_gathered(item_lengths, tile, q_parts, kv_parts)
    parts = [back[0]] + [move(back[i], i, 0) for i in (1, 2, 3)]

    lhs, send_y = call(
        functools.partial(gather_lhs_kernel, block=3),
        "project_first",
        [VMEM] * 5,
        [shape(rows, width), shape(rows, width)],
        [pltpu.VMEM((width, rows), BF)],
    )(*parts, out_w)
    got = move(send_y, 0, 1)
    keep_y, send, keep = project(lhs, out_w, (2, 1, 0), (F32, BF, F32))
    via_y, send = lax.optimization_barrier(((keep_y + got.astype(F32)).astype(BF), send))
    got_y = move(via_y, 0, 2)
    got = move(send, 0, 1)
    return (keep + got.astype(F32) + got_y.astype(F32)).astype(BF)


def body(item_lengths, refresh_slots, layer_input, *rest):
    args = (item_lengths, refresh_slots, layer_input) + rest
    if lax.axis_size("tile") != 2 * RUN:
        return layer(0, *args)
    rows = layer_input.shape[0]
    near = jnp.abs(item_lengths[0] - RUN * rows) <= rows // 2
    branches = [functools.partial(layer, parts) for parts in (2, 1)]
    return lax.cond(near, *branches, *args)


def solution(mesh):
    return jax.shard_map(
        body,
        mesh=mesh,
        in_specs=(
            P(),
            P("tile"),
            P("tile", "hid"),
            P(None, "hid"),
            P(None, "hid"),
            P("tile", "hid"),
            P("tile", "hid"),
            P("tile", "hid"),
            P("hid", None),
        ),
        out_specs=P("tile", "hid"),
        check_vma=False,
    )
```

```python
import functools

import jax
import jax.numpy as jnp
from jax import lax
from jax.experimental import pallas as pl
from jax.experimental.pallas import tpu as pltpu
from jax.sharding import PartitionSpec as P

HD = 64
BLOCK = 128
RUN = 4
NEG = -1e30
SCALE = 0.125 * 1.4426950408889634
AXES = ("tile", "hid")
BF = jnp.bfloat16
F32 = jnp.float32


def move(value, tile_mask, hid_mask):
    tiles, hids = lax.axis_size("tile"), lax.axis_size("hid")
    pairs = [
        (t * hids + h, (t ^ tile_mask) * hids + (h ^ hid_mask))
        for t in range(tiles)
        for h in range(hids)
    ]
    return lax.ppermute(value, AXES, pairs)


VMEM = pl.BlockSpec(memory_space=pltpu.VMEM)
SMEM = pl.BlockSpec(memory_space=pltpu.SMEM)
HBM = pl.BlockSpec(memory_space=pltpu.HBM)
PAD = 16


def call(kernel, name, in_specs, outs, scratch=(), limit=24):
    return pl.pallas_call(
        kernel,
        in_specs=in_specs,
        out_specs=jax.tree.map(lambda _: VMEM, outs),
        out_shape=outs,
        scratch_shapes=list(scratch),
        name=name,
        compiler_params=pltpu.CompilerParams(vmem_limit_bytes=limit * 2**20),
    )


def shape(*dims, dtype=BF):
    return jax.ShapeDtypeStruct(dims, dtype)


def pieces(group, heads):
    pair = heads // 2 * 2
    single = heads - pair
    out = [(0, pl.multiple_of(group * (pair * HD), pair * HD), pair * HD)] if pair else []
    if single:
        start = RUN * pair * HD + group * HD
        out.append((pair * HD, pl.multiple_of(start, HD), HD))
    return out


def any_fresh(slots, count):
    busy = slots[0] >= 0
    for n in range(1, count):
        busy = busy | (slots[n] >= 0)
    return busy


def weight_copy(w, part, target, sem):
    width = target.shape[0]
    start = pl.multiple_of((lax.axis_index("hid") ^ part) * width, width)
    return pltpu.make_async_copy(w.at[pl.ds(start, width), :], target, sem)


def pack_queries_kernel(q_in, *refs):
    outs, (q_buf, turned, sems) = refs[:RUN], refs[RUN:]
    copy = pltpu.make_async_copy(q_in, q_buf, sems.at[0])
    copy.start()
    copy.wait()
    turned[...] = q_buf[...].T
    low = lax.axis_index("tile") % RUN
    for i in range(RUN):
        for at, start, size in pieces(low ^ i, outs[i].shape[0] // HD):
            outs[i][at : at + size, :] = turned[pl.ds(start, size), :]


def prefetch_kernel(slots, x_in, x_c, wk, wv, kc, vc, acc, caches, token, *refs):
    later, (x_own, now, sems) = refs[:4], refs[4:]
    token[...] = jnp.zeros(token.shape, F32)
    busy = any_fresh(slots, caches.shape[1] // BLOCK)
    own = pltpu.make_async_copy(x_in, x_own, sems.at[0])
    rest = [
        pltpu.make_async_copy(kc, caches.at[0], sems.at[1]),
        pltpu.make_async_copy(vc, caches.at[1], sems.at[2]),
    ]
    copies = [
        weight_copy((wk, wv)[n % 2], n // 2, now.at[n] if n < 4 else later[n - 4], sems.at[3 + n])
        for n in range(8)
    ]

    @pl.when(busy)
    def _():
        own.start()
        for copy in copies:
            copy.start()

    for copy in rest:
        copy.start()

    @pl.when(busy)
    def _():
        own.wait()
        for n in range(4):
            x = (x_own, x_c)[n // 2]
            copies[n].wait()
            dots = jnp.dot(x[...], now[n], preferred_element_type=F32)
            acc[n % 2] = dots if n < 2 else acc[n % 2] + dots
        for copy in copies[4:]:
            copy.wait()

    for copy in rest:
        copy.wait()


def refresh_kernel(sc, x_y, x_cy, acc, caches, token, *refs):
    later, outs, mixed = refs[:4], refs[4 : 4 + RUN], refs[4 + RUN]
    width = x_y.shape[1] // RUN
    blocks = x_y.shape[0] // BLOCK
    low = lax.axis_index("tile") % RUN
    fresh = []
    for b in range(blocks):
        hit = sc[0] == b
        for n in range(1, blocks):
            hit = hit | (sc[n] == b)
        fresh.append(hit)
    busy = fresh[0]
    for hit in fresh[1:]:
        busy = busy | hit

    mixed[...] = caches[...]

    @pl.when(busy)
    def _():
        for n in range(2):
            both = jnp.dot(x_y[...], later[n][...], preferred_element_type=F32)
            both = both + jnp.dot(x_cy[...], later[2 + n][...], preferred_element_type=F32)
            total = (acc[n] + both).astype(BF)
            for b in range(blocks):
                rows = slice(b * BLOCK, (b + 1) * BLOCK)
                mixed[n, rows, :] = jnp.where(fresh[b], total[rows, :], caches[n, rows, :])

    heads = width // HD
    pair = heads // 2 * 2 * HD
    upper = lax.broadcasted_iota(jnp.int32, (x_y.shape[0], 2 * HD), 1) >= HD
    for i in range(RUN):
        group = low ^ i
        cols = pl.ds(pl.multiple_of(group * pair, 2 * HD), pair)
        outs[i][:, :pair] = mixed[0, :, cols]
        outs[i][:, pair : 2 * pair] = mixed[1, :, cols]
        if heads % 2:
            cols = pl.ds(pl.multiple_of(RUN * pair + group // 2 * (2 * HD), 2 * HD), 2 * HD)
            keys, values = mixed[0, :, cols], mixed[1, :, cols]

            @pl.when(group % 2 == 0)
            def _():
                outs[i][:, 2 * pair :] = jnp.where(upper, pltpu.roll(values, HD, 1), keys)

            @pl.when(group % 2 == 1)
            def _():
                outs[i][:, 2 * pair :] = jnp.where(upper, values, pltpu.roll(keys, HD, 1))


def item_of(start, dims, axis, split):
    index = start + lax.broadcasted_iota(jnp.int32, dims, axis)
    return jnp.where(index < split, 0, 1)


def query_flags(start, count, split, mask_item=None):
    dims = (HD, count)
    item = item_of(start, dims, 1, split)
    zero, one = item == 0, item == 1
    if mask_item is not None:
        off = item != mask_item
        zero, one = zero | off, one | off
    row = lax.broadcasted_iota(jnp.int32, dims, 0)
    hit = ((row == 0) & zero) | ((row == 1) & one)
    return jnp.where(hit, 1.0, 0.0).astype(BF)


def key_flags(start, count, split):
    dims = (count, HD)
    item = item_of(start, dims, 0, split)
    lane = lax.broadcasted_iota(jnp.int32, dims, 1)
    hit = ((lane == 0) & (item == 1)) | ((lane == 1) & (item == 0))
    return jnp.where(hit, NEG, 0.0).astype(BF)


def head_cols(h, heads):
    pair = heads // 2 * 2
    if h < pair:
        return h * HD, (pair + h) * HD
    return 2 * pair * HD, (2 * pair + 1) * HD


def extend_keys(kv_refs, starts, split, kext, vext):
    heads = kext.shape[0]
    at = 0
    for kv, start in zip(kv_refs, starts):
        count = kv.shape[0]
        aux = key_flags(start, count, split)
        for h in range(heads):
            key_col, value_col = head_cols(h, heads)
            keys = kv[:, key_col : key_col + HD]
            kext[h, at : at + count, :] = jnp.concatenate([keys, aux], 1)
            vext[h, :HD, at : at + count] = kv[:, value_col : value_col + HD].T
            vext[h, HD:, at : at + count] = jnp.ones((PAD, count), BF)
        at += count


def scores_of(kext, h, q_ref, flags):
    q = jnp.concatenate([q_ref[h * HD : (h + 1) * HD, :], flags], 0)
    return jnp.dot(kext[h], q, preferred_element_type=F32)


DEPTH = 6


def score_stream(units, score):
    ahead = [score(u) for u in units[:DEPTH]]
    for n, unit in enumerate(units):
        if n + DEPTH < len(units):
            ahead.append(score(units[n + DEPTH]))
        yield unit, ahead.pop(0)


def softmax_part(s, values):
    top = jnp.max(s, axis=0, keepdims=True)
    p = jnp.exp2((s - top) * SCALE).astype(BF)
    return top, jnp.dot(values, p, preferred_element_type=F32)


def places(rows, span):
    tile = lax.axis_index("tile")
    cube = tile // RUN
    own = [(tile ^ i) * rows for i in range(RUN)]
    far = jnp.where(cube == 0, RUN * rows, RUN * rows - span)
    edge = (tile % RUN) ^ jnp.where(cube == 0, RUN - 1, 0)
    return cube, own, far, edge


def window(rows, span):
    cube = lax.axis_index("tile") // RUN
    start = jnp.where(cube == 0, rows - span, 0)
    return pl.ds(pl.multiple_of(start, span), span)


def window_kernel(*refs):
    half = len(refs) // 2
    for value, out in zip(refs[:half], refs[half:]):
        out[...] = value[window(value.shape[0], out.shape[0]), :]


def windows(values, span):
    rows, width = values[0].shape
    if span == rows:
        return values
    return call(
        window_kernel, "window", [VMEM] * len(values), [shape(span, width)] * len(values)
    )(*values)


def pick_edge_kernel(q0, q1, q2, q3, out):
    rows, span = q0.shape[1], out.shape[1]
    edge = places(rows, span)[3]
    for i, q in enumerate((q0, q1, q2, q3)):

        @pl.when(edge == i)
        def _(q=q):
            out[...] = q[:, window(rows, span)]


def attend_guest_kernel(sc, q_ref, k0, k1, k2, k3, out, kext, vext):
    heads = kext.shape[0]
    count = q_ref.shape[1]
    cube, own, far, _ = places(k0.shape[0], count)
    extend_keys((k0, k1, k2, k3), own, sc[0], kext, vext)
    flags = query_flags(far, count, sc[0], cube)
    row = lax.broadcasted_iota(jnp.int32, (PAD, count), 0)
    logs = jnp.zeros((PAD, count), F32)
    for h, s in score_stream(list(range(heads)), lambda h: scores_of(kext, h, q_ref, flags)):
        top, o = softmax_part(s, vext[h])
        total = o[HD : HD + 1, :]
        out[h * HD : (h + 1) * HD, :] = (o[:HD, :] / total).astype(BF)
        log = top * SCALE + jnp.log2(total)
        high = log.astype(BF).astype(F32)
        mid = (log - high).astype(BF).astype(F32)
        for n, piece in enumerate((high, mid, log - high - mid)):
            logs = jnp.where(row == 3 * h + n, piece, logs)
    out[heads * HD :, :] = logs.astype(BF)


def slot_scores(sc, q_refs, starts, kext, mask_item=None):
    heads = kext.shape[0]
    count = q_refs[0].shape[1]
    flags = [query_flags(start, count, sc[0], mask_item) for start in starts]
    units = [(i, h) for i in range(len(q_refs)) for h in range(heads)]
    return score_stream(units, lambda u: scores_of(kext, u[1], q_refs[u[0]], flags[u[0]]))


def attend_own_kernel(sc, wo, q0, q1, q2, q3, kext, vext, out, out_w, sems):
    copy = pltpu.make_async_copy(wo, out_w, sems.at[0])
    copy.start()
    count = q0.shape[1]
    _, own, _, _ = places(count, count)
    for (i, h), s in slot_scores(sc, (q0, q1, q2, q3), own, kext):
        top, o = softmax_part(s, vext[h])
        out[i, h, : HD + 8, :] = o[: HD + 8, :]
        out[i, h, HD + 8 :, :] = jnp.broadcast_to(top, (8, count))
    copy.wait()


def attend_merge_kernel(sc, q0, q1, q2, q3, part, b0, b1, b2, b3, guest, *refs):
    outs, (kv, kext, vext, placed) = refs[:RUN], refs[RUN:]
    heads = kext.shape[0]
    count = q0.shape[1]
    span = kv.shape[0]
    cube, own, far, edge = places(count, span)
    placed[...] = jnp.zeros(placed.shape, BF)
    placed[:, window(count, span)] = guest[...]
    shift = lax.broadcasted_iota(jnp.int32, (1, count), 1) - jnp.where(cube == 0, count - span, 0)
    held = (shift >= 0) & (shift < span)
    kv[...] = (b0[...] + b1[...]) + (b2[...] + b3[...])
    extend_keys((kv,), (far,), sc[0], kext, vext)
    logs = placed[heads * HD :, :].astype(F32)
    for (i, h), s in slot_scores(sc, (q0, q1, q2, q3), own, kext, cube):
        at = slice(h * HD, (h + 1) * HD)
        log = logs[3 * h : 3 * h + 1, :] + logs[3 * h + 1 : 3 * h + 2, :]
        log = log + logs[3 * h + 2 : 3 * h + 3, :]
        log = jnp.where((edge == i) & held, log, NEG)
        own_log = part[i, h, HD + 8 : HD + 9, :] * SCALE
        top = jnp.maximum(own_log, jnp.max(s, axis=0, keepdims=True) * SCALE)
        top = jnp.maximum(top, log)
        p = jnp.exp2(s * SCALE - top).astype(BF)
        near = jnp.exp2(own_log - top)
        share = jnp.exp2(log - top)
        o = jnp.dot(vext[h], p, preferred_element_type=F32)
        total = o[HD : HD + 1, :] + part[i, h, HD : HD + 1, :] * near + share
        o = o[:HD, :] + part[i, h, :HD, :] * near + placed[at, :].astype(F32) * share
        outs[i][at, :] = (o / total).astype(BF)


def send_tiles(value, tile_pairs):
    hids = lax.axis_size("hid")
    pairs = [(s * hids + h, d * hids + h) for s, d in tile_pairs for h in range(hids)]
    return lax.ppermute(value, AXES, pairs)


def guest_queries(q_parts, span):
    out = shape(q_parts[0].shape[0], span)
    picked = call(pick_edge_kernel, "pick_edge", [VMEM] * RUN, out)(*q_parts)
    return move(picked, RUN, 0)


def attend_items(lengths, guest_q, q_parts, kv, kv_parts, out_weight, span):
    rows = kv[0].shape[0]
    heads = q_parts[0].shape[0] // HD
    ext = [shape(heads, RUN * rows, 2 * HD), shape(heads, HD + PAD, RUN * rows)]

    first, last = RUN - 1, RUN
    near = windows([kv[i] for i in (0, 2, 3)], span)
    guest_kv = [
        send_tiles(near[n], [(first, last + (first ^ i)), (last, i)])
        for n, i in enumerate((0, 2, 3))
    ]
    (relay,) = windows([kv_parts[1]], span)
    guest_kv.append(send_tiles(relay, [(first ^ 1, last + (first ^ 1)), (last ^ 1, 1)]))
    guest, kext, vext = call(
        attend_guest_kernel,
        "attend_guest",
        [SMEM] + [VMEM] * 5,
        [shape(heads * HD + PAD, span)] + ext,
    )(lengths, guest_q, *kv_parts)
    guest = move(guest, RUN, 0)
    own, out_w = call(
        attend_own_kernel,
        "attend_own",
        [SMEM, HBM] + [VMEM] * 6,
        [shape(RUN, heads, HD + PAD, rows, dtype=F32), shape(*out_weight.shape)],
        [pltpu.SemaphoreType.DMA((1,))],
    )(lengths, out_weight, *q_parts, kext, vext)
    return out_w, call(
        attend_merge_kernel,
        "attend_merge",
        [SMEM] + [VMEM] * 10,
        [shape(*q.shape) for q in q_parts],
        [
            pltpu.VMEM((span, kv[0].shape[1]), BF),
            pltpu.VMEM((heads, span, 2 * HD), BF),
            pltpu.VMEM((heads, HD + PAD, span), BF),
            pltpu.VMEM((heads * HD + PAD, rows), BF),
        ],
    )(lengths, *q_parts, own, *guest_kv, guest)


def attend_all_kernel(sc, starts, q_ref, kv_ref, out, kext, vext, kv_buf, sems, *, slot):
    heads = kext.shape[0]
    keys = kv_ref.shape[0]
    chunk = kv_buf.shape[0]
    flags = query_flags(starts[0], slot, sc[0])

    def step(j, state):
        rows = pl.ds(pl.multiple_of(j * chunk, chunk), chunk)
        copy = pltpu.make_async_copy(kv_ref.at[rows, :], kv_buf, sems.at[0])
        copy.start()
        copy.wait()
        parts = [kv_buf.at[slice(n * slot, (n + 1) * slot), :] for n in range(chunk // slot)]
        begin = [starts[1 + j * (chunk // slot) + n] for n in range(chunk // slot)]
        extend_keys(parts, begin, sc[0], kext, vext)
        after = []
        for h in range(heads):
            top, acc = state[h]
            s = scores_of(kext, h, q_ref, flags)
            new = jnp.maximum(top, jnp.max(s, axis=0, keepdims=True))
            p = jnp.exp2((s - new) * SCALE).astype(BF)
            acc = acc * jnp.exp2((top - new) * SCALE)
            after.append((new, acc + jnp.dot(vext[h], p, preferred_element_type=F32)))
        return tuple(after)

    start = jnp.full((1, slot), 2 * NEG, F32), jnp.zeros((HD + PAD, slot), F32)
    state = lax.fori_loop(0, keys // chunk, step, (start,) * heads)
    for h in range(heads):
        o = state[h][1]
        out[h * HD : (h + 1) * HD, :] = (o[:HD, :] / o[HD : HD + 1, :]).astype(BF)


def attend_gathered(lengths, tile, q_parts, kv_parts):
    rows = kv_parts[0].shape[0]
    heads = q_parts[0].shape[0] // HD
    masks = list(range(RUN))
    kv = jnp.concatenate(kv_parts, 0)
    bit = RUN
    while bit < lax.axis_size("tile"):
        kv = jnp.concatenate([kv, move(kv, bit, 0)], 0)
        masks = masks + [m ^ bit for m in masks]
        bit *= 2
    key_starts = (tile ^ jnp.array(masks, dtype=jnp.int32)) * rows
    chunk = RUN * rows
    outs = []
    for i, q in enumerate(q_parts):
        starts = jnp.concatenate([((tile ^ i) * rows)[None], key_starts]).astype(jnp.int32)
        outs.append(
            call(
                functools.partial(attend_all_kernel, slot=rows),
                "attend_all",
                [SMEM, SMEM, VMEM, HBM],
                shape(*q.shape),
                [
                    pltpu.VMEM((heads, chunk, 2 * HD), BF),
                    pltpu.VMEM((heads, HD + PAD, chunk), BF),
                    pltpu.VMEM((chunk, kv.shape[1]), BF),
                    pltpu.SemaphoreType.DMA((1,)),
                ],
            )(lengths, starts, q, kv)
        )
    return outs


def gather_lhs_kernel(a0, a1, a2, a3, w, lhs, out, turned, *, block):
    for i, a in enumerate((a0, a1, a2, a3)):
        for at, start, size in pieces(lax.axis_index("tile") % RUN ^ i, a.shape[0] // HD):
            turned[pl.ds(start, size), :] = a[at : at + size, :]
    lhs[...] = turned[...].T
    out[...] = block_product(lhs, w, block).astype(out.dtype)


def block_product(lhs, w, block):
    width = w.shape[0]
    cols = pl.ds(pl.multiple_of((lax.axis_index("hid") ^ block) * width, width), width)
    return jnp.dot(lhs[...], w[:, cols], preferred_element_type=F32)


def project_kernel(lhs, w, *outs, blocks):
    for out, block in zip(outs, blocks):
        out[...] = block_product(lhs, w, block).astype(out.dtype)


def project(lhs, w, blocks, dtypes):
    return call(
        functools.partial(project_kernel, blocks=blocks),
        "project",
        [VMEM, VMEM],
        [shape(lhs.shape[0], w.shape[0], dtype=dtype) for dtype in dtypes],
    )(lhs, w)


def layer(
    parts_of_edge,
    item_lengths,
    refresh_slots,
    layer_input,
    key_weight,
    value_weight,
    queries,
    key_cache,
    value_cache,
    out_weight,
):
    rows, width = queries.shape
    tile = lax.axis_index("tile")
    stay = functools.partial(pltpu.with_memory_space_constraint, memory_space=pltpu.HBM)
    x_y = move(layer_input, 0, 2)
    x_c = move(layer_input, 0, 1)
    part = width // RUN
    q_packed = call(
        pack_queries_kernel,
        "pack_queries",
        [HBM],
        [shape(part, rows)] * RUN,
        [
            pltpu.VMEM((rows, width), BF),
            pltpu.VMEM((width, rows), BF),
            pltpu.SemaphoreType.DMA((1,)),
        ],
    )(stay(queries))
    q_parts = [q_packed[0]] + [move(q_packed[i], i, 0) for i in (1, 2, 3)]
    sums, caches, token, *later = call(
        prefetch_kernel,
        "prefetch",
        [SMEM, HBM, VMEM] + [HBM] * 4,
        [
            shape(2, rows, width, dtype=F32),
            shape(2, rows, width),
            shape(8, 128, dtype=F32),
        ]
        + [shape(width, width)] * 4,
        [
            pltpu.VMEM((rows, width), BF),
            pltpu.VMEM((4, width, width), BF),
            pltpu.SemaphoreType.DMA((11,)),
        ],
    )(
        refresh_slots,
        stay(layer_input),
        x_c,
        stay(key_weight),
        stay(value_weight),
        stay(key_cache),
        stay(value_cache),
    )
    x_y, token, q_parts = lax.optimization_barrier((x_y, token, q_parts))
    x_cy = move(x_y, 0, 1)
    kv = call(
        refresh_kernel,
        "refresh",
        [SMEM] + [VMEM] * 9,
        [shape(rows, 2 * part)] * RUN,
        [pltpu.VMEM((2, rows, width), BF)],
    )(refresh_slots, x_y, x_cy, sums, caches, token, *later)
    items = parts_of_edge > 0
    if items:
        span = rows // parts_of_edge
        guest_q = guest_queries(q_parts, span)
        far_part, guest_q = lax.optimization_barrier((kv[3], guest_q))
        kv = [kv[0], kv[1], kv[2], far_part]
    moved = {i: move(kv[i], i, 0) for i in (1, 2, 3)}
    kv_parts = [kv[0], moved[1], moved[2], moved[3]]
    if items:
        out_w, back = attend_items(item_lengths, guest_q, q_parts, kv, kv_parts, stay(out_weight), span)
    else:
        out_w, back = out_weight, attend_gathered(item_lengths, tile, q_parts, kv_parts)
    parts = [back[0]] + [move(back[i], i, 0) for i in (1, 2, 3)]

    lhs, send_y = call(
        functools.partial(gather_lhs_kernel, block=3),
        "project_first",
        [VMEM] * 5,
        [shape(rows, width), shape(rows, width)],
        [pltpu.VMEM((width, rows), BF)],
    )(*parts, out_w)
    got = move(send_y, 0, 1)
    keep_y, send, keep = project(lhs, out_w, (2, 1, 0), (F32, BF, F32))
    via_y, send = lax.optimization_barrier(((keep_y + got.astype(F32)).astype(BF), send))
    got_y = move(via_y, 0, 2)
    got = move(send, 0, 1)
    return (keep + got.astype(F32) + got_y.astype(F32)).astype(BF)


def body(item_lengths, refresh_slots, layer_input, *rest):
    args = (item_lengths, refresh_slots, layer_input) + rest
    if lax.axis_size("tile") != 2 * RUN:
        return layer(0, *args)
    rows = layer_input.shape[0]
    near = jnp.abs(item_lengths[0] - RUN * rows) <= rows // 2
    branches = [functools.partial(layer, parts) for parts in (2, 1)]
    return lax.cond(near, *branches, *args)


def solution(mesh):
    return jax.shard_map(
        body,
        mesh=mesh,
        in_specs=(
            P(),
            P("tile"),
            P("tile", "hid"),
            P(None, "hid"),
            P(None, "hid"),
            P("tile", "hid"),
            P("tile", "hid"),
            P("tile", "hid"),
            P("hid", None),
        ),
        out_specs=P("tile", "hid"),
        check_vma=False,
    )
```
